256 devices in a mesh: layer: 16 (over y, z_hi), dp: 16 (over x, z_lo, core).
Axes of the slice: x: 4, y: 4, z: 8 (z_hi: 4, z_lo: 2; z = z_hi * 2 + z_lo), core: 2. Of those that a mesh axis runs over, the one named last changes fastest.
Arguments:
- states: bfloat16 [16, 4096, 512], P('layer', 'dp'), may hold values from -40 to 40
- guess: bfloat16 [16, 4096, 512], P('layer', 'dp'), may hold values from -6 to 6
- cotangent: bfloat16 [4096, 512], P('dp'), may hold values from -6 to 6
- lengths: int32 [16], P('dp'), may hold values from 128 to 256
- coarse_rate: float32 [16, 512], P('layer'), may hold values from 0.2 to 1
- w_qkv: bfloat16 [16, 512, 1536], P('layer'), may hold values from -0.25 to 0.25
- w_out: bfloat16 [16, 512, 512], P('layer'), may hold values from -0.25 to 0.25
- w_in: bfloat16 [16, 512, 2048], P('layer'), may hold values from -0.25 to 0.25
- w_back: bfloat16 [16, 2048, 512], P('layer'), may hold values from -0.125 to 0.125
- gain_attn: float32 [16, 512], P('layer'), may hold values from 0.5 to 1.5
- gain_ffn: float32 [16, 512], P('layer'), may hold values from 0.5 to 1.5
Outputs:
- adjoint: bfloat16 [16, 4096, 512], P('layer', 'dp')
- coarse_error: float32 [16, 4096, 512], P('layer', 'dp')
- grad_qkv: float32 [16, 512, 1536], P('layer', 'dp')
- grad_out: float32 [16, 512, 512], P('layer', 'dp')
- grad_in: float32 [16, 512, 2048], P('layer', 'dp')
- grad_back: float32 [16, 2048, 512], P('layer', 'dp')
- grad_gain_attn: float32 [16, 512], P('layer', 'dp')
- grad_gain_ffn: float32 [16, 512], P('layer', 'dp')
The draws below stay inside these ranges and needn't reach their ends.
All inputs are finite; a program needn't handle non-finite values.
Results may differ from the reference program's by a relative error of at most 0.028.
The reference program's roundings to bfloat16 on the way count: a program that leaves them out, or rounds other values in their place, can miss the bound.
Values may be sent and summed in bfloat16 or wider, within the bound.
No kernel may reach another device: no remote copies, remote signals or barrier semaphores. Data moves between devices by JAX's collectives and lax.ppermute only.
A program may use at most 128 MiB of HBM per device.

```python
import math
import jax
import jax.numpy as jnp
from jax import lax

D = 512
FF = 2048
HEAD_DIM = 64
SEQ = 256
FACTOR = 4
LAYERS = 16
BATCH = 16
TOKENS = 4096


def draw_states(key, part):
    base = jax.random.normal(jax.random.fold_in(key, 11), (LAYERS, TOKENS, D), jnp.float32)
    return jnp.clip(base, -6.0, 6.0).astype(jnp.bfloat16)


def touch_ends(values, key, low, high):
    longest = values.shape.index(max(values.shape))
    spots = []
    for shift in (0, 1):
        where = [jax.random.randint(jax.random.fold_in(key, axis), (), 0, length) for axis, length in enumerate(values.shape)]
        where[longest] = (where[longest] + shift) % values.shape[longest]
        spots.append(tuple(where))
    return values.at[spots[0]].set(low).at[spots[1]].set(high)


def steps_of(key, extent, cuts, low, top_value):
    def one(position, blocks):
        steps = jax.random.uniform(jax.random.fold_in(jax.random.fold_in(key, 6), position), (blocks,), jnp.float32, low / len(cuts), top_value / len(cuts))
        return jnp.repeat(jnp.exp(steps), extent[position] // blocks).reshape((-1,) + (1,) * (len(extent) - position - 1))

    level = one(*cuts[0])
    for cut in cuts[1:]:
        level = level * one(*cut)
    return level


def normal_values(own_key, dims, width, bound, split=(), kind=jnp.bfloat16):
    array = width * jax.random.normal(own_key, dims, jnp.float32)
    if split:
        array = array * steps_of(own_key, dims, split, -0.22, 0.18)
    return jnp.clip(array, -bound, bound).astype(kind)


def setup_inputs(seed: int = 0) -> dict:
    splits = jax.random.split(jax.random.key(seed), 12)
    return {
        "states": draw_states(jax.random.fold_in(splits[11], 71), 0),
        "guess": normal_values(splits[1], (LAYERS, TOKENS, D), 1.0, 6.0, ((0, 16), (1, 16))),
        "cotangent": normal_values(splits[2], (TOKENS, D), 1.0, 6.0, ((0, 16),)),
        "lengths": touch_ends(jax.random.randint(splits[3], (BATCH,), SEQ // 2, SEQ + 1), jax.random.fold_in(splits[3], 1), SEQ // 2, SEQ).astype(jnp.int32),
        "coarse_rate": jnp.clip(jnp.exp(math.log(1.0) - 1.609438 * jax.random.uniform(splits[4], (LAYERS, D), jnp.float32) ** steps_of(splits[4], (LAYERS, D), ((0, 16),), -0.2, 0.2)), 0.2, 1.0),
        "w_qkv": normal_values(splits[5], (LAYERS, D, 3 * D), D ** -0.5, 0.25, ((0, 16),)),
        "w_out": normal_values(splits[6], (LAYERS, D, D), D ** -0.5, 0.25, ((0, 16),)),
        "w_in": normal_values(splits[7], (LAYERS, D, FF), D ** -0.5, 0.25, ((0, 16),)),
        "w_back": normal_values(splits[8], (LAYERS, FF, D), FF ** -0.5, 0.125, ((0, 16),)),
        "gain_attn": jnp.clip(1.0 + 0.1 * jax.random.normal(splits[9], (LAYERS, D), jnp.float32), 0.5, 1.5),
        "gain_ffn": jnp.clip(1.0 + 0.1 * jax.random.normal(splits[10], (LAYERS, D), jnp.float32), 0.5, 1.5),
    }


EPS = 1e-05
DEPTH_GAIN = 6.73
CUBIC = 0.044715
TANH_SCALE = 0.7978845608028654

def batched(form, left, right):
    return jnp.einsum(form, left.astype(jnp.float32), right.astype(jnp.float32), precision=lax.Precision.HIGHEST)

def matmul(left, right):
    return jnp.dot(left, right, preferred_element_type=jnp.float32)

def normalize(row_sum, gain_vec):
    center = row_sum - lax.optimization_barrier(jnp.mean(row_sum, axis=-1, keepdims=True))
    inv_std = lax.rsqrt(lax.optimization_barrier(jnp.mean(center * center, axis=-1, keepdims=True)) + EPS)
    unit_rows = center * inv_std
    return (unit_rows * gain_vec, unit_rows, inv_std)

def norm_back(upstream, unit_rows, inv_std, gain_vec):
    scaled = upstream * gain_vec
    inner_term = scaled - lax.optimization_barrier(jnp.mean(scaled, axis=-1, keepdims=True)) - unit_rows * lax.optimization_barrier(jnp.mean(scaled * unit_rows, axis=-1, keepdims=True))
    return (inv_std * inner_term, lax.optimization_barrier(jnp.sum(upstream * unit_rows, axis=0)))

def forward(state_in, lengths, layer_qkv, layer_out, layer_in, layer_back, gain_one, gain_two):
    tokens = state_in.shape[0]
    model_width = state_in.shape[1]
    sentences = tokens // SEQ
    head_count = model_width // HEAD_DIM
    score_scale = HEAD_DIM ** (-0.5)
    qkv_bf = matmul(state_in, layer_qkv).astype(jnp.bfloat16)
    qkv_heads = qkv_bf.reshape(sentences, SEQ, 3, head_count, HEAD_DIM)
    queries, key_rows, value_rows = (qkv_heads[:, :, 0], qkv_heads[:, :, 1], qkv_heads[:, :, 2])
    positions = jnp.arange(SEQ, dtype=jnp.int32)
    allowed = (positions[None, :] <= positions[:, None])[None, None] & (positions[None, None, None, :] < lengths[:, None, None, None])
    scores = batched('bqhe,bkhe->bhqk', queries, key_rows) * score_scale
    scores = jnp.where(allowed, scores, -1e+30)
    row_max = lax.optimization_barrier(jnp.max(scores, axis=-1, keepdims=True))
    exp_terms = jnp.where(allowed, jnp.exp(scores - row_max), 0.0)
    attn_probs = exp_terms / lax.optimization_barrier(jnp.sum(exp_terms, axis=-1, keepdims=True))
    prob_bf = attn_probs.astype(jnp.bfloat16)
    context = batched('bhqk,bkhe->bqhe', prob_bf, value_rows).astype(jnp.bfloat16).reshape(tokens, model_width)
    first_sum = DEPTH_GAIN * state_in.astype(jnp.float32) + matmul(context, layer_out)
    normed, unit_one, inv_one = normalize(first_sum, gain_one)
    normed_bf = normed.astype(jnp.bfloat16)
    pre_act = matmul(normed_bf, layer_in)
    tanh_part = jnp.tanh(TANH_SCALE * (pre_act + CUBIC * pre_act * pre_act * pre_act))
    hidden = (0.5 * pre_act * (1.0 + tanh_part)).astype(jnp.bfloat16)
    second_sum = DEPTH_GAIN * normed + matmul(hidden, layer_back)
    _, unit_two, inv_two = normalize(second_sum, gain_two)
    return (queries, key_rows, value_rows, attn_probs, prob_bf, context, unit_one, inv_one, normed_bf, pre_act, tanh_part, hidden, unit_two, inv_two)

def backward(upstream, cache, state_in, layer_qkv, layer_out, layer_in, layer_back, gain_one, gain_two):
    queries, key_rows, value_rows, attn_probs, prob_bf, context, unit_one, inv_one, normed_bf, pre_act, tanh_part, hidden, unit_two, inv_two = cache
    tokens = state_in.shape[0]
    model_width = state_in.shape[1]
    score_scale = HEAD_DIM ** (-0.5)
    d_second, grad_two = norm_back(upstream.astype(jnp.float32), unit_two, inv_two, gain_two)
    d_out_bf = d_second.astype(jnp.bfloat16)
    d_hidden = matmul(d_out_bf, layer_back.T)
    deriv = 0.5 * (1.0 + tanh_part) + 0.5 * pre_act * (1.0 - tanh_part * tanh_part) * TANH_SCALE * (1.0 + 3.0 * CUBIC * pre_act * pre_act)
    d_pre_bf = (d_hidden * deriv).astype(jnp.bfloat16)
    d_normed = DEPTH_GAIN * d_second + matmul(d_pre_bf, layer_in.T)
    d_first, grad_one = norm_back(d_normed, unit_one, inv_one, gain_one)
    d_attn_bf = d_first.astype(jnp.bfloat16)
    d_context = matmul(d_attn_bf, layer_out.T).astype(jnp.bfloat16).reshape(queries.shape)
    d_probs = batched('bqhe,bkhe->bhqk', d_context, value_rows)
    d_values = batched('bhqk,bqhe->bkhe', prob_bf, d_context)
    d_scores = attn_probs * (d_probs - lax.optimization_barrier(jnp.sum(attn_probs * d_probs, axis=-1, keepdims=True))) * score_scale
    d_scores_bf = d_scores.astype(jnp.bfloat16)
    d_queries = batched('bhqk,bkhe->bqhe', d_scores_bf, key_rows)
    d_keys = batched('bhqk,bqhe->bkhe', d_scores_bf, queries)
    d_qkv_bf = jnp.stack([d_queries, d_keys, d_values], axis=2).astype(jnp.bfloat16).reshape(tokens, 3 * model_width)
    d_state = (DEPTH_GAIN * d_first + matmul(d_qkv_bf, layer_qkv.T)).astype(jnp.bfloat16)
    factors = (d_qkv_bf, d_attn_bf, d_pre_bf, d_out_bf, normed_bf, hidden, context, grad_one, grad_two)
    return (d_state, factors)

def reference(states, guess, cotangent, lengths, coarse_rate, w_qkv, w_out, w_in, w_back, gain_attn, gain_ffn):
    layer_total = states.shape[0]
    above = jnp.concatenate([guess[1:], cotangent[None]], axis=0)

    def relax_layer(item):
        state_in, upstream, layer_qkv, layer_out, layer_in, layer_back, gain_one, gain_two = item
        cache = forward(state_in, lengths, layer_qkv, layer_out, layer_in, layer_back, gain_one, gain_two)
        return backward(upstream, cache, state_in, layer_qkv, layer_out, layer_in, layer_back, gain_one, gain_two)[0]
    relaxed = lax.map(relax_layer, (states, above, w_qkv, w_out, w_in, w_back, gain_attn, gain_ffn))
    layer_ids = jnp.arange(layer_total, dtype=jnp.int32)
    coarse_mask = (layer_ids % FACTOR == 0) | (layer_ids == layer_total - 1)
    guess_float = guess.astype(jnp.float32)
    residuals = relaxed.astype(jnp.float32) - guess_float
    factor_rows = jnp.where(coarse_mask[:, None], coarse_rate, 1.0)
    offset_rows = jnp.where(coarse_mask[:, None, None], residuals, 0.0)

    def coarse_step(carry, item):
        rate_row, resid_row = item
        coarse_err = rate_row * carry + resid_row
        return (coarse_err, coarse_err)
    _, errors = lax.scan(coarse_step, jnp.zeros(residuals.shape[1:], jnp.float32), (factor_rows, offset_rows), reverse=True)
    corrected = jnp.where(coarse_mask[:, None, None], (guess_float + errors).astype(jnp.bfloat16), relaxed)
    below = jnp.concatenate([corrected[1:], cotangent[None]], axis=0)

    def final_layer(item):
        state_in, upstream, layer_qkv, layer_out, layer_in, layer_back, gain_one, gain_two = item
        cache = forward(state_in, lengths, layer_qkv, layer_out, layer_in, layer_back, gain_one, gain_two)
        d_state, factors = backward(upstream, cache, state_in, layer_qkv, layer_out, layer_in, layer_back, gain_one, gain_two)
        d_qkv_bf, d_attn_bf, d_pre_bf, d_out_bf, normed_bf, hidden, context, grad_one, grad_two = factors
        return (d_state, matmul(state_in.T, d_qkv_bf), matmul(context.T, d_attn_bf), matmul(normed_bf.T, d_pre_bf), matmul(hidden.T, d_out_bf), grad_one, grad_two)
    results = lax.map(final_layer, (states, below, w_qkv, w_out, w_in, w_back, gain_attn, gain_ffn))
    adjoint = jnp.where(coarse_mask[:, None, None], corrected, results[0])
    return (adjoint, errors, results[1], results[2], results[3], results[4], results[5], results[6])
```

```python
import functools

import jax
import jax.numpy as jnp
from jax import lax
from jax.experimental import pallas as pl
from jax.experimental.pallas import tpu as pltpu
from jax.sharding import Mesh
from jax.sharding import PartitionSpec as P

D = 512
FF = 2048
HEAD_DIM = 64
HEADS = D // HEAD_DIM
SEQ = 256
HALF = SEQ // 2
FACTOR = 4
LAYER = ("ly", "lz")
DP = ("x", "zl", "core")

EPS = 1e-05
DEPTH_GAIN = 6.73
CUBIC = 0.044715
TANH_SCALE = 0.7978845608028654
SCORE_SCALE = HEAD_DIM ** (-0.5)
MSG = SEQ + 16

BF = jnp.bfloat16
F32 = jnp.float32


def nn(a, b):
    return lax.dot_general(a, b, (((1,), (0,)), ((), ())), preferred_element_type=F32)


def nt(a, b):
    return lax.dot_general(a, b, (((1,), (1,)), ((), ())), preferred_element_type=F32)


def tn(a, b):
    return lax.dot_general(a, b, (((0,), (0,)), ((), ())), preferred_element_type=F32)


def row_mean(a):
    return jnp.sum(a, axis=-1, keepdims=True) * (1.0 / D)


def unit_of(rows):
    center = rows - row_mean(rows)
    inv = lax.rsqrt(row_mean(center * center) + EPS)
    return center * inv, inv


def norm_back(up, unit, inv, gain):
    scaled = up * gain
    return inv * (scaled - row_mean(scaled) - unit * row_mean(scaled * unit))


def forward_kernel(
    meta, x_ref, wqkv, wout, win, wback, g1, g2,
    qkv_t, prob_a, prob_b, ctx_t, x_t, normed_t, hidden_t, unit1, inv1, unit2, inv2, deriv,
):
    length = meta[0]
    x = x_ref[...]
    x_t[...] = x.T
    for j in range(3):
        part = nn(x, wqkv[:, j * D : (j + 1) * D]).astype(BF)
        qkv_t[j * D : (j + 1) * D, :] = part.T
    key = lax.broadcasted_iota(jnp.int32, (HALF, SEQ), 0)
    query = lax.broadcasted_iota(jnp.int32, (HALF, SEQ), 1)
    allow_a = key <= query
    key_b, query_b = key[:, :HALF], query[:, :HALF]
    allow_b = (key_b <= query_b) & (key_b + HALF < length)
    for h in range(HEADS):
        lo, hi = h * HEAD_DIM, (h + 1) * HEAD_DIM
        q = qkv_t[lo:hi, :]
        k = qkv_t[D + lo : D + hi, :]
        v = qkv_t[2 * D + lo : 2 * D + hi, :]
        s_a = jnp.where(allow_a, tn(k[:, :HALF], q), -1e30)
        s_b = jnp.where(allow_b, tn(k[:, HALF:], q[:, HALF:]), -1e30)
        m_a = jnp.max(s_a, axis=0, keepdims=True)
        m_b = jnp.max(s_b, axis=0, keepdims=True)
        m_1 = jnp.maximum(m_a[:, HALF:], m_b)
        top = jnp.concatenate([m_a[:, :HALF], m_1], axis=1)
        e_a = jnp.exp((s_a - top) * SCORE_SCALE)
        e_b = jnp.exp((s_b - m_1) * SCORE_SCALE)
        t_a = jnp.sum(e_a, axis=0, keepdims=True)
        t_1 = t_a[:, HALF:] + jnp.sum(e_b, axis=0, keepdims=True)
        r_1 = 1.0 / t_1
        r_a = jnp.concatenate([1.0 / t_a[:, :HALF], r_1], axis=1)
        p_a = e_a * r_a
        p_b = e_b * r_1
        prob_a[h] = p_a
        prob_b[h] = p_b
        c_a = nn(v[:, :HALF], p_a.astype(BF))
        c_b = nn(v[:, HALF:], p_b.astype(BF))
        ctx_t[lo:hi, :HALF] = c_a[:, :HALF].astype(BF)
        ctx_t[lo:hi, HALF:] = (c_a[:, HALF:] + c_b).astype(BF)
    first = DEPTH_GAIN * x.astype(F32) + tn(ctx_t[...], wout[...])
    u1, i1 = unit_of(first)
    unit1[...] = u1
    inv1[...] = i1
    normed = u1 * g1[...]
    normed_bf = normed.astype(BF)
    normed_t[...] = normed_bf.T
    second = DEPTH_GAIN * normed
    for j in range(FF // D):
        cols = slice(j * D, (j + 1) * D)
        pre = nn(normed_bf, win[:, cols])
        sq = pre * pre
        t = jnp.tanh(pre * (TANH_SCALE + (TANH_SCALE * CUBIC) * sq))
        gate = 0.5 + 0.5 * t
        hid = (pre * gate).astype(BF)
        deriv[:, cols] = gate + pre * (1.0 - t * t) * (
            0.5 * TANH_SCALE + (1.5 * TANH_SCALE * CUBIC) * sq
        )
        hidden_t[cols, :] = hid.T
        second = second + nn(hid, wback[cols, :])
    u2, i2 = unit_of(second)
    unit2[...] = u2
    inv2[...] = i2


def ffn_back(d2, d2_bf, deriv, win, wback, keep=None):
    dn = DEPTH_GAIN * d2
    for j in range(FF // D):
        cols = slice(j * D, (j + 1) * D)
        du = (nt(d2_bf, wback[cols, :]) * deriv[:, cols]).astype(BF)
        if keep is not None:
            keep[:, cols] = du
        dn = dn + nt(du, win[:, cols])
    return dn


def attention_back(d1_bf, wout, qkv_t, prob_a, prob_b, dqkv_t):
    dctx_t = nt(d1_bf, wout[...]).astype(BF).T
    for h in range(HEADS):
        lo, hi = h * HEAD_DIM, (h + 1) * HEAD_DIM
        q = qkv_t[lo:hi, :]
        k = qkv_t[D + lo : D + hi, :]
        v = qkv_t[2 * D + lo : 2 * D + hi, :]
        dc = dctx_t[lo:hi, :]
        p_a, p_b = prob_a[h], prob_b[h]
        dp_a = tn(v[:, :HALF], dc)
        dp_b = tn(v[:, HALF:], dc[:, HALF:])
        w_a = jnp.sum(p_a * dp_a, axis=0, keepdims=True)
        w_1 = w_a[:, HALF:] + jnp.sum(p_b * dp_b, axis=0, keepdims=True)
        w = jnp.concatenate([w_a[:, :HALF], w_1], axis=1)
        ds_a = (p_a * (dp_a - w) * SCORE_SCALE).astype(BF)
        ds_b = (p_b * (dp_b - w_1) * SCORE_SCALE).astype(BF)
        dq = nn(k[:, :HALF], ds_a)
        dqkv_t[lo:hi, :HALF] = dq[:, :HALF].astype(BF)
        dqkv_t[lo:hi, HALF:] = (dq[:, HALF:] + nn(k[:, HALF:], ds_b)).astype(BF)
        dqkv_t[D + lo : D + hi, :HALF] = nt(q, ds_a).astype(BF)
        dqkv_t[D + lo : D + hi, HALF:] = nt(q[:, HALF:], ds_b).astype(BF)
        dqkv_t[2 * D + lo : 2 * D + hi, :HALF] = nt(dc, p_a.astype(BF)).astype(BF)
        dqkv_t[2 * D + lo : 2 * D + hi, HALF:] = nt(dc[:, HALF:], p_b.astype(BF)).astype(BF)


def state_back(d1, dqkv, wqkv):
    return DEPTH_GAIN * d1 + nt(dqkv, wqkv[...])


def relax_kernel(
    meta, above, cot, guess, rate,
    qkv_t, prob_a, prob_b, unit1, inv1, unit2, inv2, deriv, wqkv, wout, win, wback, g1, g2,
    relaxed_msg, resid_msg, dqkv_t,
):
    last = meta[1] == 1
    up = jnp.where(last, cot[...].astype(F32), above[...].astype(F32))
    d2 = norm_back(up, unit2[...], inv2[...], g2[...])
    dn = ffn_back(d2, d2.astype(BF), deriv, win, wback)
    d1 = norm_back(dn, unit1[...], inv1[...], g1[...])
    attention_back(d1.astype(BF), wout, qkv_t, prob_a, prob_b, dqkv_t)
    relaxed = state_back(d1, dqkv_t[...].T, wqkv).astype(BF)
    relaxed_msg[:SEQ, :] = relaxed
    resid_msg[:SEQ, :] = (relaxed.astype(F32) - guess[...].astype(F32)).astype(BF)
    full = rate[...]
    high = full.astype(BF)
    rest = full - high.astype(F32)
    mid = rest.astype(BF)
    low = (rest - mid.astype(F32)).astype(BF)
    pad = jnp.zeros((13, D), F32)
    tail = jnp.concatenate(
        [high.astype(F32), mid.astype(F32), low.astype(F32), pad], axis=0
    ).astype(BF)
    relaxed_msg[SEQ:, :] = tail
    resid_msg[SEQ:, :] = tail


def rate_of(msg):
    tail = msg[SEQ:, :].astype(F32)
    return tail[0:1, :] + tail[1:2, :] + tail[2:3, :]


FLIPS = {"core": 1, "zl": 2, "x0": 4, "x1": 12}


def flip_of(position, order):
    flip = 0
    for bit, name in enumerate(order):
        if position & (8 >> bit):
            flip ^= FLIPS[name]
    return flip


ORDER_BACK = ("core", "x0", "x1", "zl")
ORDER_IN = ("core", "x1", "zl", "x0")
ORDER_QKV = ("core", "zl", "x0", "x1")


def place(whole, rows, order, me, keep, send):
    for p in range(16):
        start = pl.multiple_of((me ^ flip_of(p, order)) * rows, rows)
        target = keep if p < 8 else send
        target[p % 8] = whole[pl.ds(start, rows), :]


def chain_kernel(
    meta, shift_msg, m1, m2, m3, above, cot, guess, relaxed_msg, unit2, inv2, g2, hidden_t,
    d2_out, gain2_out, error_out, keep, send, whole,
):
    last = meta[1] == 1
    chained = meta[2] == 1
    me = meta[3]
    shifted = shift_msg[:SEQ, :].astype(F32)
    above_f = above[...].astype(F32)
    error = (shifted - above_f) + rate_of(shift_msg) * (
        m3[:SEQ, :].astype(F32)
        + rate_of(m3) * (m2[:SEQ, :].astype(F32) + rate_of(m2) * m1[:SEQ, :].astype(F32))
    )
    own = relaxed_msg[:SEQ, :].astype(F32) - guess[...].astype(F32)
    error_out[...] = jnp.where(last, own, error)
    corrected = (above_f + error).astype(BF).astype(F32)
    up = jnp.where(last, cot[...].astype(F32), jnp.where(chained, corrected, shifted))
    u2 = unit2[...]
    d2 = norm_back(up, u2, inv2[...], g2[...])
    gain2_out[...] = jnp.broadcast_to(jnp.sum(up * u2, axis=0, keepdims=True), (8, D))
    d2_out[...] = d2
    d2_bf = d2.astype(BF)
    for j in range(FF // D):
        rows = slice(j * D, (j + 1) * D)
        whole[rows, :] = nn(hidden_t[rows, :], d2_bf).astype(BF)
    place(whole, FF // 16, ORDER_BACK, me, keep, send)


def ffn_kernel(
    meta, d2, deriv, unit1, inv1, win, wback, g1, normed_t,
    d1_out, gain1_out, keep, send, du, whole,
):
    me = meta[3]
    d2v = d2[...]
    dn = ffn_back(d2v, d2v.astype(BF), deriv, win, wback, du)
    u1 = unit1[...]
    gain1_out[...] = jnp.broadcast_to(jnp.sum(dn * u1, axis=0, keepdims=True), (8, D))
    d1_out[...] = norm_back(dn, u1, inv1[...], g1[...])
    for j in range(FF // D):
        cols = slice(j * D, (j + 1) * D)
        whole[:, cols] = nn(normed_t[...], du[:, cols]).astype(BF)
    place(whole, D // 16, ORDER_IN, me, keep, send)


def attention_kernel(
    meta, d1, wout, qkv_t, prob_a, prob_b, x_t, ctx_t, gain1, gain2,
    dqkv_out, keep, send, dqkv_t, whole,
):
    me = meta[3]
    d1_bf = d1[...].astype(BF)
    attention_back(d1_bf, wout, qkv_t, prob_a, prob_b, dqkv_t)
    for j in range(3):
        cols = slice(j * D, (j + 1) * D)
        part = dqkv_t[cols, :].T
        dqkv_out[:, cols] = part
        whole[:, cols] = nn(x_t[...], part).astype(BF)
    whole[:, 3 * D : 4 * D] = nn(ctx_t[...], d1_bf).astype(BF)
    pair = jnp.concatenate([gain1[...], gain2[...], jnp.zeros((112, D), F32)], axis=0)
    whole[:, 4 * D :] = pair.T.astype(BF)
    place(whole, D // 16, ORDER_QKV, me, keep, send)


def state_kernel(d1, dqkv, wqkv, out):
    out[...] = state_back(d1[...], dqkv[...], wqkv).astype(BF)


VM = pl.BlockSpec(memory_space=pltpu.VMEM)
SM = pl.BlockSpec(memory_space=pltpu.SMEM)


def call(kernel, outs, scratch, args, flops, name, scalars=1):
    shapes = [jax.ShapeDtypeStruct(s, t) for s, t in outs]
    moved = sum(a.size * a.dtype.itemsize for a in args)
    return pl.pallas_call(
        kernel,
        out_shape=shapes,
        in_specs=[SM] * scalars + [VM] * (len(args) - scalars),
        out_specs=[VM] * len(shapes),
        scratch_shapes=[pltpu.VMEM(s, t) for s, t in scratch],
        compiler_params=pltpu.CompilerParams(vmem_limit_bytes=48 * 1024 * 1024),
        cost_estimate=pl.CostEstimate(flops=flops, bytes_accessed=moved, transcendentals=0),
        name=name,
    )(*args)


def by_flip(name, x):
    if name == "core":
        return lax.ppermute(x, "core", [(0, 1), (1, 0)])
    if name == "zl":
        return lax.ppermute(x, "zl", [(0, 1), (1, 0)])
    mask = 1 if name == "x0" else 3
    return lax.ppermute(x, "x", [(i, i ^ mask) for i in range(4)])


def scattered(keep, send, order):
    parts = [keep]
    size = 8
    for name in order:
        got = by_flip(name, send)
        parts.append(got)
        size //= 2
        lo, hi = (size, 2 * size) if size else (0, 1)
        total = sum(part[lo:hi].astype(F32) for part in parts)
        if size:
            send = total.astype(BF)
    return total[0]


def at(y, z):
    return FACTOR * y + z


def on_device(
    states, guess, cotangent, lengths, coarse_rate, w_qkv, w_out, w_in, w_back, gain_attn, gain_ffn
):
    x, own_guess = states[0], guess[0]
    wqkv, wout, win, wback = w_qkv[0], w_out[0], w_in[0], w_back[0]
    y, z = lax.axis_index("ly"), lax.axis_index("lz")
    layer = at(y, z)
    last = layer == 15
    chained = (z == 3) & ~last | (layer == 14)
    coarse = (z == 0) | last
    meta = jnp.stack(
        [lengths[0], last.astype(jnp.int32), chained.astype(jnp.int32), lax.axis_index(DP)]
    )
    shift = [(i, i - 1) for i in range(1, 16)]
    above = lax.ppermute(own_guess, LAYER, shift)

    tok = (SEQ, D)
    qkv_t, prob_a, prob_b, ctx_t, x_t, normed_t, hidden_t, unit1, inv1, unit2, inv2, deriv = call(
        forward_kernel,
        [
            ((3 * D, SEQ), BF), ((HEADS, HALF, SEQ), F32), ((HEADS, HALF, HALF), F32),
            ((D, SEQ), BF), ((D, SEQ), BF), ((D, SEQ), BF), ((FF, SEQ), BF),
            (tok, F32), ((SEQ, 1), F32), (tok, F32), ((SEQ, 1), F32), ((SEQ, FF), F32),
        ],
        [],
        [meta, x, wqkv, wout, win, wback, gain_attn, gain_ffn],
        1_800_000_000,
        "forward",
    )
    relaxed_msg, resid_msg = call(
        relax_kernel,
        [((MSG, D), BF), ((MSG, D), BF)],
        [((3 * D, SEQ), BF)],
        [meta, above, cotangent, own_guess, coarse_rate, qkv_t, prob_a, prob_b, unit1, inv1,
         unit2, inv2, deriv, wqkv, wout, win, wback, gain_attn, gain_ffn],
        1_900_000_000,
        "relax",
    )
    shift_msg = lax.ppermute(relaxed_msg, LAYER, shift)
    m3 = lax.ppermute(resid_msg, LAYER, [(8, 3), (12, 7), (15, 11)])
    m2 = lax.ppermute(resid_msg, LAYER, [(12, 3), (15, 7)])
    m1 = lax.ppermute(resid_msg, LAYER, [(15, 3)])
    d2, gain2, error, keep_b, send_b = call(
        chain_kernel,
        [(tok, F32), ((8, D), F32), (tok, F32), ((8, FF // 16, D), BF), ((8, FF // 16, D), BF)],
        [((FF, D), BF)],
        [meta, shift_msg, m1, m2, m3, above, cotangent, own_guess, relaxed_msg, unit2, inv2,
         gain_ffn, hidden_t],
        540_000_000,
        "chain",
    )
    d1, gain1, keep_i, send_i = call(
        ffn_kernel,
        [(tok, F32), ((8, D), F32), ((8, D // 16, FF), BF), ((8, D // 16, FF), BF)],
        [((SEQ, FF), BF), ((D, FF), BF)],
        [meta, d2, deriv, unit1, inv1, win, wback, gain_attn, normed_t],
        1_600_000_000,
        "ffn",
    )
    wide = 4 * D + 128
    dqkv, keep_q, send_q = call(
        attention_kernel,
        [((SEQ, 3 * D), BF), ((8, D // 16, wide), BF), ((8, D // 16, wide), BF)],
        [((3 * D, SEQ), BF), ((D, wide), BF)],
        [meta, d1, wout, qkv_t, prob_a, prob_b, x_t, ctx_t, gain1, gain2],
        900_000_000,
        "attention",
    )
    (swept,) = call(state_kernel, [(tok, BF)], [], [d1, dqkv, wqkv], 400_000_000, "state", 0)

    share_back = scattered(keep_b, send_b, ORDER_BACK)
    share_in = scattered(keep_i, send_i, ORDER_IN)
    share_q = scattered(keep_q, send_q, ORDER_QKV)

    error_bf = error.astype(BF)
    f1 = lax.ppermute(error_bf, LAYER, [(at(j, 3), at(j, 2)) for j in range(3)] + [(14, 13)])
    f2 = lax.ppermute(error_bf, LAYER, [(at(j, 3), at(j, 0)) for j in range(4)])
    f3 = lax.ppermute(f1, LAYER, [(at(j, 2), at(j, 1)) for j in range(3)])
    has_own = (z == 3) | (layer == 14)
    reached = jnp.where(
        has_own, error, f1.astype(F32) + f2.astype(F32) + f3.astype(F32)
    )
    relaxed = relaxed_msg[:SEQ]
    guess_f = own_guess.astype(F32)
    resid = relaxed.astype(F32) - guess_f
    coarse_err = jnp.where(z == 0, coarse_rate[0] * reached + resid, reached)
    corrected = (guess_f + coarse_err).astype(BF)
    adjoint = jnp.where(coarse, corrected, swept)
    return (
        adjoint[None],
        coarse_err[None],
        share_q[None, :, : 3 * D],
        share_q[None, :, 3 * D : 4 * D],
        share_in[None],
        share_back[None],
        share_q[:, 4 * D][None],
        share_q[:, 4 * D + 8][None],
    )


def solution(mesh):
    torus = Mesh(mesh.devices.reshape(4, 4, 4, 2, 2), LAYER + DP)
    return jax.shard_map(
        on_device,
        mesh=torus,
        in_specs=(
            P(LAYER, DP, None),
            P(LAYER, DP, None),
            P(DP, None),
            P(DP),
            P(LAYER, None),
            P(LAYER, None, None),
            P(LAYER, None, None),
            P(LAYER, None, None),
            P(LAYER, None, None),
            P(LAYER, None),
            P(LAYER, None),
        ),
        out_specs=(
            P(LAYER, DP, None),
            P(LAYER, DP, None),
            P(LAYER, DP, None),
            P(LAYER, DP, None),
            P(LAYER, DP, None),
            P(LAYER, DP, None),
            P(LAYER, DP),
            P(LAYER, DP),
        ),
        check_vma=False,
    )
```

```python
import functools

import jax
import jax.numpy as jnp
from jax import lax
from jax.experimental import pallas as pl
from jax.experimental.pallas import tpu as pltpu
from jax.sharding import Mesh
from jax.sharding import PartitionSpec as P

D = 512
FF = 2048
HEAD_DIM = 64
HEADS = D // HEAD_DIM
SEQ = 256
HALF = SEQ // 2
FACTOR = 4
LAYER = ("ly", "lz")
DP = ("x", "zl", "core")

EPS = 1e-05
DEPTH_GAIN = 6.73
CUBIC = 0.044715
TANH_SCALE = 0.7978845608028654
SCORE_SCALE = HEAD_DIM ** (-0.5)
MSG = HALF + 16
GRANT = 16

BF = jnp.bfloat16
F32 = jnp.float32


def nn(a, b):
    return lax.dot_general(a, b, (((1,), (0,)), ((), ())), preferred_element_type=F32)


def nt(a, b):
    return lax.dot_general(a, b, (((1,), (1,)), ((), ())), preferred_element_type=F32)


def tn(a, b):
    return lax.dot_general(a, b, (((0,), (0,)), ((), ())), preferred_element_type=F32)


def row_mean(a):
    return jnp.sum(a, axis=-1, keepdims=True) * (1.0 / D)


def unit_of(rows):
    center = rows - row_mean(rows)
    inv = lax.rsqrt(row_mean(center * center) + EPS)
    return center * inv, inv


def norm_back(up, unit, inv, gain):
    scaled = up * gain
    return inv * (scaled - row_mean(scaled) - unit * row_mean(scaled * unit))


def forward_kernel(
    lengths, x_hbm, wqkv_hbm, wout_hbm, win_hbm, wback_hbm, g1_hbm, g2_hbm,
    qkv_t, prob_a, prob_b, ctx_t, x_t, normed_t, hidden_t, unit1, inv1, unit2, inv2, deriv,
    wqkv, wout, win, wback, g1, g2, x_ref, sem,
):
    pairs = (
        (x_hbm, x_ref), (wqkv_hbm, wqkv), (wout_hbm, wout), (g1_hbm, g1),
        (win_hbm, win), (wback_hbm, wback), (g2_hbm, g2),
    )
    copies = [pltpu.make_async_copy(a, b, sem.at[n]) for n, (a, b) in enumerate(pairs)]
    for copy in copies:
        copy.start()
    length = lengths[0]
    copies[0].wait()
    x = x_ref[...]
    x_t[...] = x.T
    copies[1].wait()
    for j in range(3):
        part = nn(x, wqkv[:, j * D : (j + 1) * D]).astype(BF)
        qkv_t[j * D : (j + 1) * D, :] = part.T
    key = lax.broadcasted_iota(jnp.int32, (HALF, SEQ), 0)
    query = lax.broadcasted_iota(jnp.int32, (HALF, SEQ), 1)
    allow_a = key <= query
    key_b, query_b = key[:, :HALF], query[:, :HALF]
    allow_b = (key_b <= query_b) & (key_b + HALF < length)
    for h in range(HEADS):
        lo, hi = h * HEAD_DIM, (h + 1) * HEAD_DIM
        q = qkv_t[lo:hi, :]
        k = qkv_t[D + lo : D + hi, :]
        v = qkv_t[2 * D + lo : 2 * D + hi, :]
        s_a = jnp.where(allow_a, tn(k[:, :HALF], q), -1e30)
        s_b = jnp.where(allow_b, tn(k[:, HALF:], q[:, HALF:]), -1e30)
        m_a = jnp.max(s_a, axis=0, keepdims=True)
        m_b = jnp.max(s_b, axis=0, keepdims=True)
        m_1 = jnp.maximum(m_a[:, HALF:], m_b)
        top = jnp.concatenate([m_a[:, :HALF], m_1], axis=1)
        e_a = jnp.exp((s_a - top) * SCORE_SCALE)
        e_b = jnp.exp((s_b - m_1) * SCORE_SCALE)
        t_a = jnp.sum(e_a, axis=0, keepdims=True)
        t_1 = t_a[:, HALF:] + jnp.sum(e_b, axis=0, keepdims=True)
        r_1 = 1.0 / t_1
        r_a = jnp.concatenate([1.0 / t_a[:, :HALF], r_1], axis=1)
        p_a = e_a * r_a
        p_b = e_b * r_1
        prob_a[h] = p_a
        prob_b[h] = p_b
        c_a = nn(v[:, :HALF], p_a.astype(BF))
        c_b = nn(v[:, HALF:], p_b.astype(BF))
        ctx_t[lo:hi, :HALF] = c_a[:, :HALF].astype(BF)
        ctx_t[lo:hi, HALF:] = (c_a[:, HALF:] + c_b).astype(BF)
    copies[2].wait()
    copies[3].wait()
    first = DEPTH_GAIN * x.astype(F32) + tn(ctx_t[...], wout[...])
    u1, i1 = unit_of(first)
    unit1[...] = u1
    inv1[...] = i1
    normed = u1 * g1[...]
    normed_bf = normed.astype(BF)
    normed_t[...] = normed_bf.T
    second = DEPTH_GAIN * normed
    copies[4].wait()
    copies[5].wait()
    copies[6].wait()
    for j in range(FF // D):
        cols = slice(j * D, (j + 1) * D)
        pre = nn(normed_bf, win[:, cols])
        sq = pre * pre
        t = jnp.tanh(pre * (TANH_SCALE + (TANH_SCALE * CUBIC) * sq))
        gate = 0.5 + 0.5 * t
        hid = (pre * gate).astype(BF)
        deriv[:, cols] = gate + pre * (1.0 - t * t) * (
            0.5 * TANH_SCALE + (1.5 * TANH_SCALE * CUBIC) * sq
        )
        hidden_t[cols, :] = hid.T
        second = second + nn(hid, wback[cols, :])
    u2, i2 = unit_of(second)
    unit2[...] = u2
    inv2[...] = i2


def ffn_back(d2, d2_bf, deriv, win, wback, keep=None):
    dn = DEPTH_GAIN * d2
    for j in range(FF // D):
        cols = slice(j * D, (j + 1) * D)
        du = (nt(d2_bf, wback[cols, :]) * deriv[:, cols]).astype(BF)
        if keep is not None:
            keep[:, cols] = du
        dn = dn + nt(du, win[:, cols])
    return dn


def attention_back(d1_bf, wout, qkv_t, prob_a, prob_b, dqkv_t):
    dctx_t = nt(d1_bf, wout[...]).astype(BF).T
    for h in range(HEADS):
        lo, hi = h * HEAD_DIM, (h + 1) * HEAD_DIM
        q = qkv_t[lo:hi, :]
        k = qkv_t[D + lo : D + hi, :]
        v = qkv_t[2 * D + lo : 2 * D + hi, :]
        dc = dctx_t[lo:hi, :]
        p_a, p_b = prob_a[h], prob_b[h]
        dp_a = tn(v[:, :HALF], dc)
        dp_b = tn(v[:, HALF:], dc[:, HALF:])
        w_a = jnp.sum(p_a * dp_a, axis=0, keepdims=True)
        w_1 = w_a[:, HALF:] + jnp.sum(p_b * dp_b, axis=0, keepdims=True)
        w = jnp.concatenate([w_a[:, :HALF], w_1], axis=1)
        ds_a = (p_a * (dp_a - w) * SCORE_SCALE).astype(BF)
        ds_b = (p_b * (dp_b - w_1) * SCORE_SCALE).astype(BF)
        dq = nn(k[:, :HALF], ds_a)
        dqkv_t[lo:hi, :HALF] = dq[:, :HALF].astype(BF)
        dqkv_t[lo:hi, HALF:] = (dq[:, HALF:] + nn(k[:, HALF:], ds_b)).astype(BF)
        dqkv_t[D + lo : D + hi, :HALF] = nt(q, ds_a).astype(BF)
        dqkv_t[D + lo : D + hi, HALF:] = nt(q[:, HALF:], ds_b).astype(BF)
        dqkv_t[2 * D + lo : 2 * D + hi, :HALF] = nt(dc, p_a.astype(BF)).astype(BF)
        dqkv_t[2 * D + lo : 2 * D + hi, HALF:] = nt(dc[:, HALF:], p_b.astype(BF)).astype(BF)


def state_back(d1, dqkv, wqkv):
    return DEPTH_GAIN * d1 + nt(dqkv, wqkv[...])


def thirds(full):
    high = full.astype(BF)
    rest = full - high.astype(F32)
    mid = rest.astype(BF)
    low = (rest - mid.astype(F32)).astype(BF)
    parts = [part.astype(F32) for part in (high, mid, low)]
    return jnp.concatenate(parts + [jnp.zeros((13, D), F32)], axis=0).astype(BF)


def whole_of(msg):
    tail = msg[HALF:, :].astype(F32)
    return tail[0:1, :] + tail[1:2, :] + tail[2:3, :]


def rows_of(msg):
    return msg[:HALF, :].astype(F32)


def relax_kernel(
    meta, above, cot, guess, rate,
    qkv_t, prob_a, prob_b, unit1, inv1, unit2, inv2, deriv, wqkv, wout, win, wback, g1, g2,
    relaxed_out, resid_low, resid_high, dqkv_t,
):
    last = meta[1] == 1
    up = jnp.where(last, cot[...].astype(F32), above[...].astype(F32))
    d2 = norm_back(up, unit2[...], inv2[...], g2[...])
    dn = ffn_back(d2, d2.astype(BF), deriv, win, wback)
    d1 = norm_back(dn, unit1[...], inv1[...], g1[...])
    attention_back(d1.astype(BF), wout, qkv_t, prob_a, prob_b, dqkv_t)
    relaxed = state_back(d1, dqkv_t[...].T, wqkv).astype(BF)
    relaxed_out[...] = relaxed
    resid = (relaxed.astype(F32) - guess[...].astype(F32)).astype(BF)
    tail = thirds(rate[...])
    resid_low[:HALF, :] = resid[:HALF, :]
    resid_low[HALF:, :] = tail
    resid_high[:HALF, :] = resid[HALF:, :]
    resid_high[HALF:, :] = tail


def compose_kernel(meta, relaxed, guess, rate, one, two, across, low, high):
    resid = relaxed[...].astype(F32) - guess[...].astype(F32)
    r1, r2 = whole_of(one), whole_of(two)
    higher = rows_of(one) + r1 * rows_of(two)
    low[:HALF, :] = (resid[:HALF, :] + rate[...] * higher).astype(BF)
    y = meta[4]
    factor = rate[...] * jnp.where(y < 3, r1, 1.0) * jnp.where(y < 2, r2, 1.0)
    low[HALF:, :] = thirds(factor)
    top = jnp.where(meta[1] == 1, resid[HALF:, :], 0.0)
    high[:HALF, :] = (rows_of(across) + whole_of(across) * top).astype(BF)
    high[HALF:, :] = across[HALF:, :]


FLIPS = {"core": 1, "zl": 2, "x0": 4, "x1": 12}


def flip_of(position, order):
    flip = 0
    for bit, name in enumerate(order):
        if position & (8 >> bit):
            flip ^= FLIPS[name]
    return flip


ORDER_BACK = ("core", "x0", "x1", "zl")
ORDER_IN = ("core", "x1", "zl", "x0")
ORDER_QKV = ("core", "zl", "x0", "x1")
WIDE = FF + D + 128


def place(whole, rows, order, me, keep, send):
    for p in range(16):
        start = pl.multiple_of((me ^ flip_of(p, order)) * rows, rows)
        target = keep if p < 8 else send
        target[p % 8] = whole[pl.ds(start, rows), :]


def chain_kernel(
    meta, shifted_ref, composed, top1, top2, top3, high1, high2, high3,
    above, cot, guess, relaxed, unit2, inv2, g2, hidden_t,
    d2_out, gain2_out, error_out, error_bf, keep, send, whole,
):
    last = meta[1] == 1
    chained = meta[2] == 1
    me = meta[3]
    shifted = shifted_ref[...].astype(F32)
    above_f = above[...].astype(F32)
    top = rows_of(top1) + rows_of(top2) + rows_of(top3)
    low = rows_of(composed) + whole_of(composed) * top
    high = rows_of(high1) + whole_of(high1) * (
        rows_of(high2) + whole_of(high2) * rows_of(high3)
    )
    far = jnp.concatenate([low, high], axis=0)
    near = shifted - above_f
    own = relaxed[...].astype(F32) - guess[...].astype(F32)
    error = jnp.where(last, own, jnp.where(meta[0] == 1, far, near))
    error_out[...] = error
    error_bf[...] = jnp.where(meta[0] == 1, error, 0.0).astype(BF)
    corrected = (above_f + error).astype(BF).astype(F32)
    up = jnp.where(last, cot[...].astype(F32), jnp.where(chained, corrected, shifted))
    u2 = unit2[...]
    d2 = norm_back(up, u2, inv2[...], g2[...])
    gain2_out[...] = jnp.broadcast_to(jnp.sum(up * u2, axis=0, keepdims=True), (8, D))
    d2_out[...] = d2
    d2_bf = d2.astype(BF)
    for j in range(FF // D):
        rows = slice(j * D, (j + 1) * D)
        whole[rows, :] = nn(hidden_t[rows, :], d2_bf).astype(BF)
    place(whole, FF // 16, ORDER_BACK, me, keep, send)


def ffn_kernel(
    meta, d2, deriv, unit1, inv1, win, wback, g1, normed_t, ctx_t, gain2,
    d1_out, keep, send, du, whole,
):
    me = meta[3]
    d2v = d2[...]
    dn = ffn_back(d2v, d2v.astype(BF), deriv, win, wback, du)
    u1 = unit1[...]
    gain1 = jnp.broadcast_to(jnp.sum(dn * u1, axis=0, keepdims=True), (8, D))
    d1 = norm_back(dn, u1, inv1[...], g1[...])
    d1_out[...] = d1
    for j in range(FF // D):
        cols = slice(j * D, (j + 1) * D)
        whole[:, cols] = nn(normed_t[...], du[:, cols]).astype(BF)
    whole[:, FF : FF + D] = nn(ctx_t[...], d1.astype(BF)).astype(BF)
    pair = jnp.concatenate([gain1, gain2[...], jnp.zeros((112, D), F32)], axis=0)
    whole[:, FF + D :] = pair.T.astype(BF)
    place(whole, D // 16, ORDER_IN, me, keep, send)


def attention_kernel(
    meta, d1, wout, qkv_t, prob_a, prob_b, x_t, dqkv_out, keep, send, dqkv_t, whole,
):
    attention_back(d1[...].astype(BF), wout, qkv_t, prob_a, prob_b, dqkv_t)
    for j in range(3):
        cols = slice(j * D, (j + 1) * D)
        part = dqkv_t[cols, :].T
        dqkv_out[:, cols] = part
        whole[:, cols] = nn(x_t[...], part).astype(BF)
    place(whole, D // 16, ORDER_QKV, meta[3], keep, send)


def state_kernel(d1, dqkv, wqkv, out):
    out[...] = state_back(d1[...], dqkv[...], wqkv).astype(BF)


HB = pl.BlockSpec(memory_space=pltpu.HBM)
VM = pl.BlockSpec(memory_space=pltpu.VMEM)
SM = pl.BlockSpec(memory_space=pltpu.SMEM)


def call(kernel, outs, scratch, args, flops, name, scalars=1, operands=VM, grant=16, into=None):
    shapes = [jax.ShapeDtypeStruct(s, t) for s, t in outs]
    moved = sum(a.size * a.dtype.itemsize for a in args)
    return pl.pallas_call(
        kernel,
        out_shape=shapes,
        in_specs=[SM] * scalars + [operands] * (len(args) - scalars),
        out_specs=into or [VM] * len(shapes),
        scratch_shapes=[s if not isinstance(s, tuple) else pltpu.VMEM(*s) for s in scratch],
        compiler_params=pltpu.CompilerParams(vmem_limit_bytes=grant * 1024 * 1024),
        cost_estimate=pl.CostEstimate(flops=flops, bytes_accessed=moved, transcendentals=0),
        name=name,
    )(*args)


def by_flip(name, x):
    if name == "core":
        return lax.ppermute(x, "core", [(0, 1), (1, 0)])
    if name == "zl":
        return lax.ppermute(x, "zl", [(0, 1), (1, 0)])
    mask = 1 if name == "x0" else 3
    return lax.ppermute(x, "x", [(i, i ^ mask) for i in range(4)])


def sum_kernel(*refs):
    out = refs[-1]
    size = out.shape[0]
    total = refs[0][size : 2 * size].astype(F32)
    for ref in refs[1:-1]:
        total = total + ref[size : 2 * size].astype(F32)
    out[...] = total.astype(BF)


def passing(parts):
    shape = parts[-1].shape
    (out,) = call(
        sum_kernel, [((shape[0] // 2,) + shape[1:], BF)], [], list(parts), 1_000_000, "sum", 0
    )
    return out


def total_of(parts):
    total = parts[0][0].astype(F32)
    for part in parts[1:]:
        total = total + part[0].astype(F32)
    return total


def shares_kernel(
    k0, k1, k2, k3, k4, i0, i1, i2, i3, i4, back, inner, outer, gain1, gain2,
    back_v, in_v, sem,
):
    back_v[...] = total_of((k0, k1, k2, k3, k4))
    first = pltpu.make_async_copy(back_v, back, sem.at[0])
    first.start()
    in_v[...] = total_of((i0, i1, i2, i3, i4))
    second = pltpu.make_async_copy(in_v.at[:, :FF], inner, sem.at[1])
    third = pltpu.make_async_copy(in_v.at[:, FF : FF + D], outer, sem.at[2])
    second.start()
    third.start()
    turned = jnp.concatenate([in_v[:, FF + D :], jnp.zeros((96, 128), F32)], axis=0).T
    gain1[...] = turned[0:1, :32]
    gain2[...] = turned[8:9, :32]
    first.wait()
    second.wait()
    third.wait()


def qkv_kernel(k0, k1, k2, k3, k4, out, whole, sem):
    whole[...] = total_of((k0, k1, k2, k3, k4))
    copy = pltpu.make_async_copy(whole, out, sem.at[0])
    copy.start()
    copy.wait()


def after(x, *done):
    return lax.optimization_barrier((x,) + done)[0]


def at(y, z):
    return FACTOR * y + z


def on_device(
    states, guess, cotangent, lengths, coarse_rate, w_qkv, w_out, w_in, w_back, gain_attn, gain_ffn
):
    x, own_guess = states[0], guess[0]
    y, z = lax.axis_index("ly"), lax.axis_index("lz")
    layer = at(y, z)
    last = layer == 15
    chained = (z == 3) & ~last | (layer == 14)
    coarse = (z == 0) | last
    meta = jnp.stack(
        [(z == 3).astype(jnp.int32), last.astype(jnp.int32), chained.astype(jnp.int32), lax.axis_index(DP), y]
    )
    above = lax.ppermute(own_guess, LAYER, [(i, i - 1) for i in range(1, 16)])

    tok = (SEQ, D)
    (
        qkv_t, prob_a, prob_b, ctx_t, x_t, normed_t, hidden_t, unit1, inv1, unit2, inv2, deriv,
        wqkv, wout, win, wback, gain_one, gain_two,
    ) = call(
        forward_kernel,
        [
            ((3 * D, SEQ), BF), ((HEADS, HALF, SEQ), F32), ((HEADS, HALF, HALF), F32),
            ((D, SEQ), BF), ((D, SEQ), BF), ((D, SEQ), BF), ((FF, SEQ), BF),
            (tok, F32), ((SEQ, 1), F32), (tok, F32), ((SEQ, 1), F32), ((SEQ, FF), F32),
            ((D, 3 * D), BF), ((D, D), BF), ((D, FF), BF), ((FF, D), BF), ((1, D), F32),
            ((1, D), F32),
        ],
        [(tok, BF), pltpu.SemaphoreType.DMA((7,))],
        [lengths] + [pltpu.with_memory_space_constraint(a, pltpu.HBM) for a in (x, w_qkv[0], w_out[0], w_in[0], w_back[0], gain_attn, gain_ffn)],
        10_000_000,
        "forward",
        operands=HB,
        grant=GRANT,
    )
    relaxed, resid_low, resid_high = call(
        relax_kernel,
        [(tok, BF), ((MSG, D), BF), ((MSG, D), BF)],
        [((3 * D, SEQ), BF)],
        [meta, above, cotangent, own_guess, coarse_rate, qkv_t, prob_a, prob_b, unit1, inv1,
         unit2, inv2, deriv, wqkv, wout, win, wback, gain_one, gain_two],
        10_000_000,
        "relax",
    )
    across = lax.ppermute(resid_high, LAYER, [(4, 7), (8, 11), (12, 15)])
    from1 = lax.ppermute(resid_low, LAYER, [(12, 8), (8, 4), (15, 11)])
    from2 = lax.ppermute(resid_low, LAYER, [(12, 4), (15, 7)])
    from3 = lax.ppermute(resid_low, LAYER, [(15, 3)])
    shifted = lax.ppermute(
        relaxed, LAYER, [(at(j, i), at(j, i - 1)) for j in range(4) for i in range(1, 4)]
    )
    low, high = call(
        compose_kernel,
        [((MSG, D), BF), ((MSG, D), BF)],
        [],
        [meta, relaxed, own_guess, coarse_rate, from1, from2, across],
        10_000_000,
        "compose",
    )
    composed = lax.ppermute(low, LAYER, [(4, 3), (8, 7), (12, 11)])
    high1 = lax.ppermute(high, LAYER, [(15, 11), (11, 7), (7, 3)])
    high2 = lax.ppermute(high, LAYER, [(15, 7), (11, 3)])
    high3 = lax.ppermute(high, LAYER, [(15, 3)])
    d2, gain2, error, error_bf, keep_b, send_b = call(
        chain_kernel,
        [(tok, F32), ((8, D), F32), (tok, F32), (tok, BF), ((8, FF // 16, D), BF),
         ((8, FF // 16, D), BF)],
        [((FF, D), BF)],
        [meta, shifted, composed, from1, from2, from3, high1, high2, high3, above, cotangent,
         own_guess, relaxed, unit2, inv2, gain_two, hidden_t],
        10_000_000,
        "chain",
    )
    b0 = by_flip(ORDER_BACK[0], send_b)
    part_i = (8, D // 16, WIDE)
    d1, keep_i, send_i = call(
        ffn_kernel,
        [(tok, F32), (part_i, BF), (part_i, BF)],
        [((SEQ, FF), BF), ((D, WIDE), BF)],
        [meta, d2, deriv, unit1, inv1, win, wback, gain_one, normed_t, ctx_t, gain2],
        10_000_000,
        "ffn",
    )
    send_b = passing([keep_b, b0])
    b1 = by_flip(ORDER_BACK[1], send_b)
    i0 = by_flip(ORDER_IN[0], send_i)
    part_q = (8, D // 16, 3 * D)
    dqkv, keep_q, send_q = call(
        attention_kernel,
        [((SEQ, 3 * D), BF), (part_q, BF), (part_q, BF)],
        [((3 * D, SEQ), BF), ((D, 3 * D), BF)],
        [meta, after(d1, send_b), wout, qkv_t, prob_a, prob_b, x_t],
        10_000_000,
        "attention",
    )
    q0 = by_flip(ORDER_QKV[0], send_q)
    send_i = passing([keep_i, after(i0, dqkv)])
    i1 = by_flip(ORDER_IN[1], send_i)
    (swept,) = call(
        state_kernel, [(tok, BF)], [], [after(d1, send_i), dqkv, wqkv], 10_000_000, "state", 0
    )
    send_q = passing([keep_q, after(q0, swept)])
    q1 = by_flip(ORDER_QKV[1], send_q)
    send_b = passing([keep_b, b0, after(b1, send_q)])
    b2 = by_flip(ORDER_BACK[2], send_b)
    wrapped = lax.ppermute(
        after(error_bf, send_b), LAYER, [(at(j, 3), at(j, 0)) for j in range(4)]
    )
    send_q = passing([keep_q, q0, after(q1, send_b)])
    q2 = by_flip(ORDER_QKV[2], send_q)
    send_i = passing([keep_i, i0, after(i1, send_q)])
    i2 = by_flip(ORDER_IN[2], send_i)
    send_b = passing([keep_b, b0, b1, after(b2, send_i)])
    b3 = by_flip(ORDER_BACK[3], send_b)
    passed = lax.ppermute(
        after(error_bf, send_b) + wrapped,
        LAYER,
        [(at(j, 3), at(j, 2)) for j in range(4)] + [(at(j, 0), at(j, 1)) for j in range(4)],
    )
    send_q = passing([keep_q, q0, q1, after(q2, send_b)])
    q3 = by_flip(ORDER_QKV[3], send_q)
    send_i = passing([keep_i, i0, i1, after(i2, send_q)])
    i3 = by_flip(ORDER_IN[3], send_i)
    (share_q,) = call(
        qkv_kernel, [((D // 16, 3 * D), F32)],
        [((D // 16, 3 * D), F32), pltpu.SemaphoreType.DMA((1,))],
        [keep_q, q0, q1, q2, after(q3, send_i)], 1_000_000, "qkv", 0, into=[HB],
    )
    has_own = (z == 3) | (layer == 14)
    far = wrapped.astype(F32) + jnp.where(z == 0, 0, passed).astype(F32)
    reached = jnp.where(has_own, error, far)
    guess_f = own_guess.astype(F32)
    resid = relaxed.astype(F32) - guess_f
    coarse_err = jnp.where(z == 0, coarse_rate[0] * reached + resid, reached)
    corrected = (guess_f + coarse_err).astype(BF)
    adjoint = jnp.where(coarse, corrected, swept)
    share_back, share_in, share_out, share_one, share_two = call(
        shares_kernel,
        [((FF // 16, D), F32), ((D // 16, FF), F32), ((D // 16, D), F32), ((1, 32), F32),
         ((1, 32), F32)],
        [((FF // 16, D), F32), ((D // 16, WIDE), F32), pltpu.SemaphoreType.DMA((3,))],
        [keep_b, b0, b1, b2, b3, keep_i, i0, i1, i2, after(i3, share_q, adjoint, coarse_err)],
        1_000_000, "shares", 0, into=[HB, HB, HB, VM, VM],
    )
    return (
        adjoint[None],
        coarse_err[None],
        share_q[None],
        share_out[None],
        share_in[None],
        share_back[None],
        share_one,
        share_two,
    )


def solution(mesh):
    torus = Mesh(mesh.devices.reshape(4, 4, 4, 2, 2), LAYER + DP)
    return jax.shard_map(
        on_device,
        mesh=torus,
        in_specs=(
            P(LAYER, DP, None),
            P(LAYER, DP, None),
            P(DP, None),
            P(DP),
            P(LAYER, None),
            P(LAYER, None, None),
            P(LAYER, None, None),
            P(LAYER, None, None),
            P(LAYER, None, None),
            P(LAYER, None),
            P(LAYER, None),
        ),
        out_specs=(
            P(LAYER, DP, None),
            P(LAYER, DP, None),
            P(LAYER, DP, None),
            P(LAYER, DP, None),
            P(LAYER, DP, None),
            P(LAYER, DP, None),
            P(LAYER, DP),
            P(LAYER, DP),
        ),
        check_vma=False,
    )
```

```python
import functools

import jax
import jax.numpy as jnp
from jax import lax
from jax.experimental import pallas as pl
from jax.experimental.pallas import tpu as pltpu
from jax.sharding import Mesh
from jax.sharding import PartitionSpec as P

D = 512
FF = 2048
HEAD_DIM = 64
HEADS = D // HEAD_DIM
SEQ = 256
HALF = SEQ // 2
FACTOR = 4
LAYER = ("ly", "lz")
DP = ("x", "zl", "core")

EPS = 1e-05
DEPTH_GAIN = 6.73
CUBIC = 0.044715
TANH_SCALE = 0.7978845608028654
SCORE_SCALE = HEAD_DIM ** (-0.5)
LOW = 160
HIGH = SEQ - LOW
GRANT = 16

BF = jnp.bfloat16
F32 = jnp.float32


def nn(a, b):
    return lax.dot_general(a, b, (((1,), (0,)), ((), ())), preferred_element_type=F32)


def nt(a, b):
    return lax.dot_general(a, b, (((1,), (1,)), ((), ())), preferred_element_type=F32)


def tn(a, b):
    return lax.dot_general(a, b, (((0,), (0,)), ((), ())), preferred_element_type=F32)


def row_mean(a):
    return jnp.sum(a, axis=-1, keepdims=True) * (1.0 / D)


def unit_of(rows):
    center = rows - row_mean(rows)
    inv = lax.rsqrt(row_mean(center * center) + EPS)
    return center * inv, inv


def norm_back(up, unit, inv, gain):
    scaled = up * gain
    return inv * (scaled - row_mean(scaled) - unit * row_mean(scaled * unit))


def forward_kernel(
    lengths, x_hbm, wqkv_hbm, wout_hbm, win_hbm, wback_hbm, g1_hbm, g2_hbm,
    qkv_t, prob_a, prob_b, ctx_t, x_t, normed_t, hidden_t, unit1, inv1, unit2, inv2, deriv,
    wqkv, wout, win, wback, g1, g2, x_ref, sem,
):
    pairs = (
        (x_hbm, x_ref), (wqkv_hbm, wqkv), (wout_hbm, wout), (g1_hbm, g1),
        (win_hbm, win), (wback_hbm, wback), (g2_hbm, g2),
    )
    copies = [pltpu.make_async_copy(a, b, sem.at[n]) for n, (a, b) in enumerate(pairs)]
    for copy in copies:
        copy.start()
    length = lengths[0]
    copies[0].wait()
    x = x_ref[...]
    x_t[...] = x.T
    copies[1].wait()
    for j in range(3):
        part = nn(x, wqkv[:, j * D : (j + 1) * D]).astype(BF)
        qkv_t[j * D : (j + 1) * D, :] = part.T
    key = lax.broadcasted_iota(jnp.int32, (HALF, SEQ), 0)
    query = lax.broadcasted_iota(jnp.int32, (HALF, SEQ), 1)
    allow_a = key <= query
    key_b, query_b = key[:, :HALF], query[:, :HALF]
    allow_b = (key_b <= query_b) & (key_b + HALF < length)
    for h in range(HEADS):
        lo, hi = h * HEAD_DIM, (h + 1) * HEAD_DIM
        q = qkv_t[lo:hi, :]
        k = qkv_t[D + lo : D + hi, :]
        v = qkv_t[2 * D + lo : 2 * D + hi, :]
        s_a = jnp.where(allow_a, tn(k[:, :HALF], q), -1e30)
        s_b = jnp.where(allow_b, tn(k[:, HALF:], q[:, HALF:]), -1e30)
        m_a = jnp.max(s_a, axis=0, keepdims=True)
        m_b = jnp.max(s_b, axis=0, keepdims=True)
        m_1 = jnp.maximum(m_a[:, HALF:], m_b)
        top = jnp.concatenate([m_a[:, :HALF], m_1], axis=1)
        e_a = jnp.exp((s_a - top) * SCORE_SCALE)
        e_b = jnp.exp((s_b - m_1) * SCORE_SCALE)
        t_a = jnp.sum(e_a, axis=0, keepdims=True)
        t_1 = t_a[:, HALF:] + jnp.sum(e_b, axis=0, keepdims=True)
        r_1 = 1.0 / t_1
        r_a = jnp.concatenate([1.0 / t_a[:, :HALF], r_1], axis=1)
        p_a = e_a * r_a
        p_b = e_b * r_1
        prob_a[h] = p_a
        prob_b[h] = p_b
        c_a = nn(v[:, :HALF], p_a.astype(BF))
        c_b = nn(v[:, HALF:], p_b.astype(BF))
        ctx_t[lo:hi, :HALF] = c_a[:, :HALF].astype(BF)
        ctx_t[lo:hi, HALF:] = (c_a[:, HALF:] + c_b).astype(BF)
    copies[2].wait()
    copies[3].wait()
    first = DEPTH_GAIN * x.astype(F32) + tn(ctx_t[...], wout[...])
    u1, i1 = unit_of(first)
    unit1[...] = u1
    inv1[...] = i1
    normed = u1 * g1[...]
    normed_bf = normed.astype(BF)
    normed_t[...] = normed_bf.T
    second = DEPTH_GAIN * normed
    copies[4].wait()
    copies[5].wait()
    copies[6].wait()
    for j in range(FF // D):
        cols = slice(j * D, (j + 1) * D)
        pre = nn(normed_bf, win[:, cols])
        sq = pre * pre
        t = jnp.tanh(pre * (TANH_SCALE + (TANH_SCALE * CUBIC) * sq))
        gate = 0.5 + 0.5 * t
        hid = (pre * gate).astype(BF)
        deriv[:, cols] = gate + pre * (1.0 - t * t) * (
            0.5 * TANH_SCALE + (1.5 * TANH_SCALE * CUBIC) * sq
        )
        hidden_t[cols, :] = hid.T
        second = second + nn(hid, wback[cols, :])
    u2, i2 = unit_of(second)
    unit2[...] = u2
    inv2[...] = i2


def ffn_back(d2, d2_bf, deriv, win, wback, keep=None):
    dn = DEPTH_GAIN * d2
    for j in range(FF // D):
        cols = slice(j * D, (j + 1) * D)
        du = (nt(d2_bf, wback[cols, :]) * deriv[:, cols]).astype(BF)
        if keep is not None:
            keep[:, cols] = du
        dn = dn + nt(du, win[:, cols])
    return dn


def attention_back(d1_bf, wout, qkv_t, prob_a, prob_b, dqkv_t):
    dctx_t = nt(d1_bf, wout[...]).astype(BF).T
    for h in range(HEADS):
        lo, hi = h * HEAD_DIM, (h + 1) * HEAD_DIM
        q = qkv_t[lo:hi, :]
        k = qkv_t[D + lo : D + hi, :]
        v = qkv_t[2 * D + lo : 2 * D + hi, :]
        dc = dctx_t[lo:hi, :]
        p_a, p_b = prob_a[h], prob_b[h]
        dp_a = tn(v[:, :HALF], dc)
        dp_b = tn(v[:, HALF:], dc[:, HALF:])
        w_a = jnp.sum(p_a * dp_a, axis=0, keepdims=True)
        w_1 = w_a[:, HALF:] + jnp.sum(p_b * dp_b, axis=0, keepdims=True)
        w = jnp.concatenate([w_a[:, :HALF], w_1], axis=1)
        ds_a = (p_a * (dp_a - w) * SCORE_SCALE).astype(BF)
        ds_b = (p_b * (dp_b - w_1) * SCORE_SCALE).astype(BF)
        dq = nn(k[:, :HALF], ds_a)
        dqkv_t[lo:hi, :HALF] = dq[:, :HALF].astype(BF)
        dqkv_t[lo:hi, HALF:] = (dq[:, HALF:] + nn(k[:, HALF:], ds_b)).astype(BF)
        dqkv_t[D + lo : D + hi, :HALF] = nt(q, ds_a).astype(BF)
        dqkv_t[D + lo : D + hi, HALF:] = nt(q[:, HALF:], ds_b).astype(BF)
        dqkv_t[2 * D + lo : 2 * D + hi, :HALF] = nt(dc, p_a.astype(BF)).astype(BF)
        dqkv_t[2 * D + lo : 2 * D + hi, HALF:] = nt(dc[:, HALF:], p_b.astype(BF)).astype(BF)


def state_back(d1, dqkv, wqkv):
    return DEPTH_GAIN * d1 + nt(dqkv, wqkv[...])


def thirds(full):
    high = full.astype(BF)
    rest = full - high.astype(F32)
    mid = rest.astype(BF)
    low = (rest - mid.astype(F32)).astype(BF)
    parts = [part.astype(F32) for part in (high, mid, low)]
    return jnp.concatenate(parts + [jnp.zeros((13, D), F32)], axis=0).astype(BF)


def whole_of(msg):
    tail = msg[msg.shape[0] - 16 :, :].astype(F32)
    return tail[0:1, :] + tail[1:2, :] + tail[2:3, :]


def rows_of(msg):
    return msg[: msg.shape[0] - 16, :].astype(F32)


def relax_kernel(
    meta, above, cot, guess, rate,
    qkv_t, prob_a, prob_b, unit1, inv1, unit2, inv2, deriv, wqkv, wout, win, wback, g1, g2,
    relaxed_out, resid_low, resid_high, dqkv_t,
):
    last = meta[1] == 1
    up = jnp.where(last, cot[...].astype(F32), above[...].astype(F32))
    d2 = norm_back(up, unit2[...], inv2[...], g2[...])
    dn = ffn_back(d2, d2.astype(BF), deriv, win, wback)
    d1 = norm_back(dn, unit1[...], inv1[...], g1[...])
    attention_back(d1.astype(BF), wout, qkv_t, prob_a, prob_b, dqkv_t)
    relaxed = state_back(d1, dqkv_t[...].T, wqkv).astype(BF)
    relaxed_out[...] = relaxed
    resid = (relaxed.astype(F32) - guess[...].astype(F32)).astype(BF)
    tail = thirds(rate[...])
    resid_low[:LOW, :] = resid[:LOW, :]
    resid_low[LOW:, :] = tail
    resid_high[:HIGH, :] = resid[LOW:, :]
    resid_high[HIGH:, :] = tail


def compose_low_kernel(meta, relaxed, guess, rate, one, two, out):
    resid = relaxed[:LOW, :].astype(F32) - guess[:LOW, :].astype(F32)
    r1, r2 = whole_of(one), whole_of(two)
    higher = rows_of(one) + r1 * rows_of(two)
    out[:LOW, :] = (resid + rate[...] * higher).astype(BF)
    y = meta[4]
    factor = rate[...] * jnp.where(y < 3, r1, 1.0) * jnp.where(y < 2, r2, 1.0)
    out[LOW:, :] = thirds(factor)


def compose_high_kernel(meta, relaxed, guess, across, out):
    resid = relaxed[LOW:, :].astype(F32) - guess[LOW:, :].astype(F32)
    top = jnp.where(meta[1] == 1, resid, 0.0)
    out[:HIGH, :] = (rows_of(across) + whole_of(across) * top).astype(BF)
    out[HIGH:, :] = across[HIGH:, :]


def mix_kernel(error_bf, wrapped, out):
    out[...] = (error_bf[...].astype(F32) + wrapped[...].astype(F32)).astype(BF)


def finish_kernel(
    meta, error, wrapped, passed, relaxed, guess, rate, swept, adjoint, coarse_err,
    adjoint_v, error_v, sem,
):
    last, own_known, z = meta[1] == 1, (meta[0] + meta[2]) > 0, meta[5]
    far = wrapped[...].astype(F32) + jnp.where(z == 0, 0.0, passed[...].astype(F32))
    reached = jnp.where(own_known, error[...], far)
    guess_f = guess[...].astype(F32)
    resid = relaxed[...].astype(F32) - guess_f
    value = jnp.where(z == 0, rate[...] * reached + resid, reached)
    error_v[...] = value
    first = pltpu.make_async_copy(error_v, coarse_err, sem.at[0])
    first.start()
    coarse = (z == 0) | last
    kept = jnp.where(coarse, guess_f + value, swept[...].astype(F32))
    adjoint_v[...] = kept.astype(BF)
    second = pltpu.make_async_copy(adjoint_v, adjoint, sem.at[1])
    second.start()
    first.wait()
    second.wait()


FLIPS = {"core": 1, "zl": 2, "x0": 4, "x1": 12}


def flip_of(position, order):
    flip = 0
    for bit, name in enumerate(order):
        if position & (8 >> bit):
            flip ^= FLIPS[name]
    return flip


ORDER_BACK = ("core", "x0", "x1", "zl")
ORDER_IN = ("core", "x1", "zl", "x0")
ORDER_QKV = ("core", "zl", "x0", "x1")
WIDE = FF + D + 128


def place(whole, rows, order, me, keep, send):
    for p in range(16):
        start = pl.multiple_of((me ^ flip_of(p, order)) * rows, rows)
        target = keep if p < 8 else send
        target[p % 8] = whole[pl.ds(start, rows), :]


def chain_kernel(
    meta, shifted_ref, composed, top1, top2, top3, high1, high2, high3,
    above, cot, guess, relaxed, unit2, inv2, g2, hidden_t,
    d2_out, gain2_out, error_out, error_bf, keep, send, whole,
):
    last = meta[1] == 1
    chained = meta[2] == 1
    me = meta[3]
    shifted = shifted_ref[...].astype(F32)
    above_f = above[...].astype(F32)
    top = rows_of(top1) + rows_of(top2) + rows_of(top3)
    low = rows_of(composed) + whole_of(composed) * top
    high = rows_of(high1) + whole_of(high1) * (
        rows_of(high2) + whole_of(high2) * rows_of(high3)
    )
    far = jnp.concatenate([low, high], axis=0)
    near = shifted - above_f
    own = relaxed[...].astype(F32) - guess[...].astype(F32)
    error = jnp.where(last, own, jnp.where(meta[0] == 1, far, near))
    error_out[...] = error
    error_bf[...] = jnp.where(meta[0] == 1, error, 0.0).astype(BF)
    corrected = (above_f + error).astype(BF).astype(F32)
    up = jnp.where(last, cot[...].astype(F32), jnp.where(chained, corrected, shifted))
    u2 = unit2[...]
    d2 = norm_back(up, u2, inv2[...], g2[...])
    gain2_out[...] = jnp.broadcast_to(jnp.sum(up * u2, axis=0, keepdims=True), (8, D))
    d2_out[...] = d2
    d2_bf = d2.astype(BF)
    for j in range(FF // D):
        rows = slice(j * D, (j + 1) * D)
        whole[rows, :] = nn(hidden_t[rows, :], d2_bf).astype(BF)
    place(whole, FF // 16, ORDER_BACK, me, keep, send)


def ffn_kernel(
    meta, d2, deriv, unit1, inv1, win, wback, g1, normed_t, ctx_t, gain2,
    d1_out, keep, send, du, whole,
):
    me = meta[3]
    d2v = d2[...]
    dn = ffn_back(d2v, d2v.astype(BF), deriv, win, wback, du)
    u1 = unit1[...]
    gain1 = jnp.broadcast_to(jnp.sum(dn * u1, axis=0, keepdims=True), (8, D))
    d1 = norm_back(dn, u1, inv1[...], g1[...])
    d1_out[...] = d1
    for j in range(FF // D):
        cols = slice(j * D, (j + 1) * D)
        whole[:, cols] = nn(normed_t[...], du[:, cols]).astype(BF)
    whole[:, FF : FF + D] = nn(ctx_t[...], d1.astype(BF)).astype(BF)
    pair = jnp.concatenate([gain1, gain2[...], jnp.zeros((112, D), F32)], axis=0)
    whole[:, FF + D :] = pair.T.astype(BF)
    place(whole, D // 16, ORDER_IN, me, keep, send)


def attention_kernel(
    meta, d1, wout, qkv_t, prob_a, prob_b, x_t, dqkv_out, keep, send, dqkv_t, whole,
):
    attention_back(d1[...].astype(BF), wout, qkv_t, prob_a, prob_b, dqkv_t)
    for j in range(3):
        cols = slice(j * D, (j + 1) * D)
        part = dqkv_t[cols, :].T
        dqkv_out[:, cols] = part
        whole[:, cols] = nn(x_t[...], part).astype(BF)
    place(whole, D // 16, ORDER_QKV, meta[3], keep, send)


def state_kernel(d1, dqkv, wqkv, out):
    out[...] = state_back(d1[...], dqkv[...], wqkv).astype(BF)


HB = pl.BlockSpec(memory_space=pltpu.HBM)
VM = pl.BlockSpec(memory_space=pltpu.VMEM)
SM = pl.BlockSpec(memory_space=pltpu.SMEM)


def call(kernel, outs, scratch, args, flops, name, scalars=1, operands=VM, grant=16, into=None):
    shapes = [jax.ShapeDtypeStruct(s, t) for s, t in outs]
    return pl.pallas_call(
        kernel,
        out_shape=shapes,
        in_specs=[SM] * scalars + [operands] * (len(args) - scalars),
        out_specs=into or [VM] * len(shapes),
        scratch_shapes=[s if not isinstance(s, tuple) else pltpu.VMEM(*s) for s in scratch],
        compiler_params=pltpu.CompilerParams(vmem_limit_bytes=grant * 1024 * 1024),
        cost_estimate=pl.CostEstimate(flops=5000000000, bytes_accessed=0, transcendentals=0),
        name=name,
    )(*args)


def by_flip(name, x):
    if name == "core":
        return lax.ppermute(x, "core", [(0, 1), (1, 0)])
    if name == "zl":
        return lax.ppermute(x, "zl", [(0, 1), (1, 0)])
    mask = 1 if name == "x0" else 3
    return lax.ppermute(x, "x", [(i, i ^ mask) for i in range(4)])


def sum_kernel(*refs):
    out = refs[-1]
    size = out.shape[0]
    total = refs[0][size : 2 * size].astype(F32)
    for ref in refs[1:-1]:
        total = total + ref[size : 2 * size].astype(F32)
    out[...] = total.astype(BF)


def passing(parts):
    shape = parts[-1].shape
    (out,) = call(
        sum_kernel, [((shape[0] // 2,) + shape[1:], BF)], [], list(parts), 1_000_000, "sum", 0
    )
    return out


def total_of(parts):
    total = parts[0][0].astype(F32)
    for part in parts[1:]:
        total = total + part[0].astype(F32)
    return total


def shares_kernel(
    k0, k1, k2, k3, k4, i0, i1, i2, i3, i4, back, inner, outer, gain1, gain2,
    back_v, in_v, sem,
):
    back_v[...] = total_of((k0, k1, k2, k3, k4))
    first = pltpu.make_async_copy(back_v, back, sem.at[0])
    first.start()
    in_v[...] = total_of((i0, i1, i2, i3, i4))
    second = pltpu.make_async_copy(in_v.at[:, :FF], inner, sem.at[1])
    third = pltpu.make_async_copy(in_v.at[:, FF : FF + D], outer, sem.at[2])
    second.start()
    third.start()
    turned = jnp.concatenate([in_v[:, FF + D :], jnp.zeros((96, 128), F32)], axis=0).T
    gain1[...] = turned[0:1, :32]
    gain2[...] = turned[8:9, :32]
    first.wait()
    second.wait()
    third.wait()


def qkv_kernel(k0, k1, k2, k3, k4, out, whole, sem):
    whole[...] = total_of((k0, k1, k2, k3, k4))
    copy = pltpu.make_async_copy(whole, out, sem.at[0])
    copy.start()
    copy.wait()


def after(x, *done):
    return lax.optimization_barrier((x,) + done)[0]


def at(y, z):
    return FACTOR * y + z


def on_device(
    states, guess, cotangent, lengths, coarse_rate, w_qkv, w_out, w_in, w_back, gain_attn, gain_ffn
):
    x, own_guess = states[0], guess[0]
    y, z = lax.axis_index("ly"), lax.axis_index("lz")
    layer = at(y, z)
    last = layer == 15
    chained = (z == 3) & ~last | (layer == 14)
    meta = jnp.stack(
        [(z == 3).astype(jnp.int32), last.astype(jnp.int32), chained.astype(jnp.int32), lax.axis_index(DP), y, z]
    )
    above = lax.ppermute(own_guess, LAYER, [(i, i - 1) for i in range(1, 16)])

    tok = (SEQ, D)
    (
        qkv_t, prob_a, prob_b, ctx_t, x_t, normed_t, hidden_t, unit1, inv1, unit2, inv2, deriv,
        wqkv, wout, win, wback, gain_one, gain_two,
    ) = call(
        forward_kernel,
        [
            ((3 * D, SEQ), BF), ((HEADS, HALF, SEQ), F32), ((HEADS, HALF, HALF), F32),
            ((D, SEQ), BF), ((D, SEQ), BF), ((D, SEQ), BF), ((FF, SEQ), BF),
            (tok, F32), ((SEQ, 1), F32), (tok, F32), ((SEQ, 1), F32), ((SEQ, FF), F32),
            ((D, 3 * D), BF), ((D, D), BF), ((D, FF), BF), ((FF, D), BF), ((1, D), F32),
            ((1, D), F32),
        ],
        [(tok, BF), pltpu.SemaphoreType.DMA((7,))],
        [lengths] + [pltpu.with_memory_space_constraint(a, pltpu.HBM) for a in (x, w_qkv[0], w_out[0], w_in[0], w_back[0], gain_attn, gain_ffn)],
        10_000_000,
        "forward",
        operands=HB,
        grant=GRANT,
    )
    low_msg, high_msg = ((LOW + 16, D), BF), ((HIGH + 16, D), BF)
    relaxed, resid_low, resid_high = call(
        relax_kernel,
        [(tok, BF), low_msg, high_msg],
        [((3 * D, SEQ), BF)],
        [meta, above, cotangent, own_guess, coarse_rate, qkv_t, prob_a, prob_b, unit1, inv1,
         unit2, inv2, deriv, wqkv, wout, win, wback, gain_one, gain_two],
        0,
        "relax",
    )
    from1 = lax.ppermute(resid_low, LAYER, [(12, 8), (8, 4), (15, 11)])
    from2 = lax.ppermute(resid_low, LAYER, [(12, 4), (15, 7)])
    from3 = lax.ppermute(resid_low, LAYER, [(15, 3)])
    shifted = lax.ppermute(
        relaxed, LAYER, [(at(j, i), at(j, i - 1)) for j in range(4) for i in range(1, 4)]
    )
    across = lax.ppermute(resid_high, LAYER, [(4, 7), (8, 11), (12, 15)])
    (low,) = call(
        compose_low_kernel, [low_msg], [],
        [meta, relaxed, own_guess, coarse_rate, from1, from2], 0, "low",
    )
    composed = lax.ppermute(low, LAYER, [(4, 3), (8, 7), (12, 11)])
    (high,) = call(
        compose_high_kernel, [high_msg], [],
        [meta, after(relaxed, low), own_guess, across], 0, "high",
    )
    high1 = lax.ppermute(high, LAYER, [(15, 11), (11, 7), (7, 3)])
    high2 = lax.ppermute(high, LAYER, [(15, 7), (11, 3)])
    high3 = lax.ppermute(high, LAYER, [(15, 3)])
    d2, gain2, error, error_bf, keep_b, send_b = call(
        chain_kernel,
        [(tok, F32), ((8, D), F32), (tok, F32), (tok, BF), ((8, FF // 16, D), BF),
         ((8, FF // 16, D), BF)],
        [((FF, D), BF)],
        [meta, shifted, composed, from1, from2, from3, high1, high2, high3, above, cotangent,
         own_guess, relaxed, unit2, inv2, gain_two, hidden_t],
        10_000_000,
        "chain",
    )
    wrapped = lax.ppermute(error_bf, LAYER, [(at(j, 3), at(j, 0)) for j in range(4)])
    b0 = by_flip(ORDER_BACK[0], send_b)
    part_i = (8, D // 16, WIDE)
    d1, keep_i, send_i = call(
        ffn_kernel,
        [(tok, F32), (part_i, BF), (part_i, BF)],
        [((SEQ, FF), BF), ((D, WIDE), BF)],
        [meta, d2, deriv, unit1, inv1, win, wback, gain_one, normed_t, ctx_t, gain2],
        10_000_000,
        "ffn",
    )
    send_b = passing([keep_b, b0])
    b1 = by_flip(ORDER_BACK[1], send_b)
    i0 = by_flip(ORDER_IN[0], send_i)
    part_q = (8, D // 16, 3 * D)
    dqkv, keep_q, send_q = call(
        attention_kernel,
        [((SEQ, 3 * D), BF), (part_q, BF), (part_q, BF)],
        [((3 * D, SEQ), BF), ((D, 3 * D), BF)],
        [meta, after(d1, send_b), wout, qkv_t, prob_a, prob_b, x_t],
        10_000_000,
        "attention",
    )
    q0 = by_flip(ORDER_QKV[0], send_q)
    send_i = passing([keep_i, after(i0, dqkv)])
    i1 = by_flip(ORDER_IN[1], send_i)
    (swept,) = call(
        state_kernel, [(tok, BF)], [], [after(d1, send_i), dqkv, wqkv], 10_000_000, "state", 0
    )
    send_q = passing([keep_q, after(q0, swept)])
    q1 = by_flip(ORDER_QKV[1], send_q)
    send_b = passing([keep_b, b0, after(b1, send_q)])
    b2 = by_flip(ORDER_BACK[2], send_b)
    send_q = passing([keep_q, q0, after(q1, send_b)])
    q2 = by_flip(ORDER_QKV[2], send_q)
    (mixed,) = call(
        mix_kernel, [(tok, BF)], [], [after(error_bf, send_q), wrapped], 0, "mix", 0
    )
    passed = lax.ppermute(
        mixed,
        LAYER,
        [(at(j, 3), at(j, 2)) for j in range(4)] + [(at(j, 0), at(j, 1)) for j in range(4)],
    )
    send_i = passing([keep_i, i0, after(i1, mixed)])
    i2 = by_flip(ORDER_IN[2], send_i)
    send_b = passing([keep_b, b0, b1, after(b2, send_i)])
    b3 = by_flip(ORDER_BACK[3], send_b)
    send_q = passing([keep_q, q0, q1, after(q2, send_b)])
    q3 = by_flip(ORDER_QKV[3], send_q)
    send_i = passing([keep_i, i0, i1, after(i2, send_q)])
    i3 = by_flip(ORDER_IN[3], send_i)
    adjoint, coarse_err = call(
        finish_kernel, [(tok, BF), (tok, F32)],
        [(tok, BF), (tok, F32), pltpu.SemaphoreType.DMA((2,))],
        [meta, error, wrapped, passed, relaxed, own_guess, coarse_rate, after(swept, send_i)],
        0, "finish", into=[HB, HB],
    )
    (share_q,) = call(
        qkv_kernel, [((D // 16, 3 * D), F32)],
        [((D // 16, 3 * D), F32), pltpu.SemaphoreType.DMA((1,))],
        [keep_q, q0, q1, q2, after(q3, adjoint)], 1_000_000, "qkv", 0, into=[HB],
    )
    share_back, share_in, share_out, share_one, share_two = call(
        shares_kernel,
        [((FF // 16, D), F32), ((D // 16, FF), F32), ((D // 16, D), F32), ((1, 32), F32),
         ((1, 32), F32)],
        [((FF // 16, D), F32), ((D // 16, WIDE), F32), pltpu.SemaphoreType.DMA((3,))],
        [keep_b, b0, b1, b2, b3, keep_i, i0, i1, i2, after(i3, share_q)],
        1_000_000, "shares", 0, into=[HB, HB, HB, VM, VM],
    )
    return (
        adjoint[None],
        coarse_err[None],
        share_q[None],
        share_out[None],
        share_in[None],
        share_back[None],
        share_one,
        share_two,
    )


def solution(mesh):
    torus = Mesh(mesh.devices.reshape(4, 4, 4, 2, 2), LAYER + DP)
    return jax.shard_map(
        on_device,
        mesh=torus,
        in_specs=(
            P(LAYER, DP, None),
            P(LAYER, DP, None),
            P(DP, None),
            P(DP),
            P(LAYER, None),
            P(LAYER, None, None),
            P(LAYER, None, None),
            P(LAYER, None, None),
            P(LAYER, None, None),
            P(LAYER, None),
            P(LAYER, None),
        ),
        out_specs=(
            P(LAYER, DP, None),
            P(LAYER, DP, None),
            P(LAYER, DP, None),
            P(LAYER, DP, None),
            P(LAYER, DP, None),
            P(LAYER, DP, None),
            P(LAYER, DP),
            P(LAYER, DP),
        ),
        check_vma=False,
    )
```

```python
import functools

import jax
import jax.numpy as jnp
from jax import lax
from jax.experimental import pallas as pl
from jax.experimental.pallas import tpu as pltpu
from jax.sharding import Mesh
from jax.sharding import PartitionSpec as P

D = 512
FF = 2048
HEAD_DIM = 64
HEADS = D // HEAD_DIM
SEQ = 256
HALF = SEQ // 2
FACTOR = 4
LAYER = ("ly", "lz")
DP = ("x", "zl", "core")

EPS = 1e-05
DEPTH_GAIN = 6.73
CUBIC = 0.044715
TANH_SCALE = 0.7978845608028654
SCORE_SCALE = HEAD_DIM ** (-0.5)
LOW = 192
HIGH = SEQ - LOW
GRANT = 16
MAIN = 5_000_000_000
LIGHT = 1_000_000_000

BF = jnp.bfloat16
F32 = jnp.float32


def nn(a, b):
    return lax.dot_general(a, b, (((1,), (0,)), ((), ())), preferred_element_type=F32)


def nt(a, b):
    return lax.dot_general(a, b, (((1,), (1,)), ((), ())), preferred_element_type=F32)


def tn(a, b):
    return lax.dot_general(a, b, (((0,), (0,)), ((), ())), preferred_element_type=F32)


def row_mean(a):
    return jnp.sum(a, axis=-1, keepdims=True) * (1.0 / D)


def unit_of(rows):
    center = rows - row_mean(rows)
    inv = lax.rsqrt(row_mean(center * center) + EPS)
    return center * inv, inv


def norm_back(up, unit, inv, gain):
    scaled = up * gain
    return inv * (scaled - row_mean(scaled) - unit * row_mean(scaled * unit))


def forward_kernel(
    lengths, x_hbm, wqkv_hbm, wout_hbm, win_hbm, wback_hbm, g1_hbm, g2_hbm,
    qkv_t, prob_a, prob_b, ctx_t, x_t, normed_t, hidden_t, unit1, inv1, unit2, inv2, deriv,
    wqkv, wout, win, wback, g1, g2, x_ref, sem,
):
    pairs = (
        (x_hbm, x_ref), (wqkv_hbm, wqkv), (wout_hbm, wout), (g1_hbm, g1),
        (win_hbm, win), (wback_hbm, wback), (g2_hbm, g2),
    )
    copies = [pltpu.make_async_copy(a, b, sem.at[n]) for n, (a, b) in enumerate(pairs)]
    for copy in copies:
        copy.start()
    length = lengths[0]
    copies[0].wait()
    x = x_ref[...]
    x_t[...] = x.T
    copies[1].wait()
    for j in range(3):
        part = nn(x, wqkv[:, j * D : (j + 1) * D]).astype(BF)
        qkv_t[j * D : (j + 1) * D, :] = part.T
    key = lax.broadcasted_iota(jnp.int32, (HALF, SEQ), 0)
    query = lax.broadcasted_iota(jnp.int32, (HALF, SEQ), 1)
    allow_a = key <= query
    key_b, query_b = key[:, :HALF], query[:, :HALF]
    allow_b = (key_b <= query_b) & (key_b + HALF < length)
    for h in range(HEADS):
        lo, hi = h * HEAD_DIM, (h + 1) * HEAD_DIM
        q = qkv_t[lo:hi, :]
        k = qkv_t[D + lo : D + hi, :]
        v = qkv_t[2 * D + lo : 2 * D + hi, :]
        s_a = jnp.where(allow_a, tn(k[:, :HALF], q), -1e30)
        s_b = jnp.where(allow_b, tn(k[:, HALF:], q[:, HALF:]), -1e30)
        m_a = jnp.max(s_a, axis=0, keepdims=True)
        m_b = jnp.max(s_b, axis=0, keepdims=True)
        m_1 = jnp.maximum(m_a[:, HALF:], m_b)
        top = jnp.concatenate([m_a[:, :HALF], m_1], axis=1)
        e_a = jnp.exp((s_a - top) * SCORE_SCALE)
        e_b = jnp.exp((s_b - m_1) * SCORE_SCALE)
        t_a = jnp.sum(e_a, axis=0, keepdims=True)
        t_1 = t_a[:, HALF:] + jnp.sum(e_b, axis=0, keepdims=True)
        r_1 = 1.0 / t_1
        r_a = jnp.concatenate([1.0 / t_a[:, :HALF], r_1], axis=1)
        p_a = e_a * r_a
        p_b = e_b * r_1
        prob_a[h] = p_a
        prob_b[h] = p_b
        c_a = nn(v[:, :HALF], p_a.astype(BF))
        c_b = nn(v[:, HALF:], p_b.astype(BF))
        ctx_t[lo:hi, :HALF] = c_a[:, :HALF].astype(BF)
        ctx_t[lo:hi, HALF:] = (c_a[:, HALF:] + c_b).astype(BF)
    copies[2].wait()
    copies[3].wait()
    first = DEPTH_GAIN * x.astype(F32) + tn(ctx_t[...], wout[...])
    u1, i1 = unit_of(first)
    unit1[...] = u1
    inv1[...] = i1
    normed = u1 * g1[...]
    normed_bf = normed.astype(BF)
    normed_t[...] = normed_bf.T
    second = DEPTH_GAIN * normed
    copies[4].wait()
    copies[5].wait()
    copies[6].wait()
    for j in range(FF // D):
        cols = slice(j * D, (j + 1) * D)
        pre = nn(normed_bf, win[:, cols])
        sq = pre * pre
        t = jnp.tanh(pre * (TANH_SCALE + (TANH_SCALE * CUBIC) * sq))
        gate = 0.5 + 0.5 * t
        hid = (pre * gate).astype(BF)
        deriv[:, cols] = gate + pre * (1.0 - t * t) * (
            0.5 * TANH_SCALE + (1.5 * TANH_SCALE * CUBIC) * sq
        )
        hidden_t[cols, :] = hid.T
        second = second + nn(hid, wback[cols, :])
    u2, i2 = unit_of(second)
    unit2[...] = u2
    inv2[...] = i2


def ffn_back(d2, d2_bf, deriv, win, wback, keep=None):
    dn = DEPTH_GAIN * d2
    for j in range(FF // D):
        cols = slice(j * D, (j + 1) * D)
        du = (nt(d2_bf, wback[cols, :]) * deriv[:, cols]).astype(BF)
        if keep is not None:
            keep[:, cols] = du
        dn = dn + nt(du, win[:, cols])
    return dn


def attention_back(d1_bf, wout, qkv_t, prob_a, prob_b, dqkv_t):
    dctx_t = nt(d1_bf, wout[...]).astype(BF).T
    for h in range(HEADS):
        lo, hi = h * HEAD_DIM, (h + 1) * HEAD_DIM
        q = qkv_t[lo:hi, :]
        k = qkv_t[D + lo : D + hi, :]
        v = qkv_t[2 * D + lo : 2 * D + hi, :]
        dc = dctx_t[lo:hi, :]
        p_a, p_b = prob_a[h], prob_b[h]
        dp_a = tn(v[:, :HALF], dc)
        dp_b = tn(v[:, HALF:], dc[:, HALF:])
        w_a = jnp.sum(p_a * dp_a, axis=0, keepdims=True)
        w_1 = w_a[:, HALF:] + jnp.sum(p_b * dp_b, axis=0, keepdims=True)
        w = jnp.concatenate([w_a[:, :HALF], w_1], axis=1)
        ds_a = (p_a * (dp_a - w) * SCORE_SCALE).astype(BF)
        ds_b = (p_b * (dp_b - w_1) * SCORE_SCALE).astype(BF)
        dq = nn(k[:, :HALF], ds_a)
        dqkv_t[lo:hi, :HALF] = dq[:, :HALF].astype(BF)
        dqkv_t[lo:hi, HALF:] = (dq[:, HALF:] + nn(k[:, HALF:], ds_b)).astype(BF)
        dqkv_t[D + lo : D + hi, :HALF] = nt(q, ds_a).astype(BF)
        dqkv_t[D + lo : D + hi, HALF:] = nt(q[:, HALF:], ds_b).astype(BF)
        dqkv_t[2 * D + lo : 2 * D + hi, :HALF] = nt(dc, p_a.astype(BF)).astype(BF)
        dqkv_t[2 * D + lo : 2 * D + hi, HALF:] = nt(dc[:, HALF:], p_b.astype(BF)).astype(BF)


def state_back(d1, dqkv, wqkv):
    return DEPTH_GAIN * d1 + nt(dqkv, wqkv[...])


def thirds(full):
    high = full.astype(BF)
    rest = full - high.astype(F32)
    mid = rest.astype(BF)
    low = (rest - mid.astype(F32)).astype(BF)
    parts = [part.astype(F32) for part in (high, mid, low)]
    return jnp.concatenate(parts + [jnp.zeros((13, D), F32)], axis=0).astype(BF)


def whole_of(msg):
    tail = msg[msg.shape[0] - 16 :, :].astype(F32)
    return tail[0:1, :] + tail[1:2, :] + tail[2:3, :]


def rows_of(msg):
    return msg[: msg.shape[0] - 16, :].astype(F32)


def relax_kernel(
    meta, above, cot, guess, rate,
    qkv_t, prob_a, prob_b, unit1, inv1, unit2, inv2, deriv, wqkv, wout, win, wback, g1, g2,
    relaxed_out, resid_low, resid_high, dqkv_t,
):
    last = meta[1] == 1
    up = jnp.where(last, cot[...].astype(F32), above[...].astype(F32))
    d2 = norm_back(up, unit2[...], inv2[...], g2[...])
    dn = ffn_back(d2, d2.astype(BF), deriv, win, wback)
    d1 = norm_back(dn, unit1[...], inv1[...], g1[...])
    attention_back(d1.astype(BF), wout, qkv_t, prob_a, prob_b, dqkv_t)
    relaxed = state_back(d1, dqkv_t[...].T, wqkv).astype(BF)
    relaxed_out[...] = relaxed
    resid = (relaxed.astype(F32) - guess[...].astype(F32)).astype(BF)
    tail = thirds(rate[...])
    resid_low[:LOW, :] = resid[:LOW, :]
    resid_low[LOW:, :] = tail
    resid_high[:HIGH, :] = resid[LOW:, :]
    resid_high[HIGH:, :] = tail


def compose_low_kernel(meta, relaxed, guess, rate, one, two, out):
    resid = relaxed[:LOW, :].astype(F32) - guess[:LOW, :].astype(F32)
    r1, r2 = whole_of(one), whole_of(two)
    higher = rows_of(one) + r1 * rows_of(two)
    out[:LOW, :] = (resid + rate[...] * higher).astype(BF)
    y = meta[4]
    factor = rate[...] * jnp.where(y < 3, r1, 1.0) * jnp.where(y < 2, r2, 1.0)
    out[LOW:, :] = thirds(factor)


def compose_high_kernel(meta, relaxed, guess, across, out):
    resid = relaxed[LOW:, :].astype(F32) - guess[LOW:, :].astype(F32)
    top = jnp.where(meta[1] == 1, resid, 0.0)
    out[:HIGH, :] = (rows_of(across) + whole_of(across) * top).astype(BF)
    out[HIGH:, :] = across[HIGH:, :]


def mix_kernel(error_bf, wrapped, out):
    out[...] = (error_bf[...].astype(F32) + wrapped[...].astype(F32)).astype(BF)


def finish_kernel(
    meta, error, wrapped, passed, relaxed, guess, rate, swept, adjoint, coarse_err,
    adjoint_v, error_v, sem,
):
    last, own_known, z = meta[1] == 1, (meta[0] + meta[2]) > 0, meta[5]
    far = wrapped[...].astype(F32) + jnp.where(z == 0, 0.0, passed[...].astype(F32))
    reached = jnp.where(own_known, error[...], far)
    guess_f = guess[...].astype(F32)
    resid = relaxed[...].astype(F32) - guess_f
    value = jnp.where(z == 0, rate[...] * reached + resid, reached)
    error_v[...] = value
    first = pltpu.make_async_copy(error_v, coarse_err, sem.at[0])
    first.start()
    coarse = (z == 0) | last
    kept = jnp.where(coarse, guess_f + value, swept[...].astype(F32))
    adjoint_v[...] = kept.astype(BF)
    second = pltpu.make_async_copy(adjoint_v, adjoint, sem.at[1])
    second.start()
    first.wait()
    second.wait()


FLIPS = {"core": 1, "zl": 2, "x0": 4, "x1": 12}


def flip_of(position, order):
    flip = 0
    for bit, name in enumerate(order):
        if position & (8 >> bit):
            flip ^= FLIPS[name]
    return flip


ORDER_BACK = ("core", "x0", "x1", "zl")
ORDER_IN = ("core", "x1", "x0", "zl")
ORDER_QKV = ("core", "zl", "x1", "x0")
WIDE = FF + 128


def place(whole, rows, order, me, keep, send):
    for p in range(16):
        start = pl.multiple_of((me ^ flip_of(p, order)) * rows, rows)
        target = keep if p < 8 else send
        target[p % 8] = whole[pl.ds(start, rows), :]


def chain_kernel(
    meta, shifted_ref, composed, top1, top2, top3, high1, high2, high3,
    above, cot, guess, relaxed, unit2, inv2, g2, hidden_t,
    d2_out, gain2_out, error_out, error_bf, keep, send, whole,
):
    last = meta[1] == 1
    chained = meta[2] == 1
    me = meta[3]
    shifted = shifted_ref[...].astype(F32)
    above_f = above[...].astype(F32)
    top = rows_of(top1) + rows_of(top2) + rows_of(top3)
    low = rows_of(composed) + whole_of(composed) * top
    high = rows_of(high1) + whole_of(high1) * (
        rows_of(high2) + whole_of(high2) * rows_of(high3)
    )
    far = jnp.concatenate([low, high], axis=0)
    near = shifted - above_f
    own = relaxed[...].astype(F32) - guess[...].astype(F32)
    error = jnp.where(last, own, jnp.where(meta[0] == 1, far, near))
    error_out[...] = error
    error_bf[...] = jnp.where(meta[0] == 1, error, 0.0).astype(BF)
    corrected = (above_f + error).astype(BF).astype(F32)
    up = jnp.where(last, cot[...].astype(F32), jnp.where(chained, corrected, shifted))
    u2 = unit2[...]
    d2 = norm_back(up, u2, inv2[...], g2[...])
    gain2_out[...] = jnp.broadcast_to(jnp.sum(up * u2, axis=0, keepdims=True), (8, D))
    d2_out[...] = d2
    d2_bf = d2.astype(BF)
    for j in range(FF // D):
        rows = slice(j * D, (j + 1) * D)
        whole[rows, :] = nn(hidden_t[rows, :], d2_bf).astype(BF)
    place(whole, FF // 16, ORDER_BACK, me, keep, send)


def ffn_kernel(
    meta, d2, deriv, unit1, inv1, win, wback, g1, normed_t, gain2,
    d1_out, keep, send, du, whole,
):
    me = meta[3]
    d2v = d2[...]
    dn = ffn_back(d2v, d2v.astype(BF), deriv, win, wback, du)
    u1 = unit1[...]
    gain1 = jnp.broadcast_to(jnp.sum(dn * u1, axis=0, keepdims=True), (8, D))
    d1_out[...] = norm_back(dn, u1, inv1[...], g1[...])
    for j in range(FF // D):
        cols = slice(j * D, (j + 1) * D)
        whole[:, cols] = nn(normed_t[...], du[:, cols]).astype(BF)
    pair = jnp.concatenate([gain1, gain2[...], jnp.zeros((112, D), F32)], axis=0)
    whole[:, FF:] = pair.T.astype(BF)
    place(whole, D // 16, ORDER_IN, me, keep, send)


def attention_kernel(
    meta, d1, wout, qkv_t, prob_a, prob_b, x_t, ctx_t, dqkv_out, keep, send, dqkv_t, whole,
):
    d1_bf = d1[...].astype(BF)
    attention_back(d1_bf, wout, qkv_t, prob_a, prob_b, dqkv_t)
    whole[:, 3 * D :] = nn(ctx_t[...], d1_bf).astype(BF)
    for j in range(3):
        cols = slice(j * D, (j + 1) * D)
        part = dqkv_t[cols, :].T
        dqkv_out[:, cols] = part
        whole[:, cols] = nn(x_t[...], part).astype(BF)
    place(whole, D // 16, ORDER_QKV, meta[3], keep, send)


def state_kernel(d1, dqkv, wqkv, out):
    out[...] = state_back(d1[...], dqkv[...], wqkv).astype(BF)


HB = pl.BlockSpec(memory_space=pltpu.HBM)
VM = pl.BlockSpec(memory_space=pltpu.VMEM)
SM = pl.BlockSpec(memory_space=pltpu.SMEM)


def call(kernel, outs, scratch, args, flops, name, scalars=1, operands=VM, grant=16, into=None):
    shapes = [jax.ShapeDtypeStruct(s, t) for s, t in outs]
    return pl.pallas_call(
        kernel,
        out_shape=shapes,
        in_specs=[SM] * scalars + [operands] * (len(args) - scalars),
        out_specs=into or [VM] * len(shapes),
        scratch_shapes=[s if not isinstance(s, tuple) else pltpu.VMEM(*s) for s in scratch],
        compiler_params=pltpu.CompilerParams(vmem_limit_bytes=grant * 1024 * 1024),
        cost_estimate=pl.CostEstimate(flops=MAIN if flops > 5 else LIGHT, bytes_accessed=0, transcendentals=0),
        name=name,
    )(*args)


def by_flip(name, x):
    if name == "core":
        return lax.ppermute(x, "core", [(0, 1), (1, 0)])
    if name == "zl":
        return lax.ppermute(x, "zl", [(0, 1), (1, 0)])
    mask = 1 if name == "x0" else 3
    return lax.ppermute(x, "x", [(i, i ^ mask) for i in range(4)])


def sum_kernel(*refs):
    out = refs[-1]
    size = out.shape[0]
    total = refs[0][size : 2 * size].astype(F32)
    for ref in refs[1:-1]:
        total = total + ref[size : 2 * size].astype(F32)
    out[...] = total.astype(BF)


def passing(parts):
    shape = parts[-1].shape
    (out,) = call(
        sum_kernel, [((shape[0] // 2,) + shape[1:], BF)], [], list(parts), 0, "sum", 0
    )
    return out


def total_of(parts):
    total = parts[0][0].astype(F32)
    for part in parts[1:]:
        total = total + part[0].astype(F32)
    return total


def shares_kernel(
    k0, k1, k2, k3, k4, i0, i1, i2, i3, i4, back, inner, gain1, gain2,
    back_v, in_v, sem,
):
    back_v[...] = total_of((k0, k1, k2, k3, k4))
    first = pltpu.make_async_copy(back_v, back, sem.at[0])
    first.start()
    in_v[...] = total_of((i0, i1, i2, i3, i4))
    second = pltpu.make_async_copy(in_v.at[:, :FF], inner, sem.at[1])
    second.start()
    turned = jnp.concatenate([in_v[:, FF:], jnp.zeros((96, 128), F32)], axis=0).T
    gain1[...] = turned[0:1, :32]
    gain2[...] = turned[8:9, :32]
    first.wait()
    second.wait()


def qkv_kernel(k0, k1, k2, k3, k4, out, outer, whole, sem):
    whole[...] = total_of((k0, k1, k2, k3, k4))
    first = pltpu.make_async_copy(whole.at[:, : 3 * D], out, sem.at[0])
    second = pltpu.make_async_copy(whole.at[:, 3 * D :], outer, sem.at[1])
    first.start()
    second.start()
    first.wait()
    second.wait()


def after(x, *done):
    return lax.optimization_barrier((x,) + done)[0]


def at(y, z):
    return FACTOR * y + z


def on_device(
    states, guess, cotangent, lengths, coarse_rate, w_qkv, w_out, w_in, w_back, gain_attn, gain_ffn
):
    x, own_guess = states[0], guess[0]
    y, z = lax.axis_index("ly"), lax.axis_index("lz")
    layer = at(y, z)
    last = layer == 15
    chained = (z == 3) & ~last | (layer == 14)
    meta = jnp.stack(
        [(z == 3).astype(jnp.int32), last.astype(jnp.int32), chained.astype(jnp.int32), lax.axis_index(DP), y, z]
    )
    above = lax.ppermute(own_guess, LAYER, [(i, i - 1) for i in range(1, 16)])

    tok = (SEQ, D)
    (
        qkv_t, prob_a, prob_b, ctx_t, x_t, normed_t, hidden_t, unit1, inv1, unit2, inv2, deriv,
        wqkv, wout, win, wback, gain_one, gain_two,
    ) = call(
        forward_kernel,
        [
            ((3 * D, SEQ), BF), ((HEADS, HALF, SEQ), F32), ((HEADS, HALF, HALF), F32),
            ((D, SEQ), BF), ((D, SEQ), BF), ((D, SEQ), BF), ((FF, SEQ), BF),
            (tok, F32), ((SEQ, 1), F32), (tok, F32), ((SEQ, 1), F32), ((SEQ, FF), F32),
            ((D, 3 * D), BF), ((D, D), BF), ((D, FF), BF), ((FF, D), BF), ((1, D), F32),
            ((1, D), F32),
        ],
        [(tok, BF), pltpu.SemaphoreType.DMA((7,))],
        [lengths] + [pltpu.with_memory_space_constraint(a, pltpu.HBM) for a in (x, w_qkv[0], w_out[0], w_in[0], w_back[0], gain_attn, gain_ffn)],
        9,
        "forward",
        operands=HB,
        grant=GRANT,
    )
    low_msg, high_msg = ((LOW + 16, D), BF), ((HIGH + 16, D), BF)
    relaxed, resid_low, resid_high = call(
        relax_kernel,
        [(tok, BF), low_msg, high_msg],
        [((3 * D, SEQ), BF)],
        [meta, above, cotangent, own_guess, coarse_rate, qkv_t, prob_a, prob_b, unit1, inv1,
         unit2, inv2, deriv, wqkv, wout, win, wback, gain_one, gain_two],
        9,
        "relax",
    )
    from1 = lax.ppermute(resid_low, LAYER, [(12, 8), (8, 4), (15, 11)])
    from2 = lax.ppermute(resid_low, LAYER, [(12, 4), (15, 7)])
    shifted = lax.ppermute(
        relaxed, LAYER, [(at(j, i), at(j, i - 1)) for j in range(4) for i in range(1, 4)]
    )
    across = lax.ppermute(resid_high, LAYER, [(4, 7), (8, 11), (12, 15)])
    from3 = lax.ppermute(resid_low, LAYER, [(15, 3)])
    (low,) = call(
        compose_low_kernel, [low_msg], [],
        [meta, relaxed, own_guess, coarse_rate, from1, from2], 0, "low",
    )
    composed = lax.ppermute(low, LAYER, [(4, 3), (8, 7), (12, 11)])
    (high,) = call(
        compose_high_kernel, [high_msg], [],
        [meta, after(relaxed, low), own_guess, across], 0, "high",
    )
    high1 = lax.ppermute(high, LAYER, [(15, 11), (11, 7), (7, 3)])
    high2 = lax.ppermute(high, LAYER, [(15, 7), (11, 3)])
    high3 = lax.ppermute(high, LAYER, [(15, 3)])
    d2, gain2, error, error_bf, keep_b, send_b = call(
        chain_kernel,
        [(tok, F32), ((8, D), F32), (tok, F32), (tok, BF), ((8, FF // 16, D), BF),
         ((8, FF // 16, D), BF)],
        [((FF, D), BF)],
        [meta, shifted, composed, from1, from2, from3, high1, high2, high3, above, cotangent,
         own_guess, relaxed, unit2, inv2, gain_two, hidden_t],
        9,
        "chain",
    )
    wrapped = lax.ppermute(error_bf, LAYER, [(at(j, 3), at(j, 0)) for j in range(4)])
    b0 = by_flip(ORDER_BACK[0], send_b)
    part_i = (8, D // 16, WIDE)
    d1, keep_i, send_i = call(
        ffn_kernel,
        [(tok, F32), (part_i, BF), (part_i, BF)],
        [((SEQ, FF), BF), ((D, WIDE), BF)],
        [meta, d2, deriv, unit1, inv1, win, wback, gain_one, normed_t, gain2],
        9,
        "ffn",
    )
    i0 = by_flip(ORDER_IN[0], send_i)
    part_q = (8, D // 16, 4 * D)
    dqkv, keep_q, send_q = call(
        attention_kernel,
        [((SEQ, 3 * D), BF), (part_q, BF), (part_q, BF)],
        [((3 * D, SEQ), BF), ((D, 4 * D), BF)],
        [meta, d1, wout, qkv_t, prob_a, prob_b, x_t, ctx_t],
        9,
        "attention",
    )
    q0 = by_flip(ORDER_QKV[0], send_q)
    send_i = passing([keep_i, after(i0, dqkv)])
    i1 = by_flip(ORDER_IN[1], send_i)
    send_b = passing([keep_b, after(b0, send_i)])
    b1 = by_flip(ORDER_BACK[1], send_b)
    (swept,) = call(
        state_kernel, [(tok, BF)], [], [after(d1, send_b), dqkv, wqkv], 9, "state", 0
    )
    send_q = passing([keep_q, after(q0, swept)])
    q1 = by_flip(ORDER_QKV[1], send_q)
    (mixed,) = call(
        mix_kernel, [(tok, BF)], [], [after(error_bf, send_q), wrapped], 0, "mix", 0
    )
    send_i = passing([keep_i, i0, after(i1, mixed)])
    i2 = by_flip(ORDER_IN[2], send_i)
    send_b = passing([keep_b, b0, after(b1, send_i)])
    b2 = by_flip(ORDER_BACK[2], send_b)
    passed = lax.ppermute(
        after(mixed, send_b),
        LAYER,
        [(at(j, 3), at(j, 2)) for j in range(4)] + [(at(j, 0), at(j, 1)) for j in range(4)],
    )
    send_q = passing([keep_q, q0, after(q1, send_b)])
    q2 = by_flip(ORDER_QKV[2], send_q)
    send_i = passing([keep_i, i0, i1, after(i2, send_q)])
    i3 = by_flip(ORDER_IN[3], send_i)
    send_b = passing([keep_b, b0, b1, after(b2, send_i)])
    b3 = by_flip(ORDER_BACK[3], send_b)
    send_q = passing([keep_q, q0, q1, after(q2, send_b)])
    q3 = by_flip(ORDER_QKV[3], send_q)
    adjoint, coarse_err = call(
        finish_kernel, [(tok, BF), (tok, F32)],
        [(tok, BF), (tok, F32), pltpu.SemaphoreType.DMA((2,))],
        [meta, error, wrapped, passed, relaxed, own_guess, coarse_rate, after(swept, send_q)],
        0, "finish", into=[HB, HB],
    )
    share_back, share_in, share_one, share_two = call(
        shares_kernel,
        [((FF // 16, D), F32), ((D // 16, FF), F32), ((1, 32), F32), ((1, 32), F32)],
        [((FF // 16, D), F32), ((D // 16, WIDE), F32), pltpu.SemaphoreType.DMA((2,))],
        [keep_b, b0, b1, b2, b3, keep_i, i0, i1, i2, after(i3, adjoint)],
        0, "shares", 0, into=[HB, HB, VM, VM],
    )
    share_q, share_out = call(
        qkv_kernel, [((D // 16, 3 * D), F32), ((D // 16, D), F32)],
        [((D // 16, 4 * D), F32), pltpu.SemaphoreType.DMA((2,))],
        [keep_q, q0, q1, q2, after(q3, share_in)], 0, "qkv", 0, into=[HB, HB],
    )
    return (
        adjoint[None],
        coarse_err[None],
        share_q[None],
        share_out[None],
        share_in[None],
        share_back[None],
        share_one,
        share_two,
    )


def solution(mesh):
    torus = Mesh(mesh.devices.reshape(4, 4, 4, 2, 2), LAYER + DP)
    return jax.shard_map(
        on_device,
        mesh=torus,
        in_specs=(
            P(LAYER, DP, None),
            P(LAYER, DP, None),
            P(DP, None),
            P(DP),
            P(LAYER, None),
            P(LAYER, None, None),
            P(LAYER, None, None),
            P(LAYER, None, None),
            P(LAYER, None, None),
            P(LAYER, None),
            P(LAYER, None),
        ),
        out_specs=(
            P(LAYER, DP, None),
            P(LAYER, DP, None),
            P(LAYER, DP, None),
            P(LAYER, DP, None),
            P(LAYER, DP, None),
            P(LAYER, DP, None),
            P(LAYER, DP),
            P(LAYER, DP),
        ),
        check_vma=False,
    )
```

```python
import functools

import jax
import jax.numpy as jnp
from jax import lax
from jax.experimental import pallas as pl
from jax.experimental.pallas import tpu as pltpu
from jax.sharding import Mesh
from jax.sharding import PartitionSpec as P

D = 512
FF = 2048
HEAD_DIM = 64
HEADS = D // HEAD_DIM
SEQ = 256
HALF = SEQ // 2
FACTOR = 4
LAYER = ("ly", "lz")
DP = ("x", "zl", "core")

EPS = 1e-05
DEPTH_GAIN = 6.73
CUBIC = 0.044715
TANH_SCALE = 0.7978845608028654
SCORE_SCALE = HEAD_DIM ** (-0.5)
LOW = 192
HIGH = SEQ - LOW
GRANT = 16
MAIN = 5_000_000_000
LIGHT = 1_000_000_000
STAGE1 = 4_000_000_000
BIG = 6_000_000_000

BF = jnp.bfloat16
F32 = jnp.float32


def nn(a, b):
    return lax.dot_general(a, b, (((1,), (0,)), ((), ())), preferred_element_type=F32)


def nt(a, b):
    return lax.dot_general(a, b, (((1,), (1,)), ((), ())), preferred_element_type=F32)


def tn(a, b):
    return lax.dot_general(a, b, (((0,), (0,)), ((), ())), preferred_element_type=F32)


def row_mean(a):
    return jnp.sum(a, axis=-1, keepdims=True) * (1.0 / D)


def unit_of(rows):
    center = rows - row_mean(rows)
    inv = lax.rsqrt(row_mean(center * center) + EPS)
    return center * inv, inv


def norm_back(up, unit, inv, gain):
    scaled = up * gain
    return inv * (scaled - row_mean(scaled) - unit * row_mean(scaled * unit))


def forward_kernel(
    lengths, x_hbm, wqkv_hbm, wout_hbm, win_hbm, wback_hbm, g1_hbm, g2_hbm,
    qkv_t, prob_a, prob_b, ctx_t, x_t, normed_t, hidden_t, unit1, inv1, unit2, inv2, deriv,
    wqkv, wout, win, wback, g1, g2, x_ref, sem,
):
    pairs = (
        (x_hbm, x_ref), (wqkv_hbm, wqkv), (wout_hbm, wout), (g1_hbm, g1),
        (win_hbm, win), (wback_hbm, wback), (g2_hbm, g2),
    )
    copies = [pltpu.make_async_copy(a, b, sem.at[n]) for n, (a, b) in enumerate(pairs)]
    for copy in copies:
        copy.start()
    length = lengths[0]
    copies[0].wait()
    x = x_ref[...]
    x_t[...] = x.T
    copies[1].wait()
    for j in range(3):
        part = nn(x, wqkv[:, j * D : (j + 1) * D]).astype(BF)
        qkv_t[j * D : (j + 1) * D, :] = part.T
    key = lax.broadcasted_iota(jnp.int32, (HALF, SEQ), 0)
    query = lax.broadcasted_iota(jnp.int32, (HALF, SEQ), 1)
    allow_a = key <= query
    key_b, query_b = key[:, :HALF], query[:, :HALF]
    allow_b = (key_b <= query_b) & (key_b + HALF < length)
    for h in range(HEADS):
        lo, hi = h * HEAD_DIM, (h + 1) * HEAD_DIM
        q = qkv_t[lo:hi, :]
        k = qkv_t[D + lo : D + hi, :]
        v = qkv_t[2 * D + lo : 2 * D + hi, :]
        s_a = jnp.where(allow_a, tn(k[:, :HALF], q), -1e30)
        s_b = jnp.where(allow_b, tn(k[:, HALF:], q[:, HALF:]), -1e30)
        m_a = jnp.max(s_a, axis=0, keepdims=True)
        m_b = jnp.max(s_b, axis=0, keepdims=True)
        m_1 = jnp.maximum(m_a[:, HALF:], m_b)
        top = jnp.concatenate([m_a[:, :HALF], m_1], axis=1)
        e_a = jnp.exp((s_a - top) * SCORE_SCALE)
        e_b = jnp.exp((s_b - m_1) * SCORE_SCALE)
        t_a = jnp.sum(e_a, axis=0, keepdims=True)
        t_1 = t_a[:, HALF:] + jnp.sum(e_b, axis=0, keepdims=True)
        r_1 = 1.0 / t_1
        r_a = jnp.concatenate([1.0 / t_a[:, :HALF], r_1], axis=1)
        p_a = e_a * r_a
        p_b = e_b * r_1
        prob_a[h] = p_a
        prob_b[h] = p_b
        c_a = nn(v[:, :HALF], p_a.astype(BF))
        c_b = nn(v[:, HALF:], p_b.astype(BF))
        ctx_t[lo:hi, :HALF] = c_a[:, :HALF].astype(BF)
        ctx_t[lo:hi, HALF:] = (c_a[:, HALF:] + c_b).astype(BF)
    copies[2].wait()
    copies[3].wait()
    first = DEPTH_GAIN * x.astype(F32) + tn(ctx_t[...], wout[...])
    u1, i1 = unit_of(first)
    unit1[...] = u1
    inv1[...] = i1
    normed = u1 * g1[...]
    normed_bf = normed.astype(BF)
    normed_t[...] = normed_bf.T
    second = DEPTH_GAIN * normed
    copies[4].wait()
    copies[5].wait()
    copies[6].wait()
    for j in range(FF // D):
        cols = slice(j * D, (j + 1) * D)
        pre = nn(normed_bf, win[:, cols])
        sq = pre * pre
        t = jnp.tanh(pre * (TANH_SCALE + (TANH_SCALE * CUBIC) * sq))
        gate = 0.5 + 0.5 * t
        hid = (pre * gate).astype(BF)
        deriv[:, cols] = gate + pre * (1.0 - t * t) * (
            0.5 * TANH_SCALE + (1.5 * TANH_SCALE * CUBIC) * sq
        )
        hidden_t[cols, :] = hid.T
        second = second + nn(hid, wback[cols, :])
    u2, i2 = unit_of(second)
    unit2[...] = u2
    inv2[...] = i2


def ffn_back(d2, d2_bf, deriv, win, wback, keep=None):
    dn = DEPTH_GAIN * d2
    for j in range(FF // D):
        cols = slice(j * D, (j + 1) * D)
        du = (nt(d2_bf, wback[cols, :]) * deriv[:, cols]).astype(BF)
        if keep is not None:
            keep[:, cols] = du
        dn = dn + nt(du, win[:, cols])
    return dn


def attention_back(d1_bf, wout, qkv_t, prob_a, prob_b, dqkv_t):
    dctx_t = nt(d1_bf, wout[...]).astype(BF).T
    for h in range(HEADS):
        lo, hi = h * HEAD_DIM, (h + 1) * HEAD_DIM
        q = qkv_t[lo:hi, :]
        k = qkv_t[D + lo : D + hi, :]
        v = qkv_t[2 * D + lo : 2 * D + hi, :]
        dc = dctx_t[lo:hi, :]
        p_a, p_b = prob_a[h], prob_b[h]
        dp_a = tn(v[:, :HALF], dc)
        dp_b = tn(v[:, HALF:], dc[:, HALF:])
        w_a = jnp.sum(p_a * dp_a, axis=0, keepdims=True)
        w_1 = w_a[:, HALF:] + jnp.sum(p_b * dp_b, axis=0, keepdims=True)
        w = jnp.concatenate([w_a[:, :HALF], w_1], axis=1)
        ds_a = (p_a * (dp_a - w) * SCORE_SCALE).astype(BF)
        ds_b = (p_b * (dp_b - w_1) * SCORE_SCALE).astype(BF)
        dq = nn(k[:, :HALF], ds_a)
        dqkv_t[lo:hi, :HALF] = dq[:, :HALF].astype(BF)
        dqkv_t[lo:hi, HALF:] = (dq[:, HALF:] + nn(k[:, HALF:], ds_b)).astype(BF)
        dqkv_t[D + lo : D + hi, :HALF] = nt(q, ds_a).astype(BF)
        dqkv_t[D + lo : D + hi, HALF:] = nt(q[:, HALF:], ds_b).astype(BF)
        dqkv_t[2 * D + lo : 2 * D + hi, :HALF] = nt(dc, p_a.astype(BF)).astype(BF)
        dqkv_t[2 * D + lo : 2 * D + hi, HALF:] = nt(dc[:, HALF:], p_b.astype(BF)).astype(BF)


def state_back(d1, dqkv, wqkv):
    return DEPTH_GAIN * d1 + nt(dqkv, wqkv[...])


def thirds(full):
    high = full.astype(BF)
    rest = full - high.astype(F32)
    mid = rest.astype(BF)
    low = (rest - mid.astype(F32)).astype(BF)
    parts = [part.astype(F32) for part in (high, mid, low)]
    return jnp.concatenate(parts + [jnp.zeros((13, D), F32)], axis=0).astype(BF)


def whole_of(msg):
    tail = msg[msg.shape[0] - 16 :, :].astype(F32)
    return tail[0:1, :] + tail[1:2, :] + tail[2:3, :]


def rows_of(msg):
    return msg[: msg.shape[0] - 16, :].astype(F32)


def relax_kernel(
    meta, above, cot, guess, rate,
    qkv_t, prob_a, prob_b, unit1, inv1, unit2, inv2, deriv, wqkv, wout, win, wback, g1, g2,
    relaxed_out, resid_low, resid_high, dqkv_t,
):
    last = meta[1] == 1
    up = jnp.where(last, cot[...].astype(F32), above[...].astype(F32))
    d2 = norm_back(up, unit2[...], inv2[...], g2[...])
    dn = ffn_back(d2, d2.astype(BF), deriv, win, wback)
    d1 = norm_back(dn, unit1[...], inv1[...], g1[...])
    attention_back(d1.astype(BF), wout, qkv_t, prob_a, prob_b, dqkv_t)
    relaxed = state_back(d1, dqkv_t[...].T, wqkv).astype(BF)
    relaxed_out[...] = relaxed
    resid = (relaxed.astype(F32) - guess[...].astype(F32)).astype(BF)
    tail = thirds(rate[...])
    resid_low[:LOW, :] = resid[:LOW, :]
    resid_low[LOW:, :] = tail
    resid_high[:HIGH, :] = resid[LOW:, :]
    resid_high[HIGH:, :] = tail


def compose_low_kernel(meta, relaxed, guess, rate, one, two, out):
    resid = relaxed[:LOW, :].astype(F32) - guess[:LOW, :].astype(F32)
    r1, r2 = whole_of(one), whole_of(two)
    higher = rows_of(one) + r1 * rows_of(two)
    out[:LOW, :] = (resid + rate[...] * higher).astype(BF)
    y = meta[4]
    factor = rate[...] * jnp.where(y < 3, r1, 1.0) * jnp.where(y < 2, r2, 1.0)
    out[LOW:, :] = thirds(factor)


def compose_high_kernel(meta, relaxed, guess, across, out):
    resid = relaxed[LOW:, :].astype(F32) - guess[LOW:, :].astype(F32)
    top = jnp.where(meta[1] == 1, resid, 0.0)
    out[:HIGH, :] = (rows_of(across) + whole_of(across) * top).astype(BF)
    out[HIGH:, :] = across[HIGH:, :]


def mix_kernel(error_bf, wrapped, out):
    out[...] = (error_bf[...].astype(F32) + wrapped[...].astype(F32)).astype(BF)


def finish_kernel(
    meta, error, wrapped, passed, relaxed, guess, rate, swept, adjoint, coarse_err,
    adjoint_v, error_v, sem,
):
    last, own_known, z = meta[1] == 1, (meta[0] + meta[2]) > 0, meta[5]
    far = wrapped[...].astype(F32) + jnp.where(z == 0, 0.0, passed[...].astype(F32))
    reached = jnp.where(own_known, error[...], far)
    guess_f = guess[...].astype(F32)
    resid = relaxed[...].astype(F32) - guess_f
    value = jnp.where(z == 0, rate[...] * reached + resid, reached)
    error_v[...] = value
    first = pltpu.make_async_copy(error_v, coarse_err, sem.at[0])
    first.start()
    coarse = (z == 0) | last
    kept = jnp.where(coarse, guess_f + value, swept[...].astype(F32))
    adjoint_v[...] = kept.astype(BF)
    second = pltpu.make_async_copy(adjoint_v, adjoint, sem.at[1])
    second.start()
    first.wait()
    second.wait()


FLIPS = {"core": 1, "zl": 2, "x0": 4, "x1": 12}


def flip_of(position, order):
    flip = 0
    for bit, name in enumerate(order):
        if position & (8 >> bit):
            flip ^= FLIPS[name]
    return flip


ORDER_BACK = ("core", "x0", "zl", "x1")
ORDER_IN = ("core", "x1", "x0", "zl")
ORDER_QKV = ("core", "zl", "x1", "x0")
WIDE = FF + 128


def place(whole, rows, order, me, keep, send):
    for p in range(16):
        start = pl.multiple_of((me ^ flip_of(p, order)) * rows, rows)
        target = keep if p < 8 else send
        target[p % 8] = whole[pl.ds(start, rows), :]


def chain_kernel(
    meta, shifted_ref, composed, top1, top2, top3, high1, high2, high3,
    above, cot, guess, relaxed, unit2, inv2, g2, hidden_t,
    d2_out, gain2_out, error_out, error_bf, keep, send, whole,
):
    last = meta[1] == 1
    chained = meta[2] == 1
    me = meta[3]
    shifted = shifted_ref[...].astype(F32)
    above_f = above[...].astype(F32)
    top = rows_of(top1) + rows_of(top2) + rows_of(top3)
    low = rows_of(composed) + whole_of(composed) * top
    high = rows_of(high1) + whole_of(high1) * (
        rows_of(high2) + whole_of(high2) * rows_of(high3)
    )
    far = jnp.concatenate([low, high], axis=0)
    near = shifted - above_f
    own = relaxed[...].astype(F32) - guess[...].astype(F32)
    error = jnp.where(last, own, jnp.where(meta[0] == 1, far, near))
    error_out[...] = error
    error_bf[...] = jnp.where(meta[0] == 1, error, 0.0).astype(BF)
    corrected = (above_f + error).astype(BF).astype(F32)
    up = jnp.where(last, cot[...].astype(F32), jnp.where(chained, corrected, shifted))
    u2 = unit2[...]
    d2 = norm_back(up, u2, inv2[...], g2[...])
    gain2_out[...] = jnp.broadcast_to(jnp.sum(up * u2, axis=0, keepdims=True), (8, D))
    d2_out[...] = d2
    d2_bf = d2.astype(BF)
    for j in range(FF // D):
        rows = slice(j * D, (j + 1) * D)
        whole[rows, :] = nn(hidden_t[rows, :], d2_bf).astype(BF)
    place(whole, FF // 16, ORDER_BACK, me, keep, send)


def ffn_kernel(
    meta, d2, deriv, unit1, inv1, win, wback, g1, normed_t, gain2,
    d1_out, keep, send, du, whole,
):
    me = meta[3]
    d2v = d2[...]
    dn = ffn_back(d2v, d2v.astype(BF), deriv, win, wback, du)
    u1 = unit1[...]
    gain1 = jnp.broadcast_to(jnp.sum(dn * u1, axis=0, keepdims=True), (8, D))
    d1_out[...] = norm_back(dn, u1, inv1[...], g1[...])
    for j in range(FF // D):
        cols = slice(j * D, (j + 1) * D)
        whole[:, cols] = nn(normed_t[...], du[:, cols]).astype(BF)
    pair = jnp.concatenate([gain1, gain2[...], jnp.zeros((112, D), F32)], axis=0)
    whole[:, FF:] = pair.T.astype(BF)
    place(whole, D // 16, ORDER_IN, me, keep, send)


def attention_kernel(
    meta, d1, wout, qkv_t, prob_a, prob_b, x_t, ctx_t, dqkv_out, keep, send, dqkv_t, whole,
):
    d1_bf = d1[...].astype(BF)
    attention_back(d1_bf, wout, qkv_t, prob_a, prob_b, dqkv_t)
    whole[:, 3 * D :] = nn(ctx_t[...], d1_bf).astype(BF)
    for j in range(3):
        cols = slice(j * D, (j + 1) * D)
        part = dqkv_t[cols, :].T
        dqkv_out[:, cols] = part
        whole[:, cols] = nn(x_t[...], part).astype(BF)
    place(whole, D // 16, ORDER_QKV, meta[3], keep, send)


def state_kernel(d1, dqkv, wqkv, out):
    out[...] = state_back(d1[...], dqkv[...], wqkv).astype(BF)


HB = pl.BlockSpec(memory_space=pltpu.HBM)
VM = pl.BlockSpec(memory_space=pltpu.VMEM)
SM = pl.BlockSpec(memory_space=pltpu.SMEM)


def call(kernel, outs, scratch, args, flops, name, scalars=1, operands=VM, grant=16, into=None):
    shapes = [jax.ShapeDtypeStruct(s, t) for s, t in outs]
    return pl.pallas_call(
        kernel,
        out_shape=shapes,
        in_specs=[SM] * scalars + [operands] * (len(args) - scalars),
        out_specs=into or [VM] * len(shapes),
        scratch_shapes=[s if not isinstance(s, tuple) else pltpu.VMEM(*s) for s in scratch],
        compiler_params=pltpu.CompilerParams(vmem_limit_bytes=grant * 1024 * 1024),
        cost_estimate=pl.CostEstimate(flops=(LIGHT, STAGE1, BIG)[flops] if flops < 5 else MAIN, bytes_accessed=0, transcendentals=0),
        name=name,
    )(*args)


def by_flip(name, x):
    if name == "core":
        return lax.ppermute(x, "core", [(0, 1), (1, 0)])
    if name == "zl":
        return lax.ppermute(x, "zl", [(0, 1), (1, 0)])
    mask = 1 if name == "x0" else 3
    return lax.ppermute(x, "x", [(i, i ^ mask) for i in range(4)])


def sum_kernel(*refs):
    out = refs[-1]
    size = out.shape[0]
    total = refs[0][size : 2 * size].astype(F32)
    for ref in refs[1:-1]:
        total = total + ref[size : 2 * size].astype(F32)
    out[...] = total.astype(BF)


def passing(parts, cost=0):
    shape = parts[-1].shape
    (out,) = call(
        sum_kernel, [((shape[0] // 2,) + shape[1:], BF)], [], list(parts), cost, "sum", 0
    )
    return out


def total_of(parts):
    total = parts[0][0].astype(F32)
    for part in parts[1:]:
        total = total + part[0].astype(F32)
    return total


def shares_kernel(
    k0, k1, k2, k3, k4, i0, i1, i2, i3, i4, back, inner, gain1, gain2,
    back_v, in_v, sem,
):
    back_v[...] = total_of((k0, k1, k2, k3, k4))
    first = pltpu.make_async_copy(back_v, back, sem.at[0])
    first.start()
    in_v[...] = total_of((i0, i1, i2, i3, i4))
    second = pltpu.make_async_copy(in_v.at[:, :FF], inner, sem.at[1])
    second.start()
    turned = jnp.concatenate([in_v[:, FF:], jnp.zeros((96, 128), F32)], axis=0).T
    gain1[...] = turned[0:1, :32]
    gain2[...] = turned[8:9, :32]
    first.wait()
    second.wait()


def qkv_kernel(k0, k1, k2, k3, k4, out, outer, whole, sem):
    whole[...] = total_of((k0, k1, k2, k3, k4))
    first = pltpu.make_async_copy(whole.at[:, : 3 * D], out, sem.at[0])
    second = pltpu.make_async_copy(whole.at[:, 3 * D :], outer, sem.at[1])
    first.start()
    second.start()
    first.wait()
    second.wait()


def after(x, *done):
    return lax.optimization_barrier((x,) + done)[0]


def at(y, z):
    return FACTOR * y + z


def on_device(
    states, guess, cotangent, lengths, coarse_rate, w_qkv, w_out, w_in, w_back, gain_attn, gain_ffn
):
    x, own_guess = states[0], guess[0]
    y, z = lax.axis_index("ly"), lax.axis_index("lz")
    layer = at(y, z)
    last = layer == 15
    chained = (z == 3) & ~last | (layer == 14)
    meta = jnp.stack(
        [(z == 3).astype(jnp.int32), last.astype(jnp.int32), chained.astype(jnp.int32), lax.axis_index(DP), y, z]
    )
    above = lax.ppermute(own_guess, LAYER, [(i, i - 1) for i in range(1, 16)])

    tok = (SEQ, D)
    (
        qkv_t, prob_a, prob_b, ctx_t, x_t, normed_t, hidden_t, unit1, inv1, unit2, inv2, deriv,
        wqkv, wout, win, wback, gain_one, gain_two,
    ) = call(
        forward_kernel,
        [
            ((3 * D, SEQ), BF), ((HEADS, HALF, SEQ), F32), ((HEADS, HALF, HALF), F32),
            ((D, SEQ), BF), ((D, SEQ), BF), ((D, SEQ), BF), ((FF, SEQ), BF),
            (tok, F32), ((SEQ, 1), F32), (tok, F32), ((SEQ, 1), F32), ((SEQ, FF), F32),
            ((D, 3 * D), BF), ((D, D), BF), ((D, FF), BF), ((FF, D), BF), ((1, D), F32),
            ((1, D), F32),
        ],
        [(tok, BF), pltpu.SemaphoreType.DMA((7,))],
        [lengths] + [pltpu.with_memory_space_constraint(a, pltpu.HBM) for a in (x, w_qkv[0], w_out[0], w_in[0], w_back[0], gain_attn, gain_ffn)],
        9,
        "forward",
        operands=HB,
        grant=GRANT,
    )
    low_msg, high_msg = ((LOW + 16, D), BF), ((HIGH + 16, D), BF)
    relaxed, resid_low, resid_high = call(
        relax_kernel,
        [(tok, BF), low_msg, high_msg],
        [((3 * D, SEQ), BF)],
        [meta, above, cotangent, own_guess, coarse_rate, qkv_t, prob_a, prob_b, unit1, inv1,
         unit2, inv2, deriv, wqkv, wout, win, wback, gain_one, gain_two],
        9,
        "relax",
    )
    from1 = lax.ppermute(resid_low, LAYER, [(12, 8), (8, 4), (15, 11)])
    from2 = lax.ppermute(resid_low, LAYER, [(12, 4), (15, 7)])
    shifted = lax.ppermute(
        relaxed, LAYER, [(at(j, i), at(j, i - 1)) for j in range(4) for i in range(1, 4)]
    )
    across = lax.ppermute(resid_high, LAYER, [(4, 7), (8, 11), (12, 15)])
    from3 = lax.ppermute(resid_low, LAYER, [(15, 3)])
    (low,) = call(
        compose_low_kernel, [low_msg], [],
        [meta, relaxed, own_guess, coarse_rate, from1, from2], 0, "low",
    )
    composed = lax.ppermute(low, LAYER, [(4, 3), (8, 7), (12, 11)])
    (high,) = call(
        compose_high_kernel, [high_msg], [],
        [meta, after(relaxed, low), own_guess, across], 0, "high",
    )
    high1 = lax.ppermute(high, LAYER, [(15, 11), (11, 7), (7, 3)])
    high2 = lax.ppermute(high, LAYER, [(15, 7), (11, 3)])
    high3 = lax.ppermute(high, LAYER, [(15, 3)])
    d2, gain2, error, error_bf, keep_b, send_b = call(
        chain_kernel,
        [(tok, F32), ((8, D), F32), (tok, F32), (tok, BF), ((8, FF // 16, D), BF),
         ((8, FF // 16, D), BF)],
        [((FF, D), BF)],
        [meta, shifted, composed, from1, from2, from3, high1, high2, high3, above, cotangent,
         own_guess, relaxed, unit2, inv2, gain_two, hidden_t],
        9,
        "chain",
    )
    wrapped = lax.ppermute(error_bf, LAYER, [(at(j, 3), at(j, 0)) for j in range(4)])
    b0 = by_flip(ORDER_BACK[0], send_b)
    part_i = (8, D // 16, WIDE)
    d1, keep_i, send_i = call(
        ffn_kernel,
        [(tok, F32), (part_i, BF), (part_i, BF)],
        [((SEQ, FF), BF), ((D, WIDE), BF)],
        [meta, d2, deriv, unit1, inv1, win, wback, gain_one, normed_t, gain2],
        9,
        "ffn",
    )
    i0 = by_flip(ORDER_IN[0], send_i)
    part_q = (8, D // 16, 4 * D)
    dqkv, keep_q, send_q = call(
        attention_kernel,
        [((SEQ, 3 * D), BF), (part_q, BF), (part_q, BF)],
        [((3 * D, SEQ), BF), ((D, 4 * D), BF)],
        [meta, after(d1, b0), wout, qkv_t, prob_a, prob_b, x_t, ctx_t],
        2,
        "attention",
    )
    q0 = by_flip(ORDER_QKV[0], send_q)
    send_i = passing([keep_i, after(i0, dqkv)], 1)
    i1 = by_flip(ORDER_IN[1], send_i)
    (swept,) = call(
        state_kernel, [(tok, BF)], [], [after(d1, send_i), dqkv, wqkv], 1, "state", 0
    )
    send_q = passing([keep_q, after(q0, swept)], 1)
    q1 = by_flip(ORDER_QKV[1], send_q)
    send_b = passing([keep_b, after(b0, send_q)], 1)
    b1 = by_flip(ORDER_BACK[1], send_b)
    send_i = passing([keep_i, i0, after(i1, send_b)])
    i2 = by_flip(ORDER_IN[2], send_i)
    (mixed,) = call(
        mix_kernel, [(tok, BF)], [], [after(error_bf, send_i), wrapped], 0, "mix", 0
    )
    passed = lax.ppermute(
        mixed,
        LAYER,
        [(at(j, 3), at(j, 2)) for j in range(4)] + [(at(j, 0), at(j, 1)) for j in range(4)],
    )
    send_b = passing([keep_b, b0, after(b1, mixed)])
    b2 = by_flip(ORDER_BACK[2], send_b)
    send_q = passing([keep_q, q0, after(q1, send_b)])
    q2 = by_flip(ORDER_QKV[2], send_q)
    send_i = passing([keep_i, i0, i1, after(i2, send_q)])
    i3 = by_flip(ORDER_IN[3], send_i)
    send_b = passing([keep_b, b0, b1, after(b2, send_i)])
    b3 = by_flip(ORDER_BACK[3], send_b)
    send_q = passing([keep_q, q0, q1, after(q2, send_b, passed)])
    q3 = by_flip(ORDER_QKV[3], send_q)
    adjoint, coarse_err = call(
        finish_kernel, [(tok, BF), (tok, F32)],
        [(tok, BF), (tok, F32), pltpu.SemaphoreType.DMA((2,))],
        [meta, error, wrapped, passed, relaxed, own_guess, coarse_rate, after(swept, send_q)],
        0, "finish", into=[HB, HB],
    )
    share_back, share_in, share_one, share_two = call(
        shares_kernel,
        [((FF // 16, D), F32), ((D // 16, FF), F32), ((1, 32), F32), ((1, 32), F32)],
        [((FF // 16, D), F32), ((D // 16, WIDE), F32), pltpu.SemaphoreType.DMA((2,))],
        [keep_b, b0, b1, b2, b3, keep_i, i0, i1, i2, after(i3, adjoint)],
        0, "shares", 0, into=[HB, HB, VM, VM],
    )
    share_q, share_out = call(
        qkv_kernel, [((D // 16, 3 * D), F32), ((D // 16, D), F32)],
        [((D // 16, 4 * D), F32), pltpu.SemaphoreType.DMA((2,))],
        [keep_q, q0, q1, q2, after(q3, share_in)], 0, "qkv", 0, into=[HB, HB],
    )
    return (
        adjoint[None],
        coarse_err[None],
        share_q[None],
        share_out[None],
        share_in[None],
        share_back[None],
        share_one,
        share_two,
    )


def solution(mesh):
    torus = Mesh(mesh.devices.reshape(4, 4, 4, 2, 2), LAYER + DP)
    return jax.shard_map(
        on_device,
        mesh=torus,
        in_specs=(
            P(LAYER, DP, None),
            P(LAYER, DP, None),
            P(DP, None),
            P(DP),
            P(LAYER, None),
            P(LAYER, None, None),
            P(LAYER, None, None),
            P(LAYER, None, None),
            P(LAYER, None, None),
            P(LAYER, None),
            P(LAYER, None),
        ),
        out_specs=(
            P(LAYER, DP, None),
            P(LAYER, DP, None),
            P(LAYER, DP, None),
            P(LAYER, DP, None),
            P(LAYER, DP, None),
            P(LAYER, DP, None),
            P(LAYER, DP),
            P(LAYER, DP),
        ),
        check_vma=False,
    )
```

```python
import functools

import jax
import jax.numpy as jnp
from jax import lax
from jax.experimental import pallas as pl
from jax.experimental.pallas import tpu as pltpu
from jax.sharding import Mesh
from jax.sharding import PartitionSpec as P

D = 512
FF = 2048
HEAD_DIM = 64
HEADS = D // HEAD_DIM
SEQ = 256
HALF = SEQ // 2
FACTOR = 4
LAYER = ("ly", "lz")
DP = ("x", "zl", "core")

EPS = 1e-05
DEPTH_GAIN = 6.73
CUBIC = 0.044715
TANH_SCALE = 0.7978845608028654
SCORE_SCALE = HEAD_DIM ** (-0.5)
LOW = 192
HIGH = SEQ - LOW
GRANT = 16
MAIN = 5_000_000_000
LIGHT = 1_000_000_000
STAGE1 = 2_000_000_000
BIG = 6_000_000_000

BF = jnp.bfloat16
F32 = jnp.float32


def nn(a, b):
    return lax.dot_general(a, b, (((1,), (0,)), ((), ())), preferred_element_type=F32)


def nt(a, b):
    return lax.dot_general(a, b, (((1,), (1,)), ((), ())), preferred_element_type=F32)


def tn(a, b):
    return lax.dot_general(a, b, (((0,), (0,)), ((), ())), preferred_element_type=F32)


def row_mean(a):
    return jnp.sum(a, axis=-1, keepdims=True) * (1.0 / D)


def unit_of(rows):
    center = rows - row_mean(rows)
    inv = lax.rsqrt(row_mean(center * center) + EPS)
    return center * inv, inv


def norm_back(up, unit, inv, gain):
    scaled = up * gain
    return inv * (scaled - row_mean(scaled) - unit * row_mean(scaled * unit))


def forward_kernel(
    lengths, x_hbm, wqkv_hbm, wout_hbm, win_hbm, wback_hbm, g1_hbm, g2_hbm,
    qkv_t, prob_a, prob_b, ctx_t, x_t, normed_t, hidden_t, unit1, inv1, unit2, inv2, deriv,
    wqkv, wout, win, wback, g1, g2, x_ref, sem,
):
    pairs = (
        (x_hbm, x_ref), (wqkv_hbm, wqkv), (wout_hbm, wout), (g1_hbm, g1),
        (win_hbm, win), (wback_hbm, wback), (g2_hbm, g2),
    )
    copies = [pltpu.make_async_copy(a, b, sem.at[n]) for n, (a, b) in enumerate(pairs)]
    for copy in copies:
        copy.start()
    length = lengths[0]
    copies[0].wait()
    x = x_ref[...]
    x_t[...] = x.T
    copies[1].wait()
    for j in range(3):
        part = nn(x, wqkv[:, j * D : (j + 1) * D]).astype(BF)
        qkv_t[j * D : (j + 1) * D, :] = part.T
    key = lax.broadcasted_iota(jnp.int32, (HALF, SEQ), 0)
    query = lax.broadcasted_iota(jnp.int32, (HALF, SEQ), 1)
    allow_a = key <= query
    key_b, query_b = key[:, :HALF], query[:, :HALF]
    allow_b = (key_b <= query_b) & (key_b + HALF < length)
    for h in range(HEADS):
        lo, hi = h * HEAD_DIM, (h + 1) * HEAD_DIM
        q = qkv_t[lo:hi, :]
        k = qkv_t[D + lo : D + hi, :]
        v = qkv_t[2 * D + lo : 2 * D + hi, :]
        s_a = jnp.where(allow_a, tn(k[:, :HALF], q), -1e30)
        s_b = jnp.where(allow_b, tn(k[:, HALF:], q[:, HALF:]), -1e30)
        m_a = jnp.max(s_a, axis=0, keepdims=True)
        m_b = jnp.max(s_b, axis=0, keepdims=True)
        m_1 = jnp.maximum(m_a[:, HALF:], m_b)
        top = jnp.concatenate([m_a[:, :HALF], m_1], axis=1)
        e_a = jnp.exp((s_a - top) * SCORE_SCALE)
        e_b = jnp.exp((s_b - m_1) * SCORE_SCALE)
        t_a = jnp.sum(e_a, axis=0, keepdims=True)
        t_1 = t_a[:, HALF:] + jnp.sum(e_b, axis=0, keepdims=True)
        r_1 = 1.0 / t_1
        r_a = jnp.concatenate([1.0 / t_a[:, :HALF], r_1], axis=1)
        p_a = e_a * r_a
        p_b = e_b * r_1
        prob_a[h] = p_a
        prob_b[h] = p_b
        c_a = nn(v[:, :HALF], p_a.astype(BF))
        c_b = nn(v[:, HALF:], p_b.astype(BF))
        ctx_t[lo:hi, :HALF] = c_a[:, :HALF].astype(BF)
        ctx_t[lo:hi, HALF:] = (c_a[:, HALF:] + c_b).astype(BF)
    copies[2].wait()
    copies[3].wait()
    first = DEPTH_GAIN * x.astype(F32) + tn(ctx_t[...], wout[...])
    u1, i1 = unit_of(first)
    unit1[...] = u1
    inv1[...] = i1
    normed = u1 * g1[...]
    normed_bf = normed.astype(BF)
    normed_t[...] = normed_bf.T
    second = DEPTH_GAIN * normed
    copies[4].wait()
    copies[5].wait()
    copies[6].wait()
    for j in range(FF // D):
        cols = slice(j * D, (j + 1) * D)
        pre = nn(normed_bf, win[:, cols])
        sq = pre * pre
        t = jnp.tanh(pre * (TANH_SCALE + (TANH_SCALE * CUBIC) * sq))
        gate = 0.5 + 0.5 * t
        hid = (pre * gate).astype(BF)
        deriv[:, cols] = gate + pre * (1.0 - t * t) * (
            0.5 * TANH_SCALE + (1.5 * TANH_SCALE * CUBIC) * sq
        )
        hidden_t[cols, :] = hid.T
        second = second + nn(hid, wback[cols, :])
    u2, i2 = unit_of(second)
    unit2[...] = u2
    inv2[...] = i2


def ffn_back(d2, d2_bf, deriv, win, wback, keep=None):
    dn = DEPTH_GAIN * d2
    for j in range(FF // D):
        cols = slice(j * D, (j + 1) * D)
        du = (nt(d2_bf, wback[cols, :]) * deriv[:, cols]).astype(BF)
        if keep is not None:
            keep[:, cols] = du
        dn = dn + nt(du, win[:, cols])
    return dn


def attention_back(d1_bf, wout, qkv_t, prob_a, prob_b, dqkv_t):
    dctx_t = nt(d1_bf, wout[...]).astype(BF).T
    for h in range(HEADS):
        lo, hi = h * HEAD_DIM, (h + 1) * HEAD_DIM
        q = qkv_t[lo:hi, :]
        k = qkv_t[D + lo : D + hi, :]
        v = qkv_t[2 * D + lo : 2 * D + hi, :]
        dc = dctx_t[lo:hi, :]
        p_a, p_b = prob_a[h], prob_b[h]
        dp_a = tn(v[:, :HALF], dc)
        dp_b = tn(v[:, HALF:], dc[:, HALF:])
        w_a = jnp.sum(p_a * dp_a, axis=0, keepdims=True)
        w_1 = w_a[:, HALF:] + jnp.sum(p_b * dp_b, axis=0, keepdims=True)
        w = jnp.concatenate([w_a[:, :HALF], w_1], axis=1)
        ds_a = (p_a * (dp_a - w) * SCORE_SCALE).astype(BF)
        ds_b = (p_b * (dp_b - w_1) * SCORE_SCALE).astype(BF)
        dq = nn(k[:, :HALF], ds_a)
        dqkv_t[lo:hi, :HALF] = dq[:, :HALF].astype(BF)
        dqkv_t[lo:hi, HALF:] = (dq[:, HALF:] + nn(k[:, HALF:], ds_b)).astype(BF)
        dqkv_t[D + lo : D + hi, :HALF] = nt(q, ds_a).astype(BF)
        dqkv_t[D + lo : D + hi, HALF:] = nt(q[:, HALF:], ds_b).astype(BF)
        dqkv_t[2 * D + lo : 2 * D + hi, :HALF] = nt(dc, p_a.astype(BF)).astype(BF)
        dqkv_t[2 * D + lo : 2 * D + hi, HALF:] = nt(dc[:, HALF:], p_b.astype(BF)).astype(BF)


def state_back(d1, dqkv, wqkv):
    return DEPTH_GAIN * d1 + nt(dqkv, wqkv[...])


def thirds(full):
    high = full.astype(BF)
    rest = full - high.astype(F32)
    mid = rest.astype(BF)
    low = (rest - mid.astype(F32)).astype(BF)
    parts = [part.astype(F32) for part in (high, mid, low)]
    return jnp.concatenate(parts + [jnp.zeros((13, D), F32)], axis=0).astype(BF)


def whole_of(msg):
    tail = msg[msg.shape[0] - 16 :, :].astype(F32)
    return tail[0:1, :] + tail[1:2, :] + tail[2:3, :]


def rows_of(msg):
    return msg[: msg.shape[0] - 16, :].astype(F32)


def relax_kernel(
    meta, above, cot, guess, rate,
    qkv_t, prob_a, prob_b, unit1, inv1, unit2, inv2, deriv, wqkv, wout, win, wback, g1, g2,
    relaxed_out, resid_low, resid_high, dqkv_t,
):
    last = meta[1] == 1
    up = jnp.where(last, cot[...].astype(F32), above[...].astype(F32))
    d2 = norm_back(up, unit2[...], inv2[...], g2[...])
    dn = ffn_back(d2, d2.astype(BF), deriv, win, wback)
    d1 = norm_back(dn, unit1[...], inv1[...], g1[...])
    attention_back(d1.astype(BF), wout, qkv_t, prob_a, prob_b, dqkv_t)
    relaxed = state_back(d1, dqkv_t[...].T, wqkv).astype(BF)
    relaxed_out[...] = relaxed
    resid = (relaxed.astype(F32) - guess[...].astype(F32)).astype(BF)
    tail = thirds(rate[...])
    resid_low[:LOW, :] = resid[:LOW, :]
    resid_low[LOW:, :] = tail
    resid_high[:HIGH, :] = resid[LOW:, :]
    resid_high[HIGH:, :] = tail


def compose_low_kernel(meta, relaxed, guess, rate, one, two, out):
    resid = relaxed[:LOW, :].astype(F32) - guess[:LOW, :].astype(F32)
    r1, r2 = whole_of(one), whole_of(two)
    higher = rows_of(one) + r1 * rows_of(two)
    out[:LOW, :] = (resid + rate[...] * higher).astype(BF)
    y = meta[4]
    factor = rate[...] * jnp.where(y < 3, r1, 1.0) * jnp.where(y < 2, r2, 1.0)
    out[LOW:, :] = thirds(factor)


def compose_high_kernel(meta, relaxed, guess, across, out):
    resid = relaxed[LOW:, :].astype(F32) - guess[LOW:, :].astype(F32)
    top = jnp.where(meta[1] == 1, resid, 0.0)
    out[:HIGH, :] = (rows_of(across) + whole_of(across) * top).astype(BF)
    out[HIGH:, :] = across[HIGH:, :]


def mix_kernel(error_bf, wrapped, out):
    out[...] = (error_bf[...].astype(F32) + wrapped[...].astype(F32)).astype(BF)


def finish_kernel(
    meta, error, wrapped, passed, relaxed, guess, rate, swept, adjoint, coarse_err,
    adjoint_v, error_v, sem,
):
    last, own_known, z = meta[1] == 1, (meta[0] + meta[2]) > 0, meta[5]
    far = wrapped[...].astype(F32) + jnp.where(z == 0, 0.0, passed[...].astype(F32))
    reached = jnp.where(own_known, error[...], far)
    guess_f = guess[...].astype(F32)
    resid = relaxed[...].astype(F32) - guess_f
    value = jnp.where(z == 0, rate[...] * reached + resid, reached)
    error_v[...] = value
    first = pltpu.make_async_copy(error_v, coarse_err, sem.at[0])
    first.start()
    coarse = (z == 0) | last
    kept = jnp.where(coarse, guess_f + value, swept[...].astype(F32))
    adjoint_v[...] = kept.astype(BF)
    second = pltpu.make_async_copy(adjoint_v, adjoint, sem.at[1])
    second.start()
    first.wait()
    second.wait()


FLIPS = {"core": 1, "zl": 2, "x0": 4, "x1": 12}


def flip_of(position, order):
    flip = 0
    for bit, name in enumerate(order):
        if position & (8 >> bit):
            flip ^= FLIPS[name]
    return flip


ORDER_BACK = ("core", "x0", "zl", "x1")
ORDER_IN = ("core", "x1", "x0", "zl")
ORDER_QKV = ("core", "zl", "x1", "x0")
WIDE = FF + 128


def place(whole, rows, order, me, keep, send):
    for p in range(16):
        start = pl.multiple_of((me ^ flip_of(p, order)) * rows, rows)
        target = keep if p < 8 else send
        target[p % 8] = whole[pl.ds(start, rows), :]


def chain_kernel(
    meta, shifted_ref, composed, top1, top2, top3, high1, high2, high3,
    above, cot, guess, relaxed, unit2, inv2, g2, hidden_t,
    d2_out, gain2_out, error_out, error_bf, keep, send, whole,
):
    last = meta[1] == 1
    chained = meta[2] == 1
    me = meta[3]
    shifted = shifted_ref[...].astype(F32)
    above_f = above[...].astype(F32)
    top = rows_of(top1) + rows_of(top2) + rows_of(top3)
    low = rows_of(composed) + whole_of(composed) * top
    high = rows_of(high1) + whole_of(high1) * (
        rows_of(high2) + whole_of(high2) * rows_of(high3)
    )
    far = jnp.concatenate([low, high], axis=0)
    near = shifted - above_f
    own = relaxed[...].astype(F32) - guess[...].astype(F32)
    error = jnp.where(last, own, jnp.where(meta[0] == 1, far, near))
    error_out[...] = error
    error_bf[...] = jnp.where(meta[0] == 1, error, 0.0).astype(BF)
    corrected = (above_f + error).astype(BF).astype(F32)
    up = jnp.where(last, cot[...].astype(F32), jnp.where(chained, corrected, shifted))
    u2 = unit2[...]
    d2 = norm_back(up, u2, inv2[...], g2[...])
    gain2_out[...] = jnp.broadcast_to(jnp.sum(up * u2, axis=0, keepdims=True), (8, D))
    d2_out[...] = d2
    d2_bf = d2.astype(BF)
    for j in range(FF // D):
        rows = slice(j * D, (j + 1) * D)
        whole[rows, :] = nn(hidden_t[rows, :], d2_bf).astype(BF)
    place(whole, FF // 16, ORDER_BACK, me, keep, send)


def ffn_kernel(
    meta, d2, deriv, unit1, inv1, win, wback, g1, normed_t, gain2,
    d1_out, keep, send, du, whole,
):
    me = meta[3]
    d2v = d2[...]
    dn = ffn_back(d2v, d2v.astype(BF), deriv, win, wback, du)
    u1 = unit1[...]
    gain1 = jnp.broadcast_to(jnp.sum(dn * u1, axis=0, keepdims=True), (8, D))
    d1_out[...] = norm_back(dn, u1, inv1[...], g1[...])
    for j in range(FF // D):
        cols = slice(j * D, (j + 1) * D)
        whole[:, cols] = nn(normed_t[...], du[:, cols]).astype(BF)
    pair = jnp.concatenate([gain1, gain2[...], jnp.zeros((112, D), F32)], axis=0)
    whole[:, FF:] = pair.T.astype(BF)
    place(whole, D // 16, ORDER_IN, me, keep, send)


def attention_kernel(
    meta, d1, wout, qkv_t, prob_a, prob_b, x_t, ctx_t, dqkv_out, keep, send, dqkv_t, whole,
):
    d1_bf = d1[...].astype(BF)
    attention_back(d1_bf, wout, qkv_t, prob_a, prob_b, dqkv_t)
    whole[:, 3 * D :] = nn(ctx_t[...], d1_bf).astype(BF)
    for j in range(3):
        cols = slice(j * D, (j + 1) * D)
        part = dqkv_t[cols, :].T
        dqkv_out[:, cols] = part
        whole[:, cols] = nn(x_t[...], part).astype(BF)
    place(whole, D // 16, ORDER_QKV, meta[3], keep, send)


def state_kernel(d1, dqkv, wqkv, out):
    out[...] = state_back(d1[...], dqkv[...], wqkv).astype(BF)


HB = pl.BlockSpec(memory_space=pltpu.HBM)
VM = pl.BlockSpec(memory_space=pltpu.VMEM)
SM = pl.BlockSpec(memory_space=pltpu.SMEM)


def call(kernel, outs, scratch, args, flops, name, scalars=1, operands=VM, grant=16, into=None):
    shapes = [jax.ShapeDtypeStruct(s, t) for s, t in outs]
    return pl.pallas_call(
        kernel,
        out_shape=shapes,
        in_specs=[SM] * scalars + [operands] * (len(args) - scalars),
        out_specs=into or [VM] * len(shapes),
        scratch_shapes=[s if not isinstance(s, tuple) else pltpu.VMEM(*s) for s in scratch],
        compiler_params=pltpu.CompilerParams(vmem_limit_bytes=grant * 1024 * 1024),
        cost_estimate=pl.CostEstimate(flops=(LIGHT, STAGE1, BIG)[flops] if flops < 5 else MAIN, bytes_accessed=0, transcendentals=0),
        name=name,
    )(*args)


def by_flip(name, x):
    if name == "core":
        return lax.ppermute(x, "core", [(0, 1), (1, 0)])
    if name == "zl":
        return lax.ppermute(x, "zl", [(0, 1), (1, 0)])
    mask = 1 if name == "x0" else 3
    return lax.ppermute(x, "x", [(i, i ^ mask) for i in range(4)])


def sum_kernel(*refs):
    out = refs[-1]
    size = out.shape[0]
    total = refs[0][size : 2 * size].astype(F32)
    for ref in refs[1:-1]:
        total = total + ref[size : 2 * size].astype(F32)
    out[...] = total.astype(BF)


def passing(parts, cost=0):
    shape = parts[-1].shape
    (out,) = call(
        sum_kernel, [((shape[0] // 2,) + shape[1:], BF)], [], list(parts), cost, "sum", 0
    )
    return out


def total_of(parts):
    total = parts[0][0].astype(F32)
    for part in parts[1:]:
        total = total + part[0].astype(F32)
    return total


def shares_kernel(
    k0, k1, k2, k3, k4, i0, i1, i2, i3, i4, back, inner, gain1, gain2,
    back_v, in_v, sem,
):
    back_v[...] = total_of((k0, k1, k2, k3, k4))
    first = pltpu.make_async_copy(back_v, back, sem.at[0])
    first.start()
    in_v[...] = total_of((i0, i1, i2, i3, i4))
    second = pltpu.make_async_copy(in_v.at[:, :FF], inner, sem.at[1])
    second.start()
    turned = jnp.concatenate([in_v[:, FF:], jnp.zeros((96, 128), F32)], axis=0).T
    gain1[...] = turned[0:1, :32]
    gain2[...] = turned[8:9, :32]
    first.wait()
    second.wait()


def qkv_kernel(k0, k1, k2, k3, k4, out, outer, whole, sem):
    whole[...] = total_of((k0, k1, k2, k3, k4))
    first = pltpu.make_async_copy(whole.at[:, : 3 * D], out, sem.at[0])
    second = pltpu.make_async_copy(whole.at[:, 3 * D :], outer, sem.at[1])
    first.start()
    second.start()
    first.wait()
    second.wait()


def after(x, *done):
    return lax.optimization_barrier((x,) + done)[0]


def at(y, z):
    return FACTOR * y + z


def on_device(
    states, guess, cotangent, lengths, coarse_rate, w_qkv, w_out, w_in, w_back, gain_attn, gain_ffn
):
    x, own_guess = states[0], guess[0]
    y, z = lax.axis_index("ly"), lax.axis_index("lz")
    layer = at(y, z)
    last = layer == 15
    chained = (z == 3) & ~last | (layer == 14)
    meta = jnp.stack(
        [(z == 3).astype(jnp.int32), last.astype(jnp.int32), chained.astype(jnp.int32), lax.axis_index(DP), y, z]
    )
    above = lax.ppermute(own_guess, LAYER, [(i, i - 1) for i in range(1, 16)])

    tok = (SEQ, D)
    (
        qkv_t, prob_a, prob_b, ctx_t, x_t, normed_t, hidden_t, unit1, inv1, unit2, inv2, deriv,
        wqkv, wout, win, wback, gain_one, gain_two,
    ) = call(
        forward_kernel,
        [
            ((3 * D, SEQ), BF), ((HEADS, HALF, SEQ), F32), ((HEADS, HALF, HALF), F32),
            ((D, SEQ), BF), ((D, SEQ), BF), ((D, SEQ), BF), ((FF, SEQ), BF),
            (tok, F32), ((SEQ, 1), F32), (tok, F32), ((SEQ, 1), F32), ((SEQ, FF), F32),
            ((D, 3 * D), BF), ((D, D), BF), ((D, FF), BF), ((FF, D), BF), ((1, D), F32),
            ((1, D), F32),
        ],
        [(tok, BF), pltpu.SemaphoreType.DMA((7,))],
        [lengths] + [pltpu.with_memory_space_constraint(a, pltpu.HBM) for a in (x, w_qkv[0], w_out[0], w_in[0], w_back[0], gain_attn, gain_ffn)],
        9,
        "forward",
        operands=HB,
        grant=GRANT,
    )
    low_msg, high_msg = ((LOW + 16, D), BF), ((HIGH + 16, D), BF)
    relaxed, resid_low, resid_high = call(
        relax_kernel,
        [(tok, BF), low_msg, high_msg],
        [((3 * D, SEQ), BF)],
        [meta, above, cotangent, own_guess, coarse_rate, qkv_t, prob_a, prob_b, unit1, inv1,
         unit2, inv2, deriv, wqkv, wout, win, wback, gain_one, gain_two],
        9,
        "relax",
    )
    from1 = lax.ppermute(resid_low, LAYER, [(12, 8), (8, 4), (15, 11)])
    from2 = lax.ppermute(resid_low, LAYER, [(12, 4), (15, 7)])
    shifted = lax.ppermute(
        relaxed, LAYER, [(at(j, i), at(j, i - 1)) for j in range(4) for i in range(1, 4)]
    )
    across = lax.ppermute(resid_high, LAYER, [(4, 7), (8, 11), (12, 15)])
    from3 = lax.ppermute(resid_low, LAYER, [(15, 3)])
    (low,) = call(
        compose_low_kernel, [low_msg], [],
        [meta, relaxed, own_guess, coarse_rate, from1, from2], 0, "low",
    )
    composed = lax.ppermute(low, LAYER, [(4, 3), (8, 7), (12, 11)])
    (high,) = call(
        compose_high_kernel, [high_msg], [],
        [meta, after(relaxed, low), own_guess, across], 0, "high",
    )
    high1 = lax.ppermute(high, LAYER, [(15, 11), (11, 7), (7, 3)])
    high2 = lax.ppermute(high, LAYER, [(15, 7), (11, 3)])
    high3 = lax.ppermute(high, LAYER, [(15, 3)])
    d2, gain2, error, error_bf, keep_b, send_b = call(
        chain_kernel,
        [(tok, F32), ((8, D), F32), (tok, F32), (tok, BF), ((8, FF // 16, D), BF),
         ((8, FF // 16, D), BF)],
        [((FF, D), BF)],
        [meta, shifted, composed, from1, from2, from3, high1, high2, high3, above, cotangent,
         own_guess, relaxed, unit2, inv2, gain_two, hidden_t],
        9,
        "chain",
    )
    wrapped = lax.ppermute(error_bf, LAYER, [(at(j, 3), at(j, 0)) for j in range(4)])
    b0 = by_flip(ORDER_BACK[0], send_b)
    part_i = (8, D // 16, WIDE)
    d1, keep_i, send_i = call(
        ffn_kernel,
        [(tok, F32), (part_i, BF), (part_i, BF)],
        [((SEQ, FF), BF), ((D, WIDE), BF)],
        [meta, d2, deriv, unit1, inv1, win, wback, gain_one, normed_t, gain2],
        9,
        "ffn",
    )
    i0 = by_flip(ORDER_IN[0], send_i)
    part_q = (8, D // 16, 4 * D)
    dqkv, keep_q, send_q = call(
        attention_kernel,
        [((SEQ, 3 * D), BF), (part_q, BF), (part_q, BF)],
        [((3 * D, SEQ), BF), ((D, 4 * D), BF)],
        [meta, after(d1, b0), wout, qkv_t, prob_a, prob_b, x_t, ctx_t],
        2,
        "attention",
    )
    q0 = by_flip(ORDER_QKV[0], send_q)
    send_i = passing([keep_i, after(i0, dqkv)])
    i1 = by_flip(ORDER_IN[1], send_i)
    (swept,) = call(
        state_kernel, [(tok, BF)], [], [after(d1, send_i), dqkv, wqkv], 0, "state", 0
    )
    send_q = passing([keep_q, after(q0, swept)])
    q1 = by_flip(ORDER_QKV[1], send_q)
    send_b = passing([keep_b, after(b0, send_q)])
    b1 = by_flip(ORDER_BACK[1], send_b)
    (mixed,) = call(
        mix_kernel, [(tok, BF)], [], [after(error_bf, send_b), wrapped], 1, "mix", 0
    )
    passed = lax.ppermute(
        mixed,
        LAYER,
        [(at(j, 3), at(j, 2)) for j in range(4)] + [(at(j, 0), at(j, 1)) for j in range(4)],
    )
    send_i = passing([keep_i, i0, after(i1, mixed)])
    i2 = by_flip(ORDER_IN[2], send_i)
    send_b = passing([keep_b, b0, after(b1, send_i)])
    b2 = by_flip(ORDER_BACK[2], send_b)
    send_q = passing([keep_q, q0, after(q1, send_b, passed)])
    q2 = by_flip(ORDER_QKV[2], send_q)
    send_i = passing([keep_i, i0, i1, after(i2, send_q)])
    i3 = by_flip(ORDER_IN[3], send_i)
    send_b = passing([keep_b, b0, b1, after(b2, send_i)])
    b3 = by_flip(ORDER_BACK[3], send_b)
    send_q = passing([keep_q, q0, q1, after(q2, send_b)])
    q3 = by_flip(ORDER_QKV[3], send_q)
    adjoint, coarse_err = call(
        finish_kernel, [(tok, BF), (tok, F32)],
        [(tok, BF), (tok, F32), pltpu.SemaphoreType.DMA((2,))],
        [meta, error, wrapped, passed, relaxed, own_guess, coarse_rate, after(swept, send_q)],
        0, "finish", into=[HB, HB],
    )
    share_back, share_in, share_one, share_two = call(
        shares_kernel,
        [((FF // 16, D), F32), ((D // 16, FF), F32), ((1, 32), F32), ((1, 32), F32)],
        [((FF // 16, D), F32), ((D // 16, WIDE), F32), pltpu.SemaphoreType.DMA((2,))],
        [keep_b, b0, b1, b2, b3, keep_i, i0, i1, i2, after(i3, adjoint)],
        0, "shares", 0, into=[HB, HB, VM, VM],
    )
    share_q, share_out = call(
        qkv_kernel, [((D // 16, 3 * D), F32), ((D // 16, D), F32)],
        [((D // 16, 4 * D), F32), pltpu.SemaphoreType.DMA((2,))],
        [keep_q, q0, q1, q2, after(q3, share_in)], 0, "qkv", 0, into=[HB, HB],
    )
    return (
        adjoint[None],
        coarse_err[None],
        share_q[None],
        share_out[None],
        share_in[None],
        share_back[None],
        share_one,
        share_two,
    )


def solution(mesh):
    torus = Mesh(mesh.devices.reshape(4, 4, 4, 2, 2), LAYER + DP)
    return jax.shard_map(
        on_device,
        mesh=torus,
        in_specs=(
            P(LAYER, DP, None),
            P(LAYER, DP, None),
            P(DP, None),
            P(DP),
            P(LAYER, None),
            P(LAYER, None, None),
            P(LAYER, None, None),
            P(LAYER, None, None),
            P(LAYER, None, None),
            P(LAYER, None),
            P(LAYER, None),
        ),
        out_specs=(
            P(LAYER, DP, None),
            P(LAYER, DP, None),
            P(LAYER, DP, None),
            P(LAYER, DP, None),
            P(LAYER, DP, None),
            P(LAYER, DP, None),
            P(LAYER, DP),
            P(LAYER, DP),
        ),
        check_vma=False,
    )
```

```python
import functools

import jax
import jax.numpy as jnp
from jax import lax
from jax.experimental import pallas as pl
from jax.experimental.pallas import tpu as pltpu
from jax.sharding import Mesh
from jax.sharding import PartitionSpec as P

D = 512
FF = 2048
HEAD_DIM = 64
HEADS = D // HEAD_DIM
SEQ = 256
HALF = SEQ // 2
FACTOR = 4
LAYER = ("ly", "lz")
DP = ("x", "zl", "core")

EPS = 1e-05
DEPTH_GAIN = 6.73
CUBIC = 0.044715
TANH_SCALE = 0.7978845608028654
SCORE_SCALE = HEAD_DIM ** (-0.5)
LOW = 192
HIGH = SEQ - LOW
GRANT = 16
MAIN = 5_000_000_000
LIGHT = 1_000_000_000
STAGE1 = 2_000_000_000
BIG = 6_000_000_000

BF = jnp.bfloat16
F32 = jnp.float32


def nn(a, b):
    return lax.dot_general(a, b, (((1,), (0,)), ((), ())), preferred_element_type=F32)


def nt(a, b):
    return lax.dot_general(a, b, (((1,), (1,)), ((), ())), preferred_element_type=F32)


def tn(a, b):
    return lax.dot_general(a, b, (((0,), (0,)), ((), ())), preferred_element_type=F32)


def row_mean(a):
    return jnp.sum(a, axis=-1, keepdims=True) * (1.0 / D)


def unit_of(rows):
    center = rows - row_mean(rows)
    inv = lax.rsqrt(row_mean(center * center) + EPS)
    return center * inv, inv


def norm_back(up, unit, inv, gain):
    scaled = up * gain
    return inv * (scaled - row_mean(scaled) - unit * row_mean(scaled * unit))


def forward_kernel(
    lengths, x_hbm, wqkv_hbm, wout_hbm, win_hbm, wback_hbm, g1_hbm, g2_hbm,
    qkv_t, prob_a, prob_b, ctx_t, x_t, normed_t, hidden_t, unit1, inv1, unit2, inv2, deriv,
    wqkv, wout, win, wback, g1, g2, x_ref, sem,
):
    pairs = (
        (x_hbm, x_ref), (wqkv_hbm, wqkv), (wout_hbm, wout), (g1_hbm, g1),
        (win_hbm, win), (wback_hbm, wback), (g2_hbm, g2),
    )
    copies = [pltpu.make_async_copy(a, b, sem.at[n]) for n, (a, b) in enumerate(pairs)]
    for copy in copies:
        copy.start()
    length = lengths[0]
    copies[0].wait()
    x = x_ref[...]
    x_t[...] = x.T
    copies[1].wait()
    for j in range(3):
        part = nn(x, wqkv[:, j * D : (j + 1) * D]).astype(BF)
        qkv_t[j * D : (j + 1) * D, :] = part.T
    key = lax.broadcasted_iota(jnp.int32, (HALF, SEQ), 0)
    query = lax.broadcasted_iota(jnp.int32, (HALF, SEQ), 1)
    allow_a = key <= query
    key_b, query_b = key[:, :HALF], query[:, :HALF]
    allow_b = (key_b <= query_b) & (key_b + HALF < length)
    for h in range(HEADS):
        lo, hi = h * HEAD_DIM, (h + 1) * HEAD_DIM
        q = qkv_t[lo:hi, :]
        k = qkv_t[D + lo : D + hi, :]
        v = qkv_t[2 * D + lo : 2 * D + hi, :]
        s_a = jnp.where(allow_a, tn(k[:, :HALF], q), -1e30)
        s_b = jnp.where(allow_b, tn(k[:, HALF:], q[:, HALF:]), -1e30)
        m_a = jnp.max(s_a, axis=0, keepdims=True)
        m_b = jnp.max(s_b, axis=0, keepdims=True)
        m_1 = jnp.maximum(m_a[:, HALF:], m_b)
        top = jnp.concatenate([m_a[:, :HALF], m_1], axis=1)
        e_a = jnp.exp((s_a - top) * SCORE_SCALE)
        e_b = jnp.exp((s_b - m_1) * SCORE_SCALE)
        t_a = jnp.sum(e_a, axis=0, keepdims=True)
        t_1 = t_a[:, HALF:] + jnp.sum(e_b, axis=0, keepdims=True)
        r_1 = 1.0 / t_1
        r_a = jnp.concatenate([1.0 / t_a[:, :HALF], r_1], axis=1)
        p_a = e_a * r_a
        p_b = e_b * r_1
        prob_a[h] = p_a
        prob_b[h] = p_b
        c_a = nn(v[:, :HALF], p_a.astype(BF))
        c_b = nn(v[:, HALF:], p_b.astype(BF))
        ctx_t[lo:hi, :HALF] = c_a[:, :HALF].astype(BF)
        ctx_t[lo:hi, HALF:] = (c_a[:, HALF:] + c_b).astype(BF)
    copies[2].wait()
    copies[3].wait()
    first = DEPTH_GAIN * x.astype(F32) + tn(ctx_t[...], wout[...])
    u1, i1 = unit_of(first)
    unit1[...] = u1
    inv1[...] = i1
    normed = u1 * g1[...]
    normed_bf = normed.astype(BF)
    normed_t[...] = normed_bf.T
    second = DEPTH_GAIN * normed
    copies[4].wait()
    copies[5].wait()
    copies[6].wait()
    for j in range(FF // D):
        cols = slice(j * D, (j + 1) * D)
        pre = nn(normed_bf, win[:, cols])
        sq = pre * pre
        t = jnp.tanh(pre * (TANH_SCALE + (TANH_SCALE * CUBIC) * sq))
        gate = 0.5 + 0.5 * t
        hid = (pre * gate).astype(BF)
        deriv[:, cols] = gate + pre * (1.0 - t * t) * (
            0.5 * TANH_SCALE + (1.5 * TANH_SCALE * CUBIC) * sq
        )
        hidden_t[cols, :] = hid.T
        second = second + nn(hid, wback[cols, :])
    u2, i2 = unit_of(second)
    unit2[...] = u2
    inv2[...] = i2


def ffn_back(d2, d2_bf, deriv, win, wback, keep=None):
    dn = DEPTH_GAIN * d2
    for j in range(FF // D):
        cols = slice(j * D, (j + 1) * D)
        du = (nt(d2_bf, wback[cols, :]) * deriv[:, cols]).astype(BF)
        if keep is not None:
            keep[:, cols] = du
        dn = dn + nt(du, win[:, cols])
    return dn


def attention_back(d1_bf, wout, qkv_t, prob_a, prob_b, dqkv_t):
    dctx_t = nt(d1_bf, wout[...]).astype(BF).T
    for h in range(HEADS):
        lo, hi = h * HEAD_DIM, (h + 1) * HEAD_DIM
        q = qkv_t[lo:hi, :]
        k = qkv_t[D + lo : D + hi, :]
        v = qkv_t[2 * D + lo : 2 * D + hi, :]
        dc = dctx_t[lo:hi, :]
        p_a, p_b = prob_a[h], prob_b[h]
        dp_a = tn(v[:, :HALF], dc)
        dp_b = tn(v[:, HALF:], dc[:, HALF:])
        w_a = jnp.sum(p_a * dp_a, axis=0, keepdims=True)
        w_1 = w_a[:, HALF:] + jnp.sum(p_b * dp_b, axis=0, keepdims=True)
        w = jnp.concatenate([w_a[:, :HALF], w_1], axis=1)
        ds_a = (p_a * (dp_a - w) * SCORE_SCALE).astype(BF)
        ds_b = (p_b * (dp_b - w_1) * SCORE_SCALE).astype(BF)
        dq = nn(k[:, :HALF], ds_a)
        dqkv_t[lo:hi, :HALF] = dq[:, :HALF].astype(BF)
        dqkv_t[lo:hi, HALF:] = (dq[:, HALF:] + nn(k[:, HALF:], ds_b)).astype(BF)
        dqkv_t[D + lo : D + hi, :HALF] = nt(q, ds_a).astype(BF)
        dqkv_t[D + lo : D + hi, HALF:] = nt(q[:, HALF:], ds_b).astype(BF)
        dqkv_t[2 * D + lo : 2 * D + hi, :HALF] = nt(dc, p_a.astype(BF)).astype(BF)
        dqkv_t[2 * D + lo : 2 * D + hi, HALF:] = nt(dc[:, HALF:], p_b.astype(BF)).astype(BF)


def state_back(d1, dqkv, wqkv):
    return DEPTH_GAIN * d1 + nt(dqkv, wqkv[...])


def thirds(full):
    high = full.astype(BF)
    rest = full - high.astype(F32)
    mid = rest.astype(BF)
    low = (rest - mid.astype(F32)).astype(BF)
    parts = [part.astype(F32) for part in (high, mid, low)]
    return jnp.concatenate(parts + [jnp.zeros((13, D), F32)], axis=0).astype(BF)


def whole_of(msg):
    tail = msg[msg.shape[0] - 16 :, :].astype(F32)
    return tail[0:1, :] + tail[1:2, :] + tail[2:3, :]


def rows_of(msg):
    return msg[: msg.shape[0] - 16, :].astype(F32)


def relax_kernel(
    meta, above, cot, guess, rate,
    qkv_t, prob_a, prob_b, unit1, inv1, unit2, inv2, deriv, wqkv, wout, win, wback, g1, g2,
    relaxed_out, resid_low, resid_high, dqkv_t,
):
    last = meta[1] == 1
    up = jnp.where(last, cot[...].astype(F32), above[...].astype(F32))
    d2 = norm_back(up, unit2[...], inv2[...], g2[...])
    dn = ffn_back(d2, d2.astype(BF), deriv, win, wback)
    d1 = norm_back(dn, unit1[...], inv1[...], g1[...])
    attention_back(d1.astype(BF), wout, qkv_t, prob_a, prob_b, dqkv_t)
    relaxed = state_back(d1, dqkv_t[...].T, wqkv).astype(BF)
    relaxed_out[...] = relaxed
    resid = (relaxed.astype(F32) - guess[...].astype(F32)).astype(BF)
    tail = thirds(rate[...])
    resid_low[:LOW, :] = resid[:LOW, :]
    resid_low[LOW:, :] = tail
    resid_high[:HIGH, :] = resid[LOW:, :]
    resid_high[HIGH:, :] = tail


def compose_low_kernel(meta, relaxed, guess, rate, one, two, out):
    resid = relaxed[:LOW, :].astype(F32) - guess[:LOW, :].astype(F32)
    r1, r2 = whole_of(one), whole_of(two)
    higher = rows_of(one) + r1 * rows_of(two)
    out[:LOW, :] = (resid + rate[...] * higher).astype(BF)
    y = meta[4]
    factor = rate[...] * jnp.where(y < 3, r1, 1.0) * jnp.where(y < 2, r2, 1.0)
    out[LOW:, :] = thirds(factor)


def compose_high_kernel(meta, relaxed, guess, across, out):
    resid = relaxed[LOW:, :].astype(F32) - guess[LOW:, :].astype(F32)
    top = jnp.where(meta[1] == 1, resid, 0.0)
    out[:HIGH, :] = (rows_of(across) + whole_of(across) * top).astype(BF)
    out[HIGH:, :] = across[HIGH:, :]


def mix_kernel(error_bf, wrapped, out):
    out[...] = (error_bf[...].astype(F32) + wrapped[...].astype(F32)).astype(BF)


def finish_kernel(
    meta, error, wrapped, passed, relaxed, guess, rate, swept, adjoint, coarse_err,
    adjoint_v, error_v, sem,
):
    last, own_known, z = meta[1] == 1, (meta[0] + meta[2]) > 0, meta[5]
    far = wrapped[...].astype(F32) + jnp.where(z == 0, 0.0, passed[...].astype(F32))
    reached = jnp.where(own_known, error[...], far)
    guess_f = guess[...].astype(F32)
    resid = relaxed[...].astype(F32) - guess_f
    value = jnp.where(z == 0, rate[...] * reached + resid, reached)
    error_v[...] = value
    first = pltpu.make_async_copy(error_v, coarse_err, sem.at[0])
    first.start()
    coarse = (z == 0) | last
    kept = jnp.where(coarse, guess_f + value, swept[...].astype(F32))
    adjoint_v[...] = kept.astype(BF)
    second = pltpu.make_async_copy(adjoint_v, adjoint, sem.at[1])
    second.start()
    first.wait()
    second.wait()


FLIPS = {"core": 1, "zl": 2, "x0": 4, "x1": 12}


def flip_of(position, order):
    flip = 0
    for bit, name in enumerate(order):
        if position & (8 >> bit):
            flip ^= FLIPS[name]
    return flip


ORDER_BACK = ("core", "x0", "zl", "x1")
ORDER_IN = ("core", "x1", "x0", "zl")
ORDER_QKV = ("core", "zl", "x1", "x0")
WIDE = FF + 128


def place(whole, rows, order, me, keep, send):
    for p in range(16):
        start = pl.multiple_of((me ^ flip_of(p, order)) * rows, rows)
        target = keep if p < 8 else send
        target[p % 8] = whole[pl.ds(start, rows), :]


def chain_kernel(
    meta, shifted_ref, composed, top1, top2, top3, high1, high2, high3,
    above, cot, guess, relaxed, unit2, inv2, g2, hidden_t,
    d2_out, gain2_out, error_out, error_bf, keep, send, whole,
):
    last = meta[1] == 1
    chained = meta[2] == 1
    me = meta[3]
    shifted = shifted_ref[...].astype(F32)
    above_f = above[...].astype(F32)
    top = rows_of(top1) + rows_of(top2) + rows_of(top3)
    low = rows_of(composed) + whole_of(composed) * top
    high = rows_of(high1) + whole_of(high1) * (
        rows_of(high2) + whole_of(high2) * rows_of(high3)
    )
    far = jnp.concatenate([low, high], axis=0)
    near = shifted - above_f
    own = relaxed[...].astype(F32) - guess[...].astype(F32)
    error = jnp.where(last, own, jnp.where(meta[0] == 1, far, near))
    error_out[...] = error
    error_bf[...] = jnp.where(meta[0] == 1, error, 0.0).astype(BF)
    corrected = (above_f + error).astype(BF).astype(F32)
    up = jnp.where(last, cot[...].astype(F32), jnp.where(chained, corrected, shifted))
    u2 = unit2[...]
    d2 = norm_back(up, u2, inv2[...], g2[...])
    gain2_out[...] = jnp.broadcast_to(jnp.sum(up * u2, axis=0, keepdims=True), (8, D))
    d2_out[...] = d2
    d2_bf = d2.astype(BF)
    for j in range(FF // D):
        rows = slice(j * D, (j + 1) * D)
        whole[rows, :] = nn(hidden_t[rows, :], d2_bf).astype(BF)
    place(whole, FF // 16, ORDER_BACK, me, keep, send)


def ffn_kernel(
    meta, d2, deriv, unit1, inv1, win, wback, g1, normed_t, gain2,
    d1_out, keep, send, du, whole,
):
    me = meta[3]
    d2v = d2[...]
    dn = ffn_back(d2v, d2v.astype(BF), deriv, win, wback, du)
    u1 = unit1[...]
    gain1 = jnp.broadcast_to(jnp.sum(dn * u1, axis=0, keepdims=True), (8, D))
    d1_out[...] = norm_back(dn, u1, inv1[...], g1[...])
    for j in range(FF // D):
        cols = slice(j * D, (j + 1) * D)
        whole[:, cols] = nn(normed_t[...], du[:, cols]).astype(BF)
    pair = jnp.concatenate([gain1, gain2[...], jnp.zeros((112, D), F32)], axis=0)
    whole[:, FF:] = pair.T.astype(BF)
    place(whole, D // 16, ORDER_IN, me, keep, send)


def attention_kernel(
    meta, d1, wout, qkv_t, prob_a, prob_b, x_t, ctx_t, dqkv_out, keep, send, dqkv_t, whole,
):
    d1_bf = d1[...].astype(BF)
    attention_back(d1_bf, wout, qkv_t, prob_a, prob_b, dqkv_t)
    whole[:, 3 * D :] = nn(ctx_t[...], d1_bf).astype(BF)
    for j in range(3):
        cols = slice(j * D, (j + 1) * D)
        part = dqkv_t[cols, :].T
        dqkv_out[:, cols] = part
        whole[:, cols] = nn(x_t[...], part).astype(BF)
    place(whole, D // 16, ORDER_QKV, meta[3], keep, send)


def state_kernel(d1, dqkv, wqkv, out):
    out[...] = state_back(d1[...], dqkv[...], wqkv).astype(BF)


HB = pl.BlockSpec(memory_space=pltpu.HBM)
VM = pl.BlockSpec(memory_space=pltpu.VMEM)
SM = pl.BlockSpec(memory_space=pltpu.SMEM)


def call(kernel, outs, scratch, args, flops, name, scalars=1, operands=VM, grant=16, into=None):
    shapes = [jax.ShapeDtypeStruct(s, t) for s, t in outs]
    return pl.pallas_call(
        kernel,
        out_shape=shapes,
        in_specs=[SM] * scalars + [operands] * (len(args) - scalars),
        out_specs=into or [VM] * len(shapes),
        scratch_shapes=[s if not isinstance(s, tuple) else pltpu.VMEM(*s) for s in scratch],
        compiler_params=pltpu.CompilerParams(vmem_limit_bytes=grant * 1024 * 1024),
        cost_estimate=pl.CostEstimate(flops=(LIGHT, STAGE1, BIG)[flops] if flops < 5 else MAIN, bytes_accessed=0, transcendentals=0),
        name=name,
    )(*args)


def by_flip(name, x):
    if name == "core":
        return lax.ppermute(x, "core", [(0, 1), (1, 0)])
    if name == "zl":
        return lax.ppermute(x, "zl", [(0, 1), (1, 0)])
    mask = 1 if name == "x0" else 3
    return lax.ppermute(x, "x", [(i, i ^ mask) for i in range(4)])


def sum_kernel(*refs):
    out = refs[-1]
    size = out.shape[0]
    total = refs[0][size : 2 * size].astype(F32)
    for ref in refs[1:-1]:
        total = total + ref[size : 2 * size].astype(F32)
    out[...] = total.astype(BF)


def passing(parts, cost=0):
    shape = parts[-1].shape
    (out,) = call(
        sum_kernel, [((shape[0] // 2,) + shape[1:], BF)], [], list(parts), cost, "sum", 0
    )
    return out


def total_of(parts):
    total = parts[0][0].astype(F32)
    for part in parts[1:]:
        total = total + part[0].astype(F32)
    return total


def shares_kernel(
    k0, k1, k2, k3, k4, i0, i1, i2, i3, i4, back, inner, gain1, gain2,
    back_v, in_v, sem,
):
    back_v[...] = total_of((k0, k1, k2, k3, k4))
    first = pltpu.make_async_copy(back_v, back, sem.at[0])
    first.start()
    in_v[...] = total_of((i0, i1, i2, i3, i4))
    second = pltpu.make_async_copy(in_v.at[:, :FF], inner, sem.at[1])
    second.start()
    turned = jnp.concatenate([in_v[:, FF:], jnp.zeros((96, 128), F32)], axis=0).T
    gain1[...] = turned[0:1, :32]
    gain2[...] = turned[8:9, :32]
    first.wait()
    second.wait()


def qkv_kernel(k0, k1, k2, k3, k4, out, outer, whole, sem):
    whole[...] = total_of((k0, k1, k2, k3, k4))
    first = pltpu.make_async_copy(whole.at[:, : 3 * D], out, sem.at[0])
    second = pltpu.make_async_copy(whole.at[:, 3 * D :], outer, sem.at[1])
    first.start()
    second.start()
    first.wait()
    second.wait()


def after(x, *done):
    return lax.optimization_barrier((x,) + done)[0]


def at(y, z):
    return FACTOR * y + z


def on_device(
    states, guess, cotangent, lengths, coarse_rate, w_qkv, w_out, w_in, w_back, gain_attn, gain_ffn
):
    x, own_guess = states[0], guess[0]
    y, z = lax.axis_index("ly"), lax.axis_index("lz")
    layer = at(y, z)
    last = layer == 15
    chained = (z == 3) & ~last | (layer == 14)
    meta = jnp.stack(
        [(z == 3).astype(jnp.int32), last.astype(jnp.int32), chained.astype(jnp.int32), lax.axis_index(DP), y, z]
    )
    above = lax.ppermute(own_guess, LAYER, [(i, i - 1) for i in range(1, 16)])

    tok = (SEQ, D)
    (
        qkv_t, prob_a, prob_b, ctx_t, x_t, normed_t, hidden_t, unit1, inv1, unit2, inv2, deriv,
        wqkv, wout, win, wback, gain_one, gain_two,
    ) = call(
        forward_kernel,
        [
            ((3 * D, SEQ), BF), ((HEADS, HALF, SEQ), F32), ((HEADS, HALF, HALF), F32),
            ((D, SEQ), BF), ((D, SEQ), BF), ((D, SEQ), BF), ((FF, SEQ), BF),
            (tok, F32), ((SEQ, 1), F32), (tok, F32), ((SEQ, 1), F32), ((SEQ, FF), F32),
            ((D, 3 * D), BF), ((D, D), BF), ((D, FF), BF), ((FF, D), BF), ((1, D), F32),
            ((1, D), F32),
        ],
        [(tok, BF), pltpu.SemaphoreType.DMA((7,))],
        [lengths] + [pltpu.with_memory_space_constraint(a, pltpu.HBM) for a in (x, w_qkv[0], w_out[0], w_in[0], w_back[0], gain_attn, gain_ffn)],
        9,
        "forward",
        operands=HB,
        grant=GRANT,
    )
    low_msg, high_msg = ((LOW + 16, D), BF), ((HIGH + 16, D), BF)
    relaxed, resid_low, resid_high = call(
        relax_kernel,
        [(tok, BF), low_msg, high_msg],
        [((3 * D, SEQ), BF)],
        [meta, above, cotangent, own_guess, coarse_rate, qkv_t, prob_a, prob_b, unit1, inv1,
         unit2, inv2, deriv, wqkv, wout, win, wback, gain_one, gain_two],
        9,
        "relax",
    )
    from1 = lax.ppermute(resid_low, LAYER, [(12, 8), (8, 4), (15, 11)])
    from2 = lax.ppermute(resid_low, LAYER, [(12, 4), (15, 7)])
    shifted = lax.ppermute(
        relaxed, LAYER, [(at(j, i), at(j, i - 1)) for j in range(4) for i in range(1, 4)]
    )
    across = lax.ppermute(resid_high, LAYER, [(4, 7), (8, 11), (12, 15)])
    from3 = lax.ppermute(resid_low, LAYER, [(15, 3)])
    (low,) = call(
        compose_low_kernel, [low_msg], [],
        [meta, relaxed, own_guess, coarse_rate, from1, from2], 0, "low",
    )
    composed = lax.ppermute(low, LAYER, [(4, 3), (8, 7), (12, 11)])
    (high,) = call(
        compose_high_kernel, [high_msg], [],
        [meta, after(relaxed, low), own_guess, across], 0, "high",
    )
    high1 = lax.ppermute(high, LAYER, [(15, 11), (11, 7), (7, 3)])
    high2 = lax.ppermute(high, LAYER, [(15, 7), (11, 3)])
    high3 = lax.ppermute(high, LAYER, [(15, 3)])
    d2, gain2, error, error_bf, keep_b, send_b = call(
        chain_kernel,
        [(tok, F32), ((8, D), F32), (tok, F32), (tok, BF), ((8, FF // 16, D), BF),
         ((8, FF // 16, D), BF)],
        [((FF, D), BF)],
        [meta, shifted, composed, from1, from2, from3, high1, high2, high3, above, cotangent,
         own_guess, relaxed, unit2, inv2, gain_two, hidden_t],
        9,
        "chain",
    )
    wrapped = lax.ppermute(error_bf, LAYER, [(at(j, 3), at(j, 0)) for j in range(4)])
    b0 = by_flip(ORDER_BACK[0], send_b)
    part_i = (8, D // 16, WIDE)
    d1, keep_i, send_i = call(
        ffn_kernel,
        [(tok, F32), (part_i, BF), (part_i, BF)],
        [((SEQ, FF), BF), ((D, WIDE), BF)],
        [meta, d2, deriv, unit1, inv1, win, wback, gain_one, normed_t, gain2],
        9,
        "ffn",
    )
    i0 = by_flip(ORDER_IN[0], send_i)
    part_q = (8, D // 16, 4 * D)
    dqkv, keep_q, send_q = call(
        attention_kernel,
        [((SEQ, 3 * D), BF), (part_q, BF), (part_q, BF)],
        [((3 * D, SEQ), BF), ((D, 4 * D), BF)],
        [meta, after(d1, b0), wout, qkv_t, prob_a, prob_b, x_t, ctx_t],
        2,
        "attention",
    )
    q0 = by_flip(ORDER_QKV[0], send_q)
    send_i = passing([keep_i, after(i0, dqkv)])
    i1 = by_flip(ORDER_IN[1], send_i)
    (swept,) = call(
        state_kernel, [(tok, BF)], [], [after(d1, send_i), dqkv, wqkv], 0, "state", 0
    )
    send_q = passing([keep_q, after(q0, swept)])
    q1 = by_flip(ORDER_QKV[1], send_q)
    send_b = passing([keep_b, after(b0, send_q)])
    b1 = by_flip(ORDER_BACK[1], send_b)
    (mixed,) = call(
        mix_kernel, [(tok, BF)], [], [after(error_bf, send_b), wrapped], 1, "mix", 0
    )
    passed = lax.ppermute(
        mixed,
        LAYER,
        [(at(j, 3), at(j, 2)) for j in range(4)] + [(at(j, 0), at(j, 1)) for j in range(4)],
    )
    send_i = passing([keep_i, i0, after(i1, mixed)])
    i2 = by_flip(ORDER_IN[2], send_i)
    send_b = passing([keep_b, b0, after(b1, send_i)])
    b2 = by_flip(ORDER_BACK[2], send_b)
    send_q = passing([keep_q, q0, after(q1, send_b)])
    q2 = by_flip(ORDER_QKV[2], send_q)
    send_i = passing([keep_i, i0, i1, after(i2, send_q)])
    i3 = by_flip(ORDER_IN[3], send_i)
    send_b = passing([keep_b, b0, b1, after(b2, send_i)])
    b3 = by_flip(ORDER_BACK[3], send_b)
    send_q = passing([keep_q, q0, q1, after(q2, send_b)])
    q3 = by_flip(ORDER_QKV[3], send_q)
    share_back, share_in, share_one, share_two = call(
        shares_kernel,
        [((FF // 16, D), F32), ((D // 16, FF), F32), ((1, 32), F32), ((1, 32), F32)],
        [((FF // 16, D), F32), ((D // 16, WIDE), F32), pltpu.SemaphoreType.DMA((2,))],
        [keep_b, b0, b1, b2, b3, keep_i, i0, i1, i2, i3],
        0, "shares", 0, into=[HB, HB, VM, VM],
    )
    share_q, share_out = call(
        qkv_kernel, [((D // 16, 3 * D), F32), ((D // 16, D), F32)],
        [((D // 16, 4 * D), F32), pltpu.SemaphoreType.DMA((2,))],
        [keep_q, q0, q1, q2, after(q3, share_in)], 0, "qkv", 0, into=[HB, HB],
    )
    adjoint, coarse_err = call(
        finish_kernel, [(tok, BF), (tok, F32)],
        [(tok, BF), (tok, F32), pltpu.SemaphoreType.DMA((2,))],
        [meta, error, wrapped, passed, relaxed, own_guess, coarse_rate, after(swept, share_q)],
        0, "finish", into=[HB, HB],
    )
    return (
        adjoint[None],
        coarse_err[None],
        share_q[None],
        share_out[None],
        share_in[None],
        share_back[None],
        share_one,
        share_two,
    )


def solution(mesh):
    torus = Mesh(mesh.devices.reshape(4, 4, 4, 2, 2), LAYER + DP)
    return jax.shard_map(
        on_device,
        mesh=torus,
        in_specs=(
            P(LAYER, DP, None),
            P(LAYER, DP, None),
            P(DP, None),
            P(DP),
            P(LAYER, None),
            P(LAYER, None, None),
            P(LAYER, None, None),
            P(LAYER, None, None),
            P(LAYER, None, None),
            P(LAYER, None),
            P(LAYER, None),
        ),
        out_specs=(
            P(LAYER, DP, None),
            P(LAYER, DP, None),
            P(LAYER, DP, None),
            P(LAYER, DP, None),
            P(LAYER, DP, None),
            P(LAYER, DP, None),
            P(LAYER, DP),
            P(LAYER, DP),
        ),
        check_vma=False,
    )
```
